32 devices in a mesh: grp: 2 (over x), box: 16 (over z, y, core).
Axes of the slice: x: 2, y: 2, z: 4, core: 2. Of those that a mesh axis runs over, the one named last changes fastest.
Arguments:
- coarse_state: float32 [5, 128, 64, 128], P(None, 'box', 'grp'), parts along dimension 2, may hold values from -1 to 5.75, as said below
- fine_state: float32 [256, 5, 16, 256], P(('grp', 'box')), parts along dimension 0, may hold values from -1 to 5.75, as said below
- patch_box: int32 [256], P('grp'), parts along dimension 0, may hold values from 0 to 1023, as said below
- face_flags: int32 [256, 6], P('grp'), parts along dimension 0, may hold values from 0 to 1, as said below
Outputs:
- coarse_next: float32 [5, 128, 64, 128], P(None, 'box', 'grp'), parts along dimension 2
- fine_next: float32 [256, 5, 16, 256], P(('grp', 'box')), parts along dimension 0
The draws below stay inside these ranges and needn't reach their ends.
There are 2 independent parts, one for each index of `grp`. The reference program is written for one: setup_inputs(seed, part) draws one part's arguments, and reference() takes and returns one part's arrays. A program takes and returns all parts, laid end to end along the dimension named above; each array names one. Nothing has to cross between parts.
Inputs may be any that keep to these rules, and one draw needn't show every extreme that they name: `patch_box`: all entries are distinct coarse boxes. Of the 8 patches held by one device (aligned blocks of rows), at most 1 lie on boxes of one index of box, and that many do in every block. `face_flags`: A flag is 1 exactly when the coarse box across that face (periodic) is refined by no patch. `coarse_state`: density lies in 0.5 to 2, velocities in -0.5 to 0.5 and pressure in 0.5 to 2 in every cell. `fine_state`: density lies in 0.5 to 2, velocities in -0.5 to 0.5 and pressure in 0.5 to 2 in every cell.
All inputs are finite; a program needn't handle non-finite values.
Results may differ from the reference program's by a relative error of at most 0.0003.
Values sent between devices are 32-bit elements; how exact they have to be, the bound alone decides.
No kernel may reach another device: no remote copies, remote signals or barrier semaphores. Data moves between devices by JAX's collectives and lax.ppermute only.
A program may use at most 256 MiB of HBM per device.

```python
import math
import jax
import jax.numpy as jnp
from jax import lax

PATCH = 16
COARSE_EDGE = 8
NY = 128
NZ = 32
NX = 128
PATCHES_DEV = 8
PATCHES = 128
N_BOX = 16


def patch_layout(key):
    y_boxes = NY // COARSE_EDGE
    per_device = NZ // COARSE_EDGE * y_boxes
    spread_count = min(N_BOX, PATCHES_DEV)
    first_key, second_key = jax.random.split(jax.random.fold_in(key, 11))
    orders = jax.vmap(lambda inner_key: jax.random.permutation(inner_key, N_BOX))(jax.random.split(first_key, N_BOX))
    columns = jnp.arange(PATCHES_DEV, dtype=jnp.int32) % spread_count
    owners = orders[:, columns].reshape(-1).astype(jnp.int32)
    onehot = (owners[:, None] == jnp.arange(N_BOX, dtype=jnp.int32)[None, :]).astype(jnp.int32)
    before = jnp.cumsum(onehot, axis=0) - onehot
    ranks = jnp.sum(before * onehot, axis=1)
    shuffles = jax.vmap(lambda inner_key: jax.random.permutation(inner_key, per_device))(jax.random.split(second_key, N_BOX))
    local_boxes = shuffles[owners, ranks].astype(jnp.int32)
    return owners * per_device + local_boxes


def draw_patch_box(key, part):
    return patch_layout(key)


def draw_face_flags(key, part):
    boxes = patch_layout(key)
    z_boxes = NZ // COARSE_EDGE
    y_boxes = NY // COARSE_EDGE
    per_device = z_boxes * y_boxes
    occupied = jnp.zeros((N_BOX * per_device,), jnp.int32).at[boxes].set(1)
    owners = boxes // per_device
    local_boxes = boxes % per_device
    z_box = local_boxes // y_boxes
    y_box = local_boxes % y_boxes

    def box_number(owner, z_value, y_value):
        return owner % N_BOX * per_device + z_value % z_boxes * y_boxes + y_value % y_boxes
    neighbours = jnp.stack([box_number(owners - 1, z_box, y_box), box_number(owners + 1, z_box, y_box), box_number(owners, z_box - 1, y_box), box_number(owners, z_box + 1, y_box), box_number(owners, z_box, y_box - 1), box_number(owners, z_box, y_box + 1)], axis=1)
    return (1 - occupied[neighbours]).astype(jnp.int32)


def gas_fields(key, shape_rest, axis_index):
    keys = jax.random.split(jax.random.fold_in(key, 5), 5)
    density = jnp.exp(jax.random.uniform(keys[0], shape_rest, jnp.float32, math.log(0.5), math.log(2.0)))
    pressure = jnp.exp(jax.random.uniform(keys[4], shape_rest, jnp.float32, math.log(0.5), math.log(2.0)))
    speeds = [0.25 * jax.random.truncated_normal(keys[which], -2.0, 2.0, shape_rest, jnp.float32) for which in (1, 2, 3)]
    kinetic = 0.5 * density * (speeds[0] * speeds[0] + speeds[1] * speeds[1] + speeds[2] * speeds[2])
    energy = pressure / 0.4 + kinetic
    return jnp.stack([density, density * speeds[0], density * speeds[1], density * speeds[2], energy], axis=axis_index)


def draw_coarse_state(key, part):
    return gas_fields(key, (NX, NZ, NY), 0)


def draw_fine_state(key, part):
    return gas_fields(key, (PATCHES, PATCH, PATCH * PATCH), 1)


def setup_inputs(seed: int = 0, part: int = 0) -> dict:
    key_of = jax.random.split(jax.random.key(seed), 5)
    own_keys = jax.random.split(jax.random.fold_in(key_of[4], part), 5)
    coarse_state = draw_coarse_state(jax.random.fold_in(jax.random.fold_in(key_of[4], part), 71), part)
    fine_state = draw_fine_state(jax.random.fold_in(jax.random.fold_in(key_of[4], part), 71), part)
    patch_box = draw_patch_box(jax.random.fold_in(jax.random.fold_in(key_of[4], part), 71), part)
    face_flags = draw_face_flags(jax.random.fold_in(jax.random.fold_in(key_of[4], part), 71), part)
    return {"coarse_state": coarse_state, "fine_state": fine_state, "patch_box": patch_box, "face_flags": face_flags}


gas_gamma = 1.4
time_step = 0.05

def directional_flux(values, moment):
    density = values[0]
    velocity = values[moment] / density
    pressure = (gas_gamma - 1.0) * (values[4] - 0.5 * (values[1] * values[1] + values[2] * values[2] + values[3] * values[3]) / density)
    pieces = [values[moment], values[1] * velocity, values[2] * velocity, values[3] * velocity, (values[4] + pressure) * velocity]
    pieces[moment] = pieces[moment] + pressure
    signal = jnp.abs(velocity) + jnp.sqrt(gas_gamma * pressure / density)
    return (jnp.stack(pieces), signal)

def rusanov(left_state, right_state, moment):
    flux_left, speed_left = directional_flux(left_state, moment)
    flux_right, speed_right = directional_flux(right_state, moment)
    fastest = jnp.maximum(speed_left, speed_right)
    return 0.5 * (flux_left + flux_right) - 0.5 * fastest * (right_state - left_state)

def advance(padded):
    flux_x = rusanov(padded[:, :-1, 1:-1, 1:-1], padded[:, 1:, 1:-1, 1:-1], 1)
    flux_z = rusanov(padded[:, 1:-1, :-1, 1:-1], padded[:, 1:-1, 1:, 1:-1], 3)
    flux_y = rusanov(padded[:, 1:-1, 1:-1, :-1], padded[:, 1:-1, 1:-1, 1:], 2)
    interior = padded[:, 1:-1, 1:-1, 1:-1]
    change = flux_x[:, 1:] - flux_x[:, :-1] + (flux_z[:, :, 1:] - flux_z[:, :, :-1]) + (flux_y[:, :, :, 1:] - flux_y[:, :, :, :-1])
    return (interior - time_step * change, flux_x, flux_z, flux_y)

def box_faces(block):
    outer_faces = jnp.stack([block[:, 0, 1:-1, 1:-1], block[:, -1, 1:-1, 1:-1], block[:, 1:-1, 0, 1:-1], block[:, 1:-1, -1, 1:-1], block[:, 1:-1, 1:-1, 0], block[:, 1:-1, 1:-1, -1]], axis=1)
    inner_faces = jnp.stack([block[:, 1, 1:-1, 1:-1], block[:, -2, 1:-1, 1:-1], block[:, 1:-1, 1, 1:-1], block[:, 1:-1, -2, 1:-1], block[:, 1:-1, 1:-1, 1], block[:, 1:-1, 1:-1, -2]], axis=1)
    return (outer_faces, inner_faces)

def coarse_face_flux(outer_faces, inner_faces):
    moments = (1, 1, 3, 3, 2, 2)
    results = []
    for which in range(6):
        if which % 2 == 0:
            results.append(rusanov(outer_faces[:, which], inner_faces[:, which], moments[which]))
        else:
            results.append(rusanov(inner_faces[:, which], outer_faces[:, which], moments[which]))
    return jnp.stack(results, axis=1)

def widen_face(plane):
    return jnp.repeat(jnp.repeat(plane, 2, axis=1), 2, axis=2)

def fine_steps(patch_cube, outer_faces):
    padded = jnp.pad(patch_cube, ((0, 0), (1, 1), (1, 1), (1, 1)))
    padded = padded.at[:, 0, 1:-1, 1:-1].set(widen_face(outer_faces[:, 0]))
    padded = padded.at[:, -1, 1:-1, 1:-1].set(widen_face(outer_faces[:, 1]))
    padded = padded.at[:, 1:-1, 0, 1:-1].set(widen_face(outer_faces[:, 2]))
    padded = padded.at[:, 1:-1, -1, 1:-1].set(widen_face(outer_faces[:, 3]))
    padded = padded.at[:, 1:-1, 1:-1, 0].set(widen_face(outer_faces[:, 4]))
    padded = padded.at[:, 1:-1, 1:-1, -1].set(widen_face(outer_faces[:, 5]))
    current = patch_cube
    flux_total = jnp.zeros((5, 6) + patch_cube.shape[2:], jnp.float32)
    for substep in range(2):
        padded = padded.at[:, 1:-1, 1:-1, 1:-1].set(current)
        current, flux_x, flux_z, flux_y = advance(padded)
        flux_total = flux_total + jnp.stack([flux_x[:, 0], flux_x[:, -1], flux_z[:, :, 0], flux_z[:, :, -1], flux_y[:, :, :, 0], flux_y[:, :, :, -1]], axis=1)
    coarse_width = patch_cube.shape[1] // 2
    fine_flux = flux_total.reshape(5, 6, coarse_width, 2, coarse_width, 2).sum(axis=(3, 5)) / 8.0
    averaged = current.reshape(5, coarse_width, 2, coarse_width, 2, coarse_width, 2).mean(axis=(2, 4, 6))
    return (current, averaged, fine_flux)

def reference(coarse_state, fine_state, patch_box, face_flags):
    y_boxes = NY // COARSE_EDGE
    per_device = NZ // COARSE_EDGE * y_boxes
    face_signs = jnp.array([-1.0, 1.0, -1.0, 1.0, -1.0, 1.0], jnp.float32)
    padded = jnp.pad(coarse_state, ((0, 0), (1, 1), (1, 1), (1, 1)), mode='wrap')
    anchor_zero = jnp.zeros((), jnp.int32)

    def slab_update(index):
        start = (index * COARSE_EDGE).astype(jnp.int32)
        piece = lax.dynamic_slice(padded, (anchor_zero, start, anchor_zero, anchor_zero), (5, COARSE_EDGE + 2, NZ + 2, NY + 2))
        return advance(piece)[0]
    slabs = lax.map(slab_update, jnp.arange(N_BOX, dtype=jnp.int32))
    updated = jnp.moveaxis(slabs, 0, 1).reshape(5, NX, NZ, NY)
    owners = (patch_box // per_device).astype(jnp.int32)
    local_boxes = (patch_box % per_device).astype(jnp.int32)
    x_anchor = (owners * COARSE_EDGE).astype(jnp.int32)
    z_anchor = (local_boxes // y_boxes * COARSE_EDGE).astype(jnp.int32)
    y_anchor = (local_boxes % y_boxes * COARSE_EDGE).astype(jnp.int32)
    cubes = fine_state.reshape(PATCHES, 5, PATCH, PATCH, PATCH)

    def one_patch(inputs):
        patch_cube, x_start, z_start, y_start, flags = inputs
        block = lax.dynamic_slice(padded, (anchor_zero, x_start.astype(jnp.int32), z_start.astype(jnp.int32), y_start.astype(jnp.int32)), (5, COARSE_EDGE + 2, COARSE_EDGE + 2, COARSE_EDGE + 2))
        outer_faces, inner_faces = box_faces(block)
        current, averaged, fine_flux = fine_steps(patch_cube, outer_faces)
        coarse_flux = coarse_face_flux(outer_faces, inner_faces)
        correction = face_signs[None, :, None, None] * time_step * (fine_flux - coarse_flux) * flags.astype(jnp.float32)[None, :, None, None]
        return (current, averaged, correction)
    states, averages, corrections = lax.map(one_patch, (cubes, x_anchor, z_anchor, y_anchor, face_flags))
    span = jnp.arange(COARSE_EDGE, dtype=jnp.int32)
    across = span[:, None] + 0 * span[None, :]
    along = 0 * span[:, None] + span[None, :]

    def face_coords(x_start, z_start, y_start):
        blank = across * 0
        x_index = jnp.stack([blank + x_start - 1, blank + x_start + COARSE_EDGE, x_start + across, x_start + across, x_start + across, x_start + across])
        z_index = jnp.stack([z_start + across, z_start + across, blank + z_start - 1, blank + z_start + COARSE_EDGE, z_start + along, z_start + along])
        y_index = jnp.stack([y_start + along, y_start + along, y_start + along, y_start + along, blank + y_start - 1, blank + y_start + COARSE_EDGE])
        return (x_index % NX, z_index % NZ, y_index % NY)
    x_index, z_index, y_index = jax.vmap(face_coords)(x_anchor, z_anchor, y_anchor)
    updated = updated.at[:, x_index, z_index, y_index].add(jnp.moveaxis(corrections, 1, 0))
    cube_x = x_anchor[:, None, None, None] + span[None, :, None, None]
    cube_z = z_anchor[:, None, None, None] + span[None, None, :, None]
    cube_y = y_anchor[:, None, None, None] + span[None, None, None, :]
    updated = updated.at[:, cube_x, cube_z, cube_y].set(jnp.moveaxis(averages, 1, 0))
    return (updated, states.reshape(PATCHES, 5, PATCH, PATCH * PATCH))
```

```python
import functools

import jax
import jax.numpy as jnp
from jax import lax
from jax.experimental import pallas as pl
from jax.experimental.pallas import tpu as pltpu
from jax.sharding import PartitionSpec as P

gas_gamma = 1.4
time_step = 0.05

NF = 5
CW = 8
FW = 16
NP = 8
LN = 128
ZC = 32
YB = LN // CW
SIDE = ((0, 0), (0, 33), (0, 66), (1, 0), (1, 33))
XUNIT = tuple((0, 99 + 8 * u) if u < 3 else (1, 66 + 8 * (u - 3)) for u in range(10))


def take_lanes(values, index):
    return jnp.take_along_axis(values, index, axis=1, mode="promise_in_bounds")


def lanes():
    return lax.broadcasted_iota(jnp.int32, (8, LN), 1)


def roll_to(values, shift):
    if isinstance(shift, int):
        shift = shift % LN
        return values if shift == 0 else pltpu.roll(values, shift, 1)
    return pltpu.roll(values, shift & (LN - 1), 1)


def primitives(state):
    inverse = 1.0 / state[0]
    speeds = [None] + [state[m] * inverse for m in (1, 2, 3)]
    squares = state[1] * speeds[1] + state[2] * speeds[2] + state[3] * speeds[3]
    pressure = (gas_gamma - 1.0) * (state[4] - 0.5 * squares)
    sound = jnp.sqrt(gas_gamma * pressure * inverse)
    return speeds, pressure, sound, state[4] + pressure


def side_of_face(state, prims, m):
    speeds, pressure, sound, total = prims
    v = speeds[m]
    flux = [state[m], state[1] * v, state[2] * v, state[3] * v, total * v]
    flux[m] = flux[m] + pressure
    return list(state) + flux + [jnp.abs(v) + sound]


def face_flux(left, right):
    fastest = jnp.maximum(left[10], right[10])
    return [left[5 + f] + right[5 + f] - fastest * (right[f] - left[f]) for f in range(NF)]


def split_box(number, per_device):
    if per_device & (per_device - 1) == 0:
        return number >> (per_device.bit_length() - 1), number & (per_device - 1)
    owner = lax.div(number, jnp.int32(per_device))
    return owner, number - owner * per_device


def find_slots(box_ref, source, me, count, per_device):
    after = jnp.where(me == count - 1, 0, me + 1)
    before = jnp.where(me == 0, count - 1, me - 1)
    found = [jnp.int32(-1)] * 3
    rows = [jnp.int32(0)] * 3
    for j in range(NP):
        row = source * NP + j
        owner, place = split_box(box_ref[row], per_device)
        for which, slab in enumerate((me, after, before)):
            hit = owner == slab
            found[which] = jnp.where(hit, place, found[which])
            rows[which] = jnp.where(hit, row, rows[which])
    return found, rows


def anchors(place):
    return (place >> 4) * CW, (place & (YB - 1)) * CW


def pack_kernel(count, box_ref, coarse_ref, out_ref, first_ref, last_ref):
    me = lax.axis_index("box")
    per_device = ZC // CW * YB
    lane = lanes()
    for f in range(NF):
        first_ref[pl.ds(f * ZC, ZC), :] = coarse_ref[pl.ds(f * 256, ZC), :]
        last_ref[pl.ds(f * ZC, ZC), :] = coarse_ref[pl.ds(f * 256 + 7 * ZC, ZC), :]

    def one(source, carry):
        (own, after, before), _ = find_slots(box_ref, source, me, count, per_device)
        tiles = [jnp.zeros((8, LN), jnp.float32)] * 2
        for u in range(10):
            f, upper = u // 2, u % 2
            place = jnp.maximum(before if upper else after, 0)
            z0, y0 = anchors(place)
            plane = 0 if upper else CW - 1
            values = coarse_ref[pl.ds(pl.multiple_of(f * 256 + plane * ZC + z0, 8), 8), :]
            tile, base = XUNIT[u]
            moved = roll_to(values, base - y0)
            tiles[tile] = jnp.where((lane >= base) & (lane < base + 8), moved, tiles[tile])
        row0 = pl.multiple_of(source * 16, 16)
        out_ref[pl.ds(row0, 8), :] = tiles[0]
        out_ref[pl.ds(row0 + 8, 8), :] = tiles[1]

        @pl.when(own >= 0)
        def _():
            z0, y0 = anchors(own)
            below = (z0 - 1) & (ZC - 1)
            above = (z0 + CW) & (ZC - 1)
            sides = [jnp.zeros((8, LN), jnp.float32)] * 2
            for f in range(NF):
                low = coarse_ref[pl.ds(f * 256 + below, 8, stride=ZC), :]
                high = coarse_ref[pl.ds(f * 256 + above, 8, stride=ZC), :]
                piece = jnp.where(lane < 8, roll_to(low, -y0), roll_to(high, 8 - y0))
                for k in range(CW):
                    values = coarse_ref[pl.ds(f * 256 + z0 + k, 8, stride=ZC), :]
                    moved = roll_to(values, 17 + k - y0)
                    piece = jnp.where((lane == 16 + k) | (lane == 25 + k), moved, piece)
                tile, base = SIDE[f]
                piece = roll_to(piece, base)
                sides[tile] = jnp.where((lane >= base) & (lane < base + 33), piece, sides[tile])
            out_ref[pl.ds(row0, 8), :] = jnp.where(lane < 99, sides[0], out_ref[pl.ds(row0, 8), :])
            out_ref[pl.ds(row0 + 8, 8), :] = jnp.where(lane < 66, sides[1], out_ref[pl.ds(row0 + 8, 8), :])

        return carry

    lax.fori_loop(0, count, one, 0)


def fine_kernel(
    count,
    box_ref,
    ghost_ref,
    fine_ref,
    next_ref,
    out_ref,
    message,
    zghost,
    yghost,
    xghost,
    state,
    carry,
    zsum,
    ysum,
    xsum,
    packed,
    given,
    semaphores,
):
    per_device = ZC // CW * YB
    me = lax.axis_index("box")
    lane = lanes()
    halves = [pl.ds(c * LN, LN) for c in range(2)]
    loads = [pltpu.make_async_copy(fine_ref.at[:, halves[c]], given.at[c], semaphores.at[c]) for c in range(2)]
    for copy in loads:
        copy.start()
    place_y = lane & 15
    first_y = place_y == 0
    last_y = place_y == 15
    low16 = lane < 16
    high16 = lane < 112

    def slots(p):
        owner, _ = split_box(box_ref[me * NP + p], per_device)
        return owner, jnp.where(owner == 0, count - 1, owner - 1), jnp.where(owner == count - 1, 0, owner + 1)

    for p in range(NP):
        own, before, after = slots(p)
        for tile in range(2):
            start = 99 if tile == 0 else 66
            lower_parity = 0 if tile == 0 else 1
            is_x = lane >= start
            is_lower = (((lane - start) >> 3) & 1) == lower_parity
            pieces = [ghost_ref[pl.ds(pl.multiple_of(s * 16 + tile * 8, 8), 8), :] for s in (own, before, after)]
            message[pl.ds(p * 16 + tile * 8, 8), :] = jnp.where(
                is_x, jnp.where(is_lower, pieces[1], pieces[2]), pieces[0]
            )
    pair_y = place_y >> 1
    for r in range(CW):
        rows = [message[pl.ds(tile * 8 + r, 8, stride=16), :] for tile in range(2)]
        along_z = []
        along_y = [[], []]
        for f in range(NF):
            tile, base = SIDE[f]
            along_z.append(take_lanes(rows[tile], jnp.where(lane < 64, base, base + 8) + pair_y))
            for c in range(2):
                index = jnp.where(place_y < 8, base + 16, base + 25) + (lane >> 5) + 4 * c
                along_y[c].append(take_lanes(rows[tile], index))
        for i, v in enumerate(side_of_face(along_z, primitives(along_z), 3)):
            zghost[i, r] = v
        for c in range(2):
            for i, v in enumerate(side_of_face(along_y[c], primitives(along_y[c]), 2)):
                yghost[i, r, c] = v
        for u in range(10):
            tile, base = XUNIT[u]
            moved = take_lanes(rows[tile], base + pair_y)
            f, upper = u // 2, u % 2
            c = r // 4
            if r % 4 == 0:
                xghost[upper, f, c] = moved
            else:
                xghost[upper, f, c] = jnp.where((lane >> 5) == r % 4, moved, xghost[upper, f, c])
    for upper in range(2):
        for c in range(2):
            values = [xghost[upper, f, c] for f in range(NF)]
            for i, v in enumerate(side_of_face(values, primitives(values), 1)):
                xghost[upper, i, c] = v

    step = 0.5 * time_step

    def substep(first):
        def finish(plane, part, flux):
            for c in range(2):
                for f in range(NF):
                    value = part[c][f] - step * flux[c][f]
                    state[f, plane, c] = value

        for c in range(2):
            for i in range(11):
                carry[i, c] = xghost[0, i, c]
            for f in range(NF):
                carry[11 + f, c] = jnp.zeros((8, LN), jnp.float32)

        def pair(r, unused):
            zg = [zghost[i, r] for i in range(11)]
            zb = [None] * NF
            yb = [[None] * NF for _ in range(2)]
            for half in range(2):
                x = 2 * r + half
                if first:
                    cells = [
                        [given[c, pl.ds(f * FW + x, NP, stride=NF * FW), :] for f in range(NF)] for c in range(2)
                    ]
                else:
                    cells = [[state[f, x + 1, c] for f in range(NF)] for c in range(2)]
                prims = [primitives(u) for u in cells]
                flux_x = []
                for c in range(2):
                    here = side_of_face(cells[c], prims[c], 1)
                    behind = [carry[i, c] for i in range(11)]
                    flux_x.append(face_flux(behind, here))
                    for i in range(11):
                        carry[i, c] = here[i]
                finish(x, [[carry[11 + f, c] for f in range(NF)] for c in range(2)], flux_x)

                if half == 0:

                    @pl.when(r == 0)
                    def _():
                        for c in range(2):
                            for f in range(NF):
                                value = flux_x[c][f]
                                xsum[0, f, c] = value if first else xsum[0, f, c] + value

                here = [side_of_face(cells[c], prims[c], 3) for c in range(2)]
                turned = [[roll_to(v, 16) for v in here[c]] for c in range(2)]
                left = [
                    [jnp.where(low16, zg[i], turned[0][i]) for i in range(11)],
                    [jnp.where(low16, turned[0][i], turned[1][i]) for i in range(11)],
                ]
                lower = [face_flux(left[c], here[c]) for c in range(2)]
                last = face_flux(here[1], zg)
                change = [[], []]
                for f in range(NF):
                    back = [roll_to(lower[c][f], -16) for c in range(2)]
                    change[0].append(jnp.where(high16, back[0], back[1]) - lower[0][f])
                    change[1].append(jnp.where(high16, back[1], last[f]) - lower[1][f])
                    edge = jnp.where(lane < 64, lower[0][f], last[f])
                    zb[f] = edge if half == 0 else zb[f] + edge
                for c in range(2):
                    yg = [yghost[i, r, c] for i in range(11)]
                    here = side_of_face(cells[c], prims[c], 2)
                    left = [jnp.where(first_y, yg[i], roll_to(here[i], 1)) for i in range(11)]
                    lower_y = face_flux(left, here)
                    last_flux = face_flux(here, yg)
                    for f in range(NF):
                        upper_y = jnp.where(last_y, last_flux[f], roll_to(lower_y[f], -1))
                        change[c][f] = change[c][f] + (upper_y - lower_y[f])
                        edge = jnp.where(place_y < 8, lower_y[f], last_flux[f])
                        yb[c][f] = edge if half == 0 else yb[c][f] + edge
                for c in range(2):
                    for f in range(NF):
                        carry[11 + f, c] = cells[c][f] - step * (change[c][f] - flux_x[c][f])
            for f in range(NF):
                zsum[f, r] = zb[f] if first else zsum[f, r] + zb[f]
                for c in range(2):
                    ysum[f, r, c] = yb[c][f] if first else ysum[f, r, c] + yb[c][f]
            return unused

        lax.fori_loop(0, CW, pair, 0)
        flux_x = [
            face_flux([carry[i, c] for i in range(11)], [xghost[1, i, c] for i in range(11)]) for c in range(2)
        ]
        finish(FW, [[carry[11 + f, c] for f in range(NF)] for c in range(2)], flux_x)
        for c in range(2):
            for f in range(NF):
                value = flux_x[c][f]
                xsum[1, f, c] = value if first else xsum[1, f, c] + value

    for copy in loads:
        copy.wait()
    substep(True)
    substep(False)

    source_avg = ((lane & 31) >> 3) * 32 + (lane & 7) * 2
    source_z = jnp.where(lane < 88, (lane - 80) * 2, 112 + (lane - 88) * 2) & (LN - 1)
    source_y = jnp.where(lane < 72, 0, 15) + (lane & 3) * 32
    for f in range(NF):
        xpool = []
        for side in range(2):
            cols = []
            for c in range(2):
                v = xsum[side, f, c]
                v = v + roll_to(v, -1)
                cols.append(v + roll_to(v, -16))
            xpool.append(cols)

        for r in range(CW):
            average = None
            for c in range(2):
                v = []
                for half in range(2):
                    value = state[f, 2 * r + half + 1, c]
                    given[c, pl.ds(f * FW + 2 * r + half, NP, stride=NF * FW), :] = value
                    v.append(value)
                v = v[0] + v[1]
                v = v + roll_to(v, -1)
                v = v + roll_to(v, -16)
                v = take_lanes(v, source_avg)
                average = v if c == 0 else jnp.where(lane < 32, average, v)
            v = zsum[f, r]
            z_part = take_lanes(v + roll_to(v, -1), source_z)
            y_part = []
            for c in range(2):
                v = ysum[f, r, c]
                y_part.append(take_lanes(v + roll_to(v, -16), source_y))
            y_part = jnp.where((lane & 7) < 4, y_part[0], y_part[1])
            source_x = (r % 4) * 32 + (lane & 7) * 2
            x_part = [take_lanes(xpool[side][r // 4], source_x) for side in range(2)]
            x_part = jnp.where(lane < 104, x_part[0], x_part[1])
            fluxes = jnp.where(lane < 80, y_part, jnp.where(lane < 96, z_part, x_part)) * 0.0625
            row = jnp.where(lane < 64, average * 0.125, fluxes)
            packed[pl.ds(f * 8 + r, NP, stride=NF * 8), :] = row

    stores = [pltpu.make_async_copy(given.at[c], next_ref.at[:, halves[c]], semaphores.at[2 + c]) for c in range(2)]
    for copy in stores:
        copy.start()
    for p in range(NP):
        own, before, after = slots(p)
        for f in range(NF):
            tile = packed[pl.ds(p * 40 + f * 8, 8), :]
            for slot, low, high in ((own, 0, 96), (before, 96, 104), (after, 104, 112)):
                target = out_ref.at[pl.ds(pl.multiple_of(slot * 40 + f * 8, 8), 8), :]
                pltpu.store(target, tile, mask=(lane >= low) & (lane < high))
    for copy in stores:
        copy.wait()


def coarse_kernel(coarse_ref, low_ref, high_ref, next_ref, ylow_ref, yhigh_ref, zlow_ref, xedge_ref, carry):
    step = 0.5 * time_step
    rows = lax.broadcasted_iota(jnp.int32, (ZC, LN), 0)
    values = [low_ref[pl.ds(f * ZC, ZC), :] for f in range(NF)]
    for i, v in enumerate(side_of_face(values, primitives(values), 1)):
        carry[i] = v

    def store(ref, f, x, value):
        ref[pl.ds(pl.multiple_of(f * 256 + x * ZC, ZC), ZC), :] = value

    def plane(x, unused):
        cells = [coarse_ref[pl.ds(pl.multiple_of(f * 256 + x * ZC, ZC), ZC), :] for f in range(NF)]
        prims = primitives(cells)
        here = side_of_face(cells, prims, 1)
        flux_x = face_flux([carry[i] for i in range(11)], here)

        @pl.when(x > 0)
        def _():
            for f in range(NF):
                store(next_ref, f, x - 1, carry[11 + f] - step * flux_x[f])

        @pl.when(x == 0)
        def _():
            for f in range(NF):
                xedge_ref[pl.ds(f * 64, ZC), :] = flux_x[f]

        for i in range(11):
            carry[i] = here[i]
        here = side_of_face(cells, prims, 3)
        left = [pltpu.roll(v, 1, 0) for v in here]
        lower_z = face_flux(left, here)
        here = side_of_face(cells, prims, 2)
        left = [pltpu.roll(v, 1, 1) for v in here]
        lower_y = face_flux(left, here)
        for f in range(NF):
            upper_y = pltpu.roll(lower_y[f], LN - 1, 1)
            change = (pltpu.roll(lower_z[f], ZC - 1, 0) - lower_z[f]) + (upper_y - lower_y[f])
            carry[11 + f] = cells[f] - step * (change - flux_x[f])
            store(ylow_ref, f, x, lower_y[f])
            store(yhigh_ref, f, x, upper_y)
            store(zlow_ref, f, x, lower_z[f])
        return unused

    lax.fori_loop(0, CW, plane, 0)
    values = [high_ref[pl.ds(f * ZC, ZC), :] for f in range(NF)]
    flux_x = face_flux([carry[i] for i in range(11)], side_of_face(values, primitives(values), 1))
    for f in range(NF):
        store(next_ref, f, CW - 1, carry[11 + f] - step * flux_x[f])
        xedge_ref[pl.ds(f * 64 + ZC, ZC), :] = flux_x[f]


def apply_kernel(count, box_ref, flag_ref, result_ref, base_ref, ylow_ref, yhigh_ref, zlow_ref, xedge_ref, out_ref):
    me = lax.axis_index("box")
    per_device = ZC // CW * YB
    lane = lanes()
    sub = lax.broadcasted_iota(jnp.int32, (8, LN), 0)
    out_ref[...] = base_ref[...]

    def weight(row, face):
        return flag_ref[row, face].astype(jnp.float32) * (time_step if face % 2 else -time_step)

    def one(source, unused):
        found, rows = find_slots(box_ref, source, me, count, per_device)
        row0 = pl.multiple_of(source * 40, 8)

        def tile(f):
            return result_ref[pl.ds(row0 + f * 8, 8), :]

        for upper in range(2):
            place = found[1 + upper]

            @pl.when(place >= 0)
            def _():
                z0, y0 = anchors(place)
                scale = weight(rows[1 + upper], upper)
                inside = (lane >= y0) & (lane < y0 + CW)
                for f in range(NF):
                    moved = roll_to(tile(f), y0 - 96 - 8 * upper)
                    plane = 0 if upper else CW - 1
                    at = pl.ds(pl.multiple_of(f * 256 + plane * ZC + z0, 8), 8)
                    edge = xedge_ref[pl.ds(pl.multiple_of(f * 64 + (1 - upper) * ZC + z0, 8), 8), :]
                    old = out_ref[at, :]
                    out_ref[at, :] = jnp.where(inside, old + scale * (moved - 0.5 * edge), old)

        place = found[0]

        @pl.when(place >= 0)
        def _():
            z0, y0 = anchors(place)
            inside = (lane >= y0) & (lane < y0 + CW)
            for upper in range(2):
                scale = weight(rows[0], 2 + upper)
                target = (z0 + (CW if upper else -1)) & (ZC - 1)
                face = target if upper else z0
                for f in range(NF):
                    moved = roll_to(tile(f), y0 - 80 - 8 * upper)
                    at = pl.ds(f * 256 + target, 8, stride=ZC)
                    edge = zlow_ref[pl.ds(f * 256 + face, 8, stride=ZC), :]
                    old = out_ref[at, :]
                    out_ref[at, :] = jnp.where(inside, old + scale * (moved - 0.5 * edge), old)
            before = lane == ((y0 - 1) & (LN - 1))
            after = lane == ((y0 + CW) & (LN - 1))
            index = jnp.where(inside, sub * CW + (lane - y0), jnp.where(before, 64 + sub, 72 + sub))
            scale = jnp.where(before, weight(rows[0], 4), jnp.where(after, weight(rows[0], 5), 0.0))
            for f in range(NF):
                for x in range(CW):
                    at = pl.ds(pl.multiple_of(f * 256 + x * ZC + z0, 8), 8)
                    line = jnp.broadcast_to(result_ref[pl.ds(row0 + f * 8 + x, 1), :], (8, LN))
                    got = take_lanes(line, index)
                    edge = jnp.where(before, yhigh_ref[at, :], ylow_ref[at, :])
                    out_ref[at, :] = jnp.where(inside, got, out_ref[at, :] + scale * (got - 0.5 * edge))

        return unused

    lax.fori_loop(0, count, one, 0)


def local(coarse_state, fine_state, patch_box, face_flags):
    count = lax.axis_size("box")
    assert coarse_state.shape == (NF, CW, ZC, LN) and fine_state.shape == (NP, NF, FW, FW * FW)
    coarse = coarse_state.reshape(NF * CW * ZC, LN)
    fine = fine_state.reshape(NP * NF * FW, FW * FW)
    f32 = jnp.float32
    vmem = pl.BlockSpec(memory_space=pltpu.VMEM)
    anywhere = pl.BlockSpec(memory_space=pl.ANY)
    smem = pl.BlockSpec(memory_space=pltpu.SMEM)

    def shaped(*shape):
        return jax.ShapeDtypeStruct(shape, f32)

    def cost(flops, size):
        return pl.CostEstimate(flops=flops, bytes_accessed=size, transcendentals=0)

    packets, first, last = pl.pallas_call(
        functools.partial(pack_kernel, count),
        out_shape=(shaped(count * 16, LN), shaped(NF * ZC, LN), shaped(NF * ZC, LN)),
        in_specs=[smem, vmem],
        out_specs=(vmem, vmem, vmem),
        cost_estimate=cost(1000000, 1000000),
        name="pack",
    )(patch_box, coarse)
    arrived = lax.all_to_all(packets.reshape(count, 16, LN), "box", split_axis=0, concat_axis=0, tiled=True)
    ring = [(i, (i + 1) % count) for i in range(count)]
    low = lax.ppermute(last, "box", ring)
    high = lax.ppermute(first, "box", [(b, a) for a, b in ring])
    fine_next, outbox = pl.pallas_call(
        functools.partial(fine_kernel, count),
        out_shape=(shaped(NP * NF * FW, FW * FW), shaped(count * 40, LN)),
        in_specs=[smem, vmem, anywhere],
        out_specs=(anywhere, vmem),
        scratch_shapes=[
            pltpu.VMEM((NP * 16, LN), f32),
            pltpu.VMEM((11, CW, 8, LN), f32),
            pltpu.VMEM((11, CW, 2, 8, LN), f32),
            pltpu.VMEM((2, 11, 2, 8, LN), f32),
            pltpu.VMEM((NF, FW + 1, 2, 8, LN), f32),
            pltpu.VMEM((16, 2, 8, LN), f32),
            pltpu.VMEM((NF, CW, 8, LN), f32),
            pltpu.VMEM((NF, CW, 2, 8, LN), f32),
            pltpu.VMEM((2, NF, 2, 8, LN), f32),
            pltpu.VMEM((NP * 40, LN), f32),
            pltpu.VMEM((2, NP * NF * FW, LN), f32),
            pltpu.SemaphoreType.DMA((4,)),
        ],
        cost_estimate=cost(20000000, 4000000),
        name="fine",
    )(patch_box, arrived.reshape(count * 16, LN), fine)
    returned = lax.all_to_all(outbox.reshape(count, 40, LN), "box", split_axis=0, concat_axis=0, tiled=True)
    size = NF * CW * ZC
    base, ylow, yhigh, zlow, xedge = pl.pallas_call(
        coarse_kernel,
        out_shape=(shaped(size, LN),) * 4 + (shaped(NF * 2 * ZC, LN),),
        in_specs=[vmem] * 3,
        out_specs=(vmem,) * 5,
        scratch_shapes=[pltpu.VMEM((16, ZC, LN), f32)],
        cost_estimate=cost(10000000, 4000000),
        name="coarse",
    )(coarse, low, high)
    coarse_next = pl.pallas_call(
        functools.partial(apply_kernel, count),
        out_shape=shaped(size, LN),
        in_specs=[smem, smem] + [vmem] * 6,
        out_specs=vmem,
        cost_estimate=cost(2000000, 4000000),
        name="apply",
    )(patch_box, face_flags, returned.reshape(count * 40, LN), base, ylow, yhigh, zlow, xedge)
    return coarse_next.reshape(coarse_state.shape), fine_next.reshape(fine_state.shape)


def solution(mesh):
    placed = (
        P(None, "box", "grp", None),
        P(("grp", "box"), None, None, None),
        P("grp"),
        P("grp", None),
    )
    return jax.shard_map(
        local,
        mesh=mesh,
        in_specs=placed,
        out_specs=(P(None, "box", "grp", None), P(("grp", "box"), None, None, None)),
        check_vma=False,
    )
```

```python
import functools

import jax
import jax.numpy as jnp
from jax import lax
from jax.experimental import pallas as pl
from jax.experimental.pallas import tpu as pltpu
from jax.sharding import PartitionSpec as P


gas_gamma = 1.4
time_step = 0.05

NF = 5
CW = 8
FW = 16
NP = 8
LN = 128
ZC = 32
YB = LN // CW
SIDE = ((0, 0), (0, 33), (0, 66), (1, 0), (1, 33))
XUNIT = tuple((0, 99 + 8 * u) if u < 3 else (1, 66 + 8 * (u - 3)) for u in range(10))


def take_lanes(values, index):
    return jnp.take_along_axis(values, index, axis=1, mode="promise_in_bounds")


def lanes():
    return lax.broadcasted_iota(jnp.int32, (8, LN), 1)


def roll_to(values, shift):
    if isinstance(shift, int):
        shift = shift % LN
        return values if shift == 0 else pltpu.roll(values, shift, 1)
    return pltpu.roll(values, shift & (LN - 1), 1)


def primitives(state):
    inverse = 1.0 / state[0]
    speeds = [None] + [state[m] * inverse for m in (1, 2, 3)]
    squares = state[1] * speeds[1] + state[2] * speeds[2] + state[3] * speeds[3]
    pressure = (gas_gamma - 1.0) * (state[4] - 0.5 * squares)
    sound = jnp.sqrt(gas_gamma * pressure * inverse)
    return speeds, pressure, sound, state[4] + pressure


def side_of_face(state, prims, m):
    speeds, pressure, sound, total = prims
    v = speeds[m]
    flux = [state[m], state[1] * v, state[2] * v, state[3] * v, total * v]
    flux[m] = flux[m] + pressure
    return list(state) + flux + [jnp.abs(v) + sound]


def face_flux(left, right):
    fastest = jnp.maximum(left[10], right[10])
    return [left[5 + f] + right[5 + f] - fastest * (right[f] - left[f]) for f in range(NF)]


def split_box(number, per_device):
    if per_device & (per_device - 1) == 0:
        return number >> (per_device.bit_length() - 1), number & (per_device - 1)
    owner = lax.div(number, jnp.int32(per_device))
    return owner, number - owner * per_device


def fill_slots(box_ref, slot_ref, own_ref, me, count, per_device):
    def clear(i, unused):
        for k in range(3):
            slot_ref[k * count + i] = jnp.int32(-1)
        return unused

    lax.fori_loop(0, count, clear, 0)

    def one(source, used):
        for j in range(NP):
            row = source * NP + j
            owner, _ = split_box(box_ref[row], per_device)
            k = owner - me + 1
            k = jnp.where(k < 0, k + count, k)
            k = jnp.where(k >= count, k - count, k)
            slot_ref[jnp.minimum(k, 3) * count + source] = row
            own_ref[1 + used] = row
            used = used + jnp.where(k == 1, 1, 0)
        return used

    own_ref[0] = lax.fori_loop(0, count, one, 0)


def place_of(box_ref, row, per_device):
    return split_box(box_ref[jnp.maximum(row, 0)], per_device)[1]


def anchors(place):
    return (place >> 4) * CW, (place & (YB - 1)) * CW


def pack_kernel(count, box_hbm, coarse_hbm, out_ref, first_ref, last_ref, slot_ref, own_ref, box_ref, turned, semaphores):
    me = lax.axis_index("box")
    per_device = ZC // CW * YB
    lane = lanes()
    numbers = pltpu.make_async_copy(box_hbm, box_ref, semaphores.at[0])
    numbers.start()
    copies = [
        pltpu.make_async_copy(coarse_hbm.at[:, 0], first_ref, semaphores.at[1]),
        pltpu.make_async_copy(coarse_hbm.at[:, CW - 1], last_ref, semaphores.at[2]),
    ]
    for x in range(CW):
        copies.append(pltpu.make_async_copy(coarse_hbm.at[:, x], turned.at[:, :, x, :], semaphores.at[3 + x]))
    for copy in copies:
        copy.start()
    numbers.wait()
    fill_slots(box_ref, slot_ref, own_ref, me, count, per_device)
    for copy in copies:
        copy.wait()
    spot = jnp.where((lane >= 16) & (lane < 24), lane - 16, jnp.where((lane >= 25) & (lane < 33), lane - 25, -1))

    def edges(block, unused):
        for i in range(4):
            source = block * 4 + i
            before, after = slot_ref[source], slot_ref[2 * count + source]
            ends = [anchors(place_of(box_ref, row, per_device)) for row in (after, before)]
            tiles = [jnp.zeros((8, LN), jnp.float32)] * 2
            for u in range(10):
                f, upper = u // 2, u % 2
                z0, y0 = ends[upper]
                values = (first_ref if upper else last_ref)[f, pl.ds(pl.multiple_of(z0, 8), 8), :]
                tile, base = XUNIT[u]
                moved = roll_to(values, base - y0)
                tiles[tile] = jnp.where(lane >= base, moved, tiles[tile])
            row0 = pl.multiple_of(source * 16, 16)
            out_ref[pl.ds(row0, 8), :] = tiles[0]
            out_ref[pl.ds(row0 + 8, 8), :] = tiles[1]
        return unused

    lax.fori_loop(0, count // 4, edges, 0)

    def faces(pair, unused):
        for i in range(2):
            own = own_ref[1 + jnp.minimum(2 * pair + i, used - 1)]
            row0 = pl.multiple_of(own // NP * 16, 16)
            z0, y0 = anchors(place_of(box_ref, own, per_device))
            below = (z0 - 1) & (ZC - 1)
            above = (z0 + CW) & (ZC - 1)
            sides = [None, None]
            pieces = []
            for f in range(NF):
                piece = jnp.where(lane < 8, roll_to(turned[f, below], -y0), roll_to(turned[f, above], 8 - y0))
                for k in range(CW):
                    piece = jnp.where(spot == k, roll_to(turned[f, z0 + k], 17 + k - y0), piece)
                pieces.append(piece)
            for f in range(NF):
                tile, base = SIDE[f]
                piece = roll_to(pieces[f], base)
                sides[tile] = piece if base == 0 else jnp.where(lane >= base, piece, sides[tile])
            pltpu.store(out_ref.at[pl.ds(row0, 8), :], sides[0], mask=lane < 99)
            pltpu.store(out_ref.at[pl.ds(row0 + 8, 8), :], sides[1], mask=lane < 66)
        return unused

    used = own_ref[0]
    lax.fori_loop(0, (used + 1) // 2, faces, 0)


def spread_kernel(fine_ref, out_ref, semaphores):
    copies = [
        pltpu.make_async_copy(
            fine_ref.at[p, :, :, pl.ds(c * LN, LN)], out_ref.at[:, :, c, p, :], semaphores.at[p * 2 + c]
        )
        for p in range(NP)
        for c in range(2)
    ]
    for copy in copies:
        copy.start()
    for copy in copies:
        copy.wait()


def collect_kernel(state_ref, out_ref, semaphores):
    copies = [
        pltpu.make_async_copy(
            state_ref.at[:, pl.ds(1, FW), c, p, :], out_ref.at[p, :, :, pl.ds(c * LN, LN)], semaphores.at[p * 2 + c]
        )
        for p in range(NP)
        for c in range(2)
    ]
    for copy in copies:
        copy.start()
    for copy in copies:
        copy.wait()


def fine_kernel(
    count,
    box_ref,
    ghost_ref,
    given_ref,
    out_ref,
    last_ref,
    message,
    rows,
    zghost,
    yghost,
    xghost,
    middle,
    carry,
    zsum,
    ysum,
    xsum,
    xpool,
    packed,
):
    per_device = ZC // CW * YB
    me = lax.axis_index("box")
    lane = lanes()
    place_y = lane & 15
    first_y = place_y == 0
    last_y = place_y == 15
    low16 = lane < 16
    high16 = lane < 112

    def slots(p):
        owner, _ = split_box(box_ref[me * NP + p], per_device)
        return owner, jnp.where(owner == 0, count - 1, owner - 1), jnp.where(owner == count - 1, 0, owner + 1)

    for p in range(NP):
        own, before, after = slots(p)
        for tile in range(2):
            start = 99 if tile == 0 else 66
            lower_parity = 0 if tile == 0 else 1
            is_x = lane >= start
            is_lower = (((lane - start) >> 3) & 1) == lower_parity
            pieces = [ghost_ref[pl.ds(pl.multiple_of(s * 16 + tile * 8, 8), 8), :] for s in (own, before, after)]
            message[pl.ds(p * 16 + tile * 8, 8), :] = jnp.where(
                is_x, jnp.where(is_lower, pieces[1], pieces[2]), pieces[0]
            )
    for i in range(16):
        rows[i] = message[pl.ds(i, NP, stride=16), :]
    pair_y = place_y >> 1
    for f in range(NF):
        tile, base = SIDE[f]
        index = jnp.where(lane < 64, base, base + 8) + pair_y
        for r in range(CW):
            zghost[f, r] = take_lanes(rows[tile * 8 + r], index)
        for c in range(2):
            index = jnp.where(place_y < 8, base + 16, base + 25) + (lane >> 5) + 4 * c
            for r in range(CW):
                yghost[f, c, r] = take_lanes(rows[tile * 8 + r], index)
    dense = {}
    for c in range(2):
        for f in range(NF):
            (tile_low, low), (tile_high, high) = XUNIT[2 * f], XUNIT[2 * f + 1]
            for k in range(4):
                moved = roll_to(rows[tile_low * 8 + 4 * c + k], 32 * k - low)
                if (tile_high, high) != (tile_low, low + 8):
                    other = roll_to(rows[tile_high * 8 + 4 * c + k], 32 * k + 8 - high)
                    moved = jnp.where((lane & 15) < 8, moved, other)
                dense[c, f] = moved if k == 0 else jnp.where(lane >= 32 * k, moved, dense[c, f])
    for upper in range(2):
        unfold = (lane & 96) + pair_y + 8 * upper
        for c in range(2):
            for f in range(NF):
                xghost[upper, f, c] = take_lanes(dense[c, f], unfold)
    for half in range(2):
        some = pl.ds(4 * half, 4)
        values = [zghost[f, some] for f in range(NF)]
        for i, v in enumerate(side_of_face(values, primitives(values), 3)[NF:]):
            zghost[NF + i, some] = v
        for c in range(2):
            values = [yghost[f, c, some] for f in range(NF)]
            for i, v in enumerate(side_of_face(values, primitives(values), 2)[NF:]):
                yghost[NF + i, c, some] = v
    for upper in range(2):
        values = [xghost[upper, f] for f in range(NF)]
        for i, v in enumerate(side_of_face(values, primitives(values), 1)[NF:]):
            xghost[upper, NF + i] = v

    step = 0.5 * time_step

    def substep(first):
        target = middle if first else last_ref

        def finish(plane, part, flux):
            for c in range(2):
                for f in range(NF):
                    target[f, plane, c] = part[c][f] - step * flux[c][f]

        for c in range(2):
            for i in range(11):
                carry[i, c] = xghost[0, i, c]
            for f in range(NF):
                carry[11 + f, c] = jnp.zeros((8, LN), jnp.float32)

        def pair(r, unused):
            zg = [zghost[i, r] for i in range(11)]
            zb = [None] * NF
            yb = [[None] * NF for _ in range(2)]
            for half in range(2):
                x = 2 * r + half
                if first:
                    cells = [[given_ref[f, x, c] for f in range(NF)] for c in range(2)]
                else:
                    cells = [[middle[f, x + 1, c] for f in range(NF)] for c in range(2)]
                prims = [primitives(u) for u in cells]
                flux_x = []
                for c in range(2):
                    here = side_of_face(cells[c], prims[c], 1)
                    behind = [carry[i, c] for i in range(11)]
                    flux_x.append(face_flux(behind, here))
                    for i in range(11):
                        carry[i, c] = here[i]
                finish(x, [[carry[11 + f, c] for f in range(NF)] for c in range(2)], flux_x)

                if half == 0:

                    @pl.when(r == 0)
                    def _():
                        for c in range(2):
                            for f in range(NF):
                                value = flux_x[c][f]
                                xsum[0, f, c] = value if first else xsum[0, f, c] + value

                here = [side_of_face(cells[c], prims[c], 3) for c in range(2)]
                turned = [[roll_to(v, 16) for v in here[c]] for c in range(2)]
                left = [
                    [jnp.where(low16, zg[i], turned[0][i]) for i in range(11)],
                    [jnp.where(low16, turned[0][i], turned[1][i]) for i in range(11)],
                ]
                lower = [face_flux(left[c], here[c]) for c in range(2)]
                last = face_flux(here[1], zg)
                change = [[], []]
                for f in range(NF):
                    back = [roll_to(lower[c][f], -16) for c in range(2)]
                    change[0].append(jnp.where(high16, back[0], back[1]) - lower[0][f])
                    change[1].append(jnp.where(high16, back[1], last[f]) - lower[1][f])
                    edge = jnp.where(lane < 64, lower[0][f], last[f])
                    zb[f] = edge if half == 0 else zb[f] + edge
                for c in range(2):
                    yg = [yghost[i, c, r] for i in range(11)]
                    here = side_of_face(cells[c], prims[c], 2)
                    left = [jnp.where(first_y, yg[i], roll_to(here[i], 1)) for i in range(11)]
                    lower_y = face_flux(left, here)
                    last_flux = face_flux(here, yg)
                    for f in range(NF):
                        upper_y = jnp.where(last_y, last_flux[f], roll_to(lower_y[f], -1))
                        change[c][f] = change[c][f] + (upper_y - lower_y[f])
                        edge = jnp.where(place_y < 8, lower_y[f], last_flux[f])
                        yb[c][f] = edge if half == 0 else yb[c][f] + edge
                for c in range(2):
                    for f in range(NF):
                        carry[11 + f, c] = cells[c][f] - step * (change[c][f] - flux_x[c][f])
            for f in range(NF):
                zsum[f, r] = zb[f] if first else zsum[f, r] + zb[f]
                for c in range(2):
                    ysum[f, r, c] = yb[c][f] if first else ysum[f, r, c] + yb[c][f]
            return unused

        lax.fori_loop(0, CW, pair, 0)
        flux_x = [
            face_flux([carry[i, c] for i in range(11)], [xghost[1, i, c] for i in range(11)]) for c in range(2)
        ]
        finish(FW, [[carry[11 + f, c] for f in range(NF)] for c in range(2)], flux_x)
        for c in range(2):
            for f in range(NF):
                value = flux_x[c][f]
                xsum[1, f, c] = value if first else xsum[1, f, c] + value

    substep(True)
    substep(False)

    odd = (lane & 1) == 1
    odd_z = (lane & 16) == 16
    outer = (place_y == 0) | (place_y == 15)

    def shifted(values, shift):
        return [roll_to(v, shift) for v in values]

    def added(left, right):
        return [a + b for a, b in zip(left, right)]

    def dense(values):
        values = added(values, shifted(values, -1))
        return [jnp.where(odd, b, a) for a, b in zip(values, shifted(values, -7))]

    ends = [xsum[side, f, c] for f in range(NF) for side in range(2) for c in range(2)]
    ends = dense(added(ends, shifted(ends, -16)))
    for i, v in enumerate(ends):
        xpool[i] = v
    for f in range(NF):
        sums = [[last_ref[f, 2 * r + 1, c] + last_ref[f, 2 * r + 2, c] for r in range(CW)] for c in range(2)]
        turned = [shifted(sums[0], -1), shifted(sums[1], 1)]
        average = [jnp.where(odd, sums[1][r] + turned[1][r], sums[0][r] + turned[0][r]) for r in range(CW)]
        average = added(average, shifted(average, -16))
        v = [[ysum[f, r, c] for r in range(CW)] for c in range(2)]
        turned = [shifted(v[1], 1), shifted(v[1], -1)]
        fluxes = [
            jnp.where(outer, v[0][r], jnp.where(place_y < 8, turned[0][r], turned[1][r])) for r in range(CW)
        ]
        fluxes = added(fluxes, shifted(fluxes, 16))
        ends = dense([zsum[f, r] for r in range(CW)])
        for low, part in (
            (18, shifted(ends, 18)),
            (114, shifted(ends, 2)),
            (50, [roll_to(xpool[f * 4 + r // 4], 50 - r % 4 * 32) for r in range(CW)]),
            (82, [roll_to(xpool[f * 4 + 2 + r // 4], 82 - r % 4 * 32) for r in range(CW)]),
        ):
            mask = (lane >= low) & (lane < low + 8)
            fluxes = [jnp.where(mask, part[r], fluxes[r]) for r in range(CW)]
        for r in range(CW):
            row = jnp.where(odd_z, fluxes[r] * 0.0625, average[r] * 0.125)
            packed[pl.ds(f * 8 + r, NP, stride=NF * 8), :] = row

    lower_x = (lane >= 50) & (lane < 58)
    upper_x = (lane >= 82) & (lane < 90)
    others = ~(lower_x | upper_x)
    for p in range(NP):
        own, before, after = slots(p)
        for f in range(NF):
            tile = packed[pl.ds(p * 40 + f * 8, 8), :]
            for slot, mask in ((own, others), (before, lower_x), (after, upper_x)):
                target = out_ref.at[pl.ds(pl.multiple_of(slot * 40 + f * 8, 8), 8), :]
                pltpu.store(target, tile, mask=mask)


def coarse_kernel(coarse_ref, low_ref, high_ref, next_ref, yedge_ref, zedge_ref, xedge_ref, carry):
    step = 0.5 * time_step
    upper_edge = (lax.broadcasted_iota(jnp.int32, (ZC, LN), 1) & (CW - 1)) == CW - 1
    values = [low_ref[pl.ds(f * ZC, ZC), :] for f in range(NF)]
    for i, v in enumerate(side_of_face(values, primitives(values), 1)):
        carry[i] = v

    def store(ref, f, x, value):
        ref[pl.ds(pl.multiple_of(f * 256 + x * ZC, ZC), ZC), :] = value

    def plane(x, unused):
        cells = [coarse_ref[pl.ds(pl.multiple_of(f * 256 + x * ZC, ZC), ZC), :] for f in range(NF)]
        prims = primitives(cells)
        here = side_of_face(cells, prims, 1)
        flux_x = face_flux([carry[i] for i in range(11)], here)

        @pl.when(x > 0)
        def _():
            for f in range(NF):
                store(next_ref, f, x - 1, carry[11 + f] - step * flux_x[f])

        @pl.when(x == 0)
        def _():
            for f in range(NF):
                xedge_ref[pl.ds(f * 64, ZC), :] = 0.5 * flux_x[f]

        for i in range(11):
            carry[i] = here[i]
        here = side_of_face(cells, prims, 3)
        left = [pltpu.roll(v, 1, 0) for v in here]
        lower_z = face_flux(left, here)
        here = side_of_face(cells, prims, 2)
        left = [pltpu.roll(v, 1, 1) for v in here]
        lower_y = face_flux(left, here)
        for f in range(NF):
            upper_y = pltpu.roll(lower_y[f], LN - 1, 1)
            change = (pltpu.roll(lower_z[f], ZC - 1, 0) - lower_z[f]) + (upper_y - lower_y[f])
            carry[11 + f] = cells[f] - step * (change - flux_x[f])
            store(yedge_ref, f, x, 0.5 * jnp.where(upper_edge, upper_y, lower_y[f]))
            for k in range(ZC // CW):
                zedge_ref[pl.ds((f * 4 + k) * 8 + x, 1), :] = 0.5 * lower_z[f][k * CW : k * CW + 1, :]
        return unused

    lax.fori_loop(0, CW, plane, 0)
    values = [high_ref[pl.ds(f * ZC, ZC), :] for f in range(NF)]
    flux_x = face_flux([carry[i] for i in range(11)], side_of_face(values, primitives(values), 1))
    for f in range(NF):
        store(next_ref, f, CW - 1, carry[11 + f] - step * flux_x[f])
        xedge_ref[pl.ds(f * 64 + ZC, ZC), :] = 0.5 * flux_x[f]


def apply_kernel(count, box_ref, flag_ref, slot_ref, result_ref, base_ref, yedge_ref, zedge_ref, xedge_ref, out_ref):
    per_device = ZC // CW * YB
    lane = lanes()
    sub = lax.broadcasted_iota(jnp.int32, (8, LN), 0)
    out_ref[...] = base_ref[...]

    def weight(row, face):
        return flag_ref[row, face].astype(jnp.float32) * (time_step if face % 2 else -time_step)

    def one(source, unused):
        before_row, own, after_row = (slot_ref[k * count + source] for k in range(3))
        row0 = pl.multiple_of(source * 40, 8)

        def tile(f):
            return result_ref[pl.ds(row0 + f * 8, 8), :]

        def unmix(y0, first):
            place = lane - y0
            return (first + (place & 3) * 2 + ((place >> 2) & 1)) & (LN - 1)

        for upper in range(2):
            row = before_row if upper else after_row

            @pl.when(row >= 0)
            def _():
                z0, y0 = anchors(place_of(box_ref, row, per_device))
                scale = weight(row, upper)
                inside = (lane >= y0) & (lane < y0 + CW)
                index = unmix(y0, 82 if upper else 50)
                plane = 0 if upper else CW - 1
                places = [pl.ds(pl.multiple_of(f * 256 + plane * ZC + z0, 8), 8) for f in range(NF)]
                new = []
                for f in range(NF):
                    edge = xedge_ref[pl.ds(pl.multiple_of(f * 64 + (1 - upper) * ZC + z0, 8), 8), :]
                    old = out_ref[places[f], :]
                    new.append(jnp.where(inside, old + scale * (take_lanes(tile(f), index) - edge), old))
                for f in range(NF):
                    out_ref[places[f], :] = new[f]

        @pl.when(own >= 0)
        def _():
            place = place_of(box_ref, own, per_device)
            z0, y0 = anchors(place)
            inside = (lane >= y0) & (lane < y0 + CW)
            below = (z0 - 1) & (ZC - 1)
            above = (z0 + CW) & (ZC - 1)
            for upper, target, face in ((0, below, z0), (1, above, above)):
                scale = weight(own, 2 + upper)
                index = unmix(y0, 114 if upper else 18)
                new = []
                for f in range(NF):
                    edge = zedge_ref[pl.ds(pl.multiple_of(f * 32 + face, 8), 8), :]
                    old = out_ref[pl.ds(f * 256 + target, 8, stride=ZC), :]
                    new.append(jnp.where(inside, old + scale * (take_lanes(tile(f), index) - edge), old))
                for f in range(NF):
                    out_ref[pl.ds(f * 256 + target, 8, stride=ZC), :] = new[f]
            before = lane == ((y0 - 1) & (LN - 1))
            after = lane == ((y0 + CW) & (LN - 1))
            part = (sub & 3) * 32 + (sub >> 2)
            faces = jnp.where(before, part + 16, (sub & 3) * 32 + 31 - (sub >> 2))
            index = jnp.where(inside, part + 2 * ((lane - y0) & 7), faces)
            scale = jnp.where(before, weight(own, 4), jnp.where(after, weight(own, 5), 0.0))
            for f in range(NF):
                places = [pl.ds(pl.multiple_of(f * 256 + x * ZC + z0, 8), 8) for x in range(CW)]
                new = []
                for x in range(CW):
                    line = jnp.broadcast_to(result_ref[pl.ds(row0 + f * 8 + x, 1), :], (8, LN))
                    got = take_lanes(line, index)
                    new.append(jnp.where(inside, got, out_ref[places[x], :] + scale * (got - yedge_ref[places[x], :])))
                for x in range(CW):
                    out_ref[places[x], :] = new[x]

        return unused

    lax.fori_loop(0, count, one, 0)


def local(coarse_state, fine_state, patch_box, face_flags):
    count = lax.axis_size("box")
    assert coarse_state.shape == (NF, CW, ZC, LN) and fine_state.shape == (NP, NF, FW, FW * FW)
    coarse = coarse_state.reshape(NF * CW * ZC, LN)
    f32 = jnp.float32
    vmem = pl.BlockSpec(memory_space=pltpu.VMEM)
    smem = pl.BlockSpec(memory_space=pltpu.SMEM)
    hbm = pl.BlockSpec(memory_space=pltpu.HBM)
    anywhere = pl.BlockSpec(memory_space=pl.ANY)

    def shaped(*shape):
        return jax.ShapeDtypeStruct(shape, f32)

    def call(kernel, out_shape, in_specs, out_specs, flops, size, scratch=(), limit=16):
        return pl.pallas_call(
            kernel,
            out_shape=out_shape,
            in_specs=in_specs,
            out_specs=out_specs,
            scratch_shapes=scratch,
            cost_estimate=pl.CostEstimate(flops=flops, bytes_accessed=size, transcendentals=0),
            compiler_params=pltpu.CompilerParams(vmem_limit_bytes=limit * 1024 * 1024),
        )

    packets, first, last, slots, _ = call(
        functools.partial(pack_kernel, count),
        (
            shaped(count * 16, LN),
            shaped(NF, ZC, LN),
            shaped(NF, ZC, LN),
            jax.ShapeDtypeStruct((4 * count,), jnp.int32),
            jax.ShapeDtypeStruct((count + 2,), jnp.int32),
        ),
        [hbm, hbm],
        (vmem, vmem, vmem, smem, smem),
        1000000,
        1000000,
        (
            pltpu.SMEM((count * NP,), jnp.int32),
            pltpu.VMEM((NF, ZC, CW, LN), f32),
            pltpu.SemaphoreType.DMA((3 + CW,)),
        ),
        limit=63,
    )(patch_box, coarse_state)
    arrived = lax.all_to_all(packets.reshape(count, 16, LN), "box", split_axis=0, concat_axis=0, tiled=True)
    ring = [(i, (i + 1) % count) for i in range(count)]
    low = lax.ppermute(last, "box", ring)
    high = lax.ppermute(first, "box", [(b, a) for a, b in ring])
    given = call(
        spread_kernel, shaped(NF, FW, 2, NP, LN), [hbm], vmem, 1000000, 4000000, (pltpu.SemaphoreType.DMA((2 * NP,)),)
    )(fine_state)
    outbox, state = call(
        functools.partial(fine_kernel, count),
        (shaped(count * 40, LN), shaped(NF, FW + 1, 2, NP, LN)),
        [smem, vmem, vmem],
        (vmem, vmem),
        20000000,
        4000000,
        (
            pltpu.VMEM((NP * 16, LN), f32),
            pltpu.VMEM((16, NP, LN), f32),
            pltpu.VMEM((11, CW, 8, LN), f32),
            pltpu.VMEM((11, 2, CW, 8, LN), f32),
            pltpu.VMEM((2, 11, 2, 8, LN), f32),
            pltpu.VMEM((NF, FW + 1, 2, 8, LN), f32),
            pltpu.VMEM((16, 2, 8, LN), f32),
            pltpu.VMEM((NF, CW, 8, LN), f32),
            pltpu.VMEM((NF, CW, 2, 8, LN), f32),
            pltpu.VMEM((2, NF, 2, 8, LN), f32),
            pltpu.VMEM((4 * NF, NP, LN), f32),
            pltpu.VMEM((NP * 40, LN), f32),
        ),
    )(patch_box, arrived.reshape(count * 16, LN), given)
    returned = lax.all_to_all(outbox.reshape(count, 40, LN), "box", split_axis=0, concat_axis=0, tiled=True)
    fine_next = call(
        collect_kernel,
        shaped(*fine_state.shape),
        [vmem],
        anywhere,
        1000000,
        4000000,
        (pltpu.SemaphoreType.DMA((2 * NP,)),),
    )(state)
    size = NF * CW * ZC
    base, yedge, zedge, xedge = call(
        coarse_kernel,
        (shaped(size, LN), shaped(size, LN), shaped(NF * 32, LN), shaped(NF * 2 * ZC, LN)),
        [vmem] * 3,
        (vmem,) * 4,
        10000000,
        4000000,
        (pltpu.VMEM((16, ZC, LN), f32),),
    )(coarse, low.reshape(NF * ZC, LN), high.reshape(NF * ZC, LN))
    coarse_next = call(
        functools.partial(apply_kernel, count), shaped(size, LN), [smem] * 3 + [vmem] * 5, vmem, 2000000, 4000000
    )(patch_box, face_flags, slots, returned.reshape(count * 40, LN), base, yedge, zedge, xedge)
    return coarse_next.reshape(coarse_state.shape), fine_next


def solution(mesh):
    placed = (
        P(None, "box", "grp", None),
        P(("grp", "box"), None, None, None),
        P("grp"),
        P("grp", None),
    )
    return jax.shard_map(
        local,
        mesh=mesh,
        in_specs=placed,
        out_specs=(P(None, "box", "grp", None), P(("grp", "box"), None, None, None)),
        check_vma=False,
    )
```

```python
import functools

import jax
import jax.numpy as jnp
from jax import lax
from jax.experimental import pallas as pl
from jax.experimental.pallas import tpu as pltpu
from jax.sharding import PartitionSpec as P


gas_gamma = 1.4
time_step = 0.05

NF = 5
CW = 8
FW = 16
NP = 8
LN = 128
ZC = 32
YB = LN // CW
SIDE = ((0, 0), (0, 33), (0, 66), (1, 0), (1, 33))
XUNIT = tuple((0, 99 + 8 * u) if u < 3 else (1, 66 + 8 * (u - 3)) for u in range(10))


def take_lanes(values, index):
    return jnp.take_along_axis(values, index, axis=1, mode="promise_in_bounds")


def lanes():
    return lax.broadcasted_iota(jnp.int32, (8, LN), 1)


def roll_to(values, shift):
    if isinstance(shift, int):
        shift = shift % LN
        return values if shift == 0 else pltpu.roll(values, shift, 1)
    return pltpu.roll(values, shift & (LN - 1), 1)


def primitives(state):
    inverse = 1.0 / state[0]
    speeds = [None] + [state[m] * inverse for m in (1, 2, 3)]
    squares = state[1] * speeds[1] + state[2] * speeds[2] + state[3] * speeds[3]
    pressure = (gas_gamma - 1.0) * (state[4] - 0.5 * squares)
    sound = jnp.sqrt(gas_gamma * pressure * inverse)
    return speeds, pressure, sound, state[4] + pressure


def side_of_face(state, prims, m):
    speeds, pressure, sound, total = prims
    v = speeds[m]
    flux = [state[m], state[1] * v, state[2] * v, state[3] * v, total * v]
    flux[m] = flux[m] + pressure
    return list(state) + flux + [jnp.abs(v) + sound]


def face_flux(left, right):
    fastest = jnp.maximum(left[10], right[10])
    return [left[5 + f] + right[5 + f] - fastest * (right[f] - left[f]) for f in range(NF)]


def split_box(number, per_device):
    if per_device & (per_device - 1) == 0:
        return number >> (per_device.bit_length() - 1), number & (per_device - 1)
    owner = lax.div(number, jnp.int32(per_device))
    return owner, number - owner * per_device


def fill_slots(box_ref, slot_ref, own_ref, me, count, per_device):
    def clear(i, unused):
        for k in range(3):
            slot_ref[k * count + i] = jnp.int32(-1)
        return unused

    lax.fori_loop(0, count, clear, 0)
    power = count & (count - 1) == 0
    shifted = me - 1

    def one(source, unused):
        for j in range(NP):
            row = source * NP + j
            owner, _ = split_box(box_ref[row], per_device)
            k = owner - shifted
            if power:
                k = k & (count - 1)
            else:
                k = jnp.where(k < 0, k + count, k)
                k = jnp.where(k >= count, k - count, k)
            slot_ref[jnp.minimum(k, 3) * count + source] = row
        return unused

    lax.fori_loop(0, count, one, 0)

    def listed(source, used):
        row = slot_ref[count + source]
        own_ref[1 + used] = row
        return used + jnp.where(row >= 0, 1, 0)

    own_ref[0] = lax.fori_loop(0, count, listed, 0)


def place_of(box_ref, row, per_device):
    return split_box(box_ref[jnp.maximum(row, 0)], per_device)[1]


def anchors(place):
    return (place >> 4) * CW, (place & (YB - 1)) * CW


def pack_kernel(count, box_hbm, coarse_hbm, out_ref, first_ref, last_ref, slot_ref, own_ref, box_ref, turned, semaphores):
    me = lax.axis_index("box")
    per_device = ZC // CW * YB
    lane = lanes()
    numbers = pltpu.make_async_copy(box_hbm, box_ref, semaphores.at[0])
    numbers.start()
    copies = [
        pltpu.make_async_copy(coarse_hbm.at[:, 0], first_ref, semaphores.at[1]),
        pltpu.make_async_copy(coarse_hbm.at[:, CW - 1], last_ref, semaphores.at[2]),
    ]
    for x in range(CW):
        copies.append(pltpu.make_async_copy(coarse_hbm.at[:, x], turned.at[:, :, x, :], semaphores.at[3 + x]))
    for copy in copies:
        copy.start()
    numbers.wait()
    fill_slots(box_ref, slot_ref, own_ref, me, count, per_device)
    for copy in copies:
        copy.wait()
    spot = jnp.where((lane >= 16) & (lane < 24), lane - 16, jnp.where((lane >= 25) & (lane < 33), lane - 25, -1))

    def edges(block, unused):
        for i in range(4):
            source = block * 4 + i
            before, after = slot_ref[source], slot_ref[2 * count + source]
            ends = [anchors(place_of(box_ref, row, per_device)) for row in (after, before)]
            tiles = [jnp.zeros((8, LN), jnp.float32)] * 2
            for u in range(10):
                f, upper = u // 2, u % 2
                z0, y0 = ends[upper]
                values = (first_ref if upper else last_ref)[f, pl.ds(pl.multiple_of(z0, 8), 8), :]
                tile, base = XUNIT[u]
                moved = roll_to(values, base - y0)
                tiles[tile] = jnp.where(lane >= base, moved, tiles[tile])
            row0 = pl.multiple_of(source * 16, 16)
            out_ref[pl.ds(row0, 8), :] = tiles[0]
            out_ref[pl.ds(row0 + 8, 8), :] = tiles[1]
        return unused

    lax.fori_loop(0, count // 4, edges, 0)

    def faces(pair, unused):
        for i in range(2):
            own = own_ref[1 + jnp.minimum(2 * pair + i, used - 1)]
            row0 = pl.multiple_of(own // NP * 16, 16)
            z0, y0 = anchors(place_of(box_ref, own, per_device))
            below = (z0 - 1) & (ZC - 1)
            above = (z0 + CW) & (ZC - 1)
            sides = [None, None]
            pieces = []
            for f in range(NF):
                piece = jnp.where(lane < 8, roll_to(turned[f, below], -y0), roll_to(turned[f, above], 8 - y0))
                for k in range(CW):
                    piece = jnp.where(spot == k, roll_to(turned[f, z0 + k], 17 + k - y0), piece)
                pieces.append(piece)
            for f in range(NF):
                tile, base = SIDE[f]
                piece = roll_to(pieces[f], base)
                sides[tile] = piece if base == 0 else jnp.where(lane >= base, piece, sides[tile])
            pltpu.store(out_ref.at[pl.ds(row0, 8), :], sides[0], mask=lane < 99)
            pltpu.store(out_ref.at[pl.ds(row0 + 8, 8), :], sides[1], mask=lane < 66)
        return unused

    used = own_ref[0]
    lax.fori_loop(0, (used + 1) // 2, faces, 0)


def interior_kernel(fine_ref, middle_ref, cells_ref, given, carry, semaphores):
    step = 0.5 * time_step
    lane = lanes()
    low16 = lane < 16
    high16 = lane < 112
    first_y = (lane & 15) == 0
    copies = [
        pltpu.make_async_copy(fine_ref.at[p, :, :, pl.ds(c * LN, LN)], given.at[:, :, c, p, :], semaphores.at[p * 2 + c])
        for p in range(NP)
        for c in range(2)
    ]
    for copy in copies:
        copy.start()
    for copy in copies:
        copy.wait()
    for c in range(2):
        cells = [given[f, 0, c] for f in range(NF)]
        for i, v in enumerate(side_of_face(cells, primitives(cells), 1)):
            carry[i, c] = v
        for f in range(NF):
            carry[11 + f, c] = jnp.zeros((8, LN), jnp.float32)

    def pair(r, unused):
        for half in range(2):
            x = 2 * r + half
            cells = [[given[f, x, c] for f in range(NF)] for c in range(2)]
            prims = [primitives(u) for u in cells]
            for c in range(2):
                speeds, pressure, sound, _ = prims[c]
                for i, v in enumerate(cells[c] + [speeds[2], speeds[3], pressure, sound]):
                    cells_ref[i, x, c] = v
            flux_x = []
            for c in range(2):
                here = side_of_face(cells[c], prims[c], 1)
                flux = face_flux([carry[i, c] for i in range(11)], here)
                if half == 0:
                    flux = [jnp.where(r == 0, 0.0, v) for v in flux]
                flux_x.append(flux)
                for i in range(11):
                    carry[i, c] = here[i]
                for f in range(NF):
                    middle_ref[f, x, c] = carry[11 + f, c] - step * flux[f]
            here = [side_of_face(cells[c], prims[c], 3) for c in range(2)]
            turned = [[roll_to(v, 16) for v in here[c]] for c in range(2)]
            left = [turned[0], [jnp.where(low16, turned[0][i], turned[1][i]) for i in range(11)]]
            lower = [face_flux(left[c], here[c]) for c in range(2)]
            lower[0] = [jnp.where(low16, 0.0, v) for v in lower[0]]
            change = [[], []]
            for f in range(NF):
                back = [roll_to(lower[c][f], -16) for c in range(2)]
                change[0].append(jnp.where(high16, back[0], back[1]) - lower[0][f])
                change[1].append(jnp.where(high16, back[1], back[0]) - lower[1][f])
            for c in range(2):
                here = side_of_face(cells[c], prims[c], 2)
                lower_y = face_flux([roll_to(v, 1) for v in here], here)
                lower_y = [jnp.where(first_y, 0.0, v) for v in lower_y]
                for f in range(NF):
                    total = change[c][f] + (roll_to(lower_y[f], -1) - lower_y[f]) - flux_x[c][f]
                    carry[11 + f, c] = cells[c][f] - step * total
        return unused

    lax.fori_loop(0, CW, pair, 0)
    for c in range(2):
        for f in range(NF):
            middle_ref[f, FW, c] = carry[11 + f, c]


def collect_kernel(state_ref, out_ref, semaphores):
    copies = [
        pltpu.make_async_copy(
            state_ref.at[:, pl.ds(1, FW), c, p, :], out_ref.at[p, :, :, pl.ds(c * LN, LN)], semaphores.at[p * 2 + c]
        )
        for p in range(NP)
        for c in range(2)
    ]
    for copy in copies:
        copy.start()
    for copy in copies:
        copy.wait()


def fine_kernel(
    count,
    box_ref,
    ghost_ref,
    middle_ref,
    cells_ref,
    out_ref,
    last_ref,
    message,
    rows,
    zghost,
    yghost,
    xghost,
    middle,
    carry,
    zsum,
    ysum,
    xsum,
    xpool,
    packed,
):
    per_device = ZC // CW * YB
    me = lax.axis_index("box")
    lane = lanes()
    place_y = lane & 15
    first_y = place_y == 0
    last_y = place_y == 15
    low16 = lane < 16
    high16 = lane < 112

    def slots(p):
        owner, _ = split_box(box_ref[me * NP + p], per_device)
        return owner, jnp.where(owner == 0, count - 1, owner - 1), jnp.where(owner == count - 1, 0, owner + 1)

    for p in range(NP):
        own, before, after = slots(p)
        for tile in range(2):
            start = 99 if tile == 0 else 66
            lower_parity = 0 if tile == 0 else 1
            is_x = lane >= start
            is_lower = (((lane - start) >> 3) & 1) == lower_parity
            pieces = [ghost_ref[pl.ds(pl.multiple_of(s * 16 + tile * 8, 8), 8), :] for s in (own, before, after)]
            message[pl.ds(p * 16 + tile * 8, 8), :] = jnp.where(
                is_x, jnp.where(is_lower, pieces[1], pieces[2]), pieces[0]
            )
    for i in range(16):
        rows[i] = message[pl.ds(i, NP, stride=16), :]
    pair_y = place_y >> 1
    for f in range(NF):
        tile, base = SIDE[f]
        index = jnp.where(lane < 64, base, base + 8) + pair_y
        for r in range(CW):
            zghost[f, r] = take_lanes(rows[tile * 8 + r], index)
        for c in range(2):
            index = jnp.where(place_y < 8, base + 16, base + 25) + (lane >> 5) + 4 * c
            for r in range(CW):
                yghost[f, c, r] = take_lanes(rows[tile * 8 + r], index)
    dense = {}
    for c in range(2):
        for f in range(NF):
            (tile_low, low), (tile_high, high) = XUNIT[2 * f], XUNIT[2 * f + 1]
            for k in range(4):
                moved = roll_to(rows[tile_low * 8 + 4 * c + k], 32 * k - low)
                if (tile_high, high) != (tile_low, low + 8):
                    other = roll_to(rows[tile_high * 8 + 4 * c + k], 32 * k + 8 - high)
                    moved = jnp.where((lane & 15) < 8, moved, other)
                dense[c, f] = moved if k == 0 else jnp.where(lane >= 32 * k, moved, dense[c, f])
    for upper in range(2):
        unfold = (lane & 96) + pair_y + 8 * upper
        for c in range(2):
            for f in range(NF):
                xghost[upper, f, c] = take_lanes(dense[c, f], unfold)
    for half in range(2):
        some = pl.ds(4 * half, 4)
        values = [zghost[f, some] for f in range(NF)]
        for i, v in enumerate(side_of_face(values, primitives(values), 3)[NF:]):
            zghost[NF + i, some] = v
        for c in range(2):
            values = [yghost[f, c, some] for f in range(NF)]
            for i, v in enumerate(side_of_face(values, primitives(values), 2)[NF:]):
                yghost[NF + i, c, some] = v
    for upper in range(2):
        values = [xghost[upper, f] for f in range(NF)]
        for i, v in enumerate(side_of_face(values, primitives(values), 1)[NF:]):
            xghost[upper, NF + i] = v

    step = 0.5 * time_step

    sign_z = jnp.where(lane < 64, -1.0, 1.0)
    sign_y = jnp.where(place_y < 8, -1.0, 1.0)
    scale_z = [jnp.where(low16, step, 0.0), jnp.where(high16, 0.0, -step)]
    scale_y = jnp.where(first_y, step, jnp.where(last_y, -step, 0.0))

    def outer_flux(inside, ghost, sign):
        fastest = jnp.maximum(inside[10], ghost[10]) * sign
        return [inside[5 + f] + ghost[5 + f] - fastest * (ghost[f] - inside[f]) for f in range(NF)]

    def outer_faces(r, unused):
        both = pl.ds(2 * r, 2)
        cells = [[cells_ref[i, both, c] for i in range(9)] for c in range(2)]

        def inside(values, m):
            speeds = [None, None, values[5], values[6]]
            return side_of_face(values[:NF], (speeds, values[7], values[8], values[4] + values[7]), m)

        edge = [jnp.where(lane < 64, cells[0][i], cells[1][i]) for i in range(9)]
        flux_z = outer_flux(inside(edge, 3), [zghost[i, r] for i in range(11)], sign_z)
        for f in range(NF):
            zsum[f, r] = flux_z[f][0] + flux_z[f][1]
        for c in range(2):
            flux_y = outer_flux(inside(cells[c], 2), [yghost[i, c, r] for i in range(11)], sign_y)
            for f in range(NF):
                ysum[f, r, c] = flux_y[f][0] + flux_y[f][1]
                old = middle_ref[f, pl.ds(2 * r + 1, 2), c]
                middle[f, both, c] = old + flux_y[f] * scale_y + flux_z[f] * scale_z[c]
        return unused

    lax.fori_loop(0, CW, outer_faces, 0)
    for side, plane in ((0, 0), (1, FW - 1)):
        values = [cells_ref[f, plane] for f in range(NF)]
        sides = [[xghost[side, i] for i in range(11)], side_of_face(values, primitives(values), 1)]
        flux_x = face_flux(*(sides[::-1] if side else sides))
        for f in range(NF):
            xsum[side, f] = flux_x[f]
            middle[f, plane] = middle[f, plane] + (-step if side else step) * flux_x[f]

    def finish(plane, part, flux):
        for c in range(2):
            for f in range(NF):
                last_ref[f, plane, c] = part[c][f] - step * flux[c][f]

    for c in range(2):
        for i in range(11):
            carry[i, c] = xghost[0, i, c]
        for f in range(NF):
            carry[11 + f, c] = jnp.zeros((8, LN), jnp.float32)

    def pair(r, unused):
        zg = [zghost[i, r] for i in range(11)]
        zb = [None] * NF
        yb = [[None] * NF for _ in range(2)]
        for half in range(2):
            x = 2 * r + half
            cells = [[middle[f, x, c] for f in range(NF)] for c in range(2)]
            prims = [primitives(u) for u in cells]
            flux_x = []
            for c in range(2):
                here = side_of_face(cells[c], prims[c], 1)
                behind = [carry[i, c] for i in range(11)]
                flux_x.append(face_flux(behind, here))
                for i in range(11):
                    carry[i, c] = here[i]
            finish(x, [[carry[11 + f, c] for f in range(NF)] for c in range(2)], flux_x)

            if half == 0:

                @pl.when(r == 0)
                def _():
                    for c in range(2):
                        for f in range(NF):
                            xsum[0, f, c] = xsum[0, f, c] + flux_x[c][f]

            here = [side_of_face(cells[c], prims[c], 3) for c in range(2)]
            turned = [[roll_to(v, 16) for v in here[c]] for c in range(2)]
            left = [
                [jnp.where(low16, zg[i], turned[0][i]) for i in range(11)],
                [jnp.where(low16, turned[0][i], turned[1][i]) for i in range(11)],
            ]
            lower = [face_flux(left[c], here[c]) for c in range(2)]
            last = face_flux(here[1], zg)
            change = [[], []]
            for f in range(NF):
                back = [roll_to(lower[c][f], -16) for c in range(2)]
                change[0].append(jnp.where(high16, back[0], back[1]) - lower[0][f])
                change[1].append(jnp.where(high16, back[1], last[f]) - lower[1][f])
                edge = jnp.where(lane < 64, lower[0][f], last[f])
                zb[f] = edge if half == 0 else zb[f] + edge
            for c in range(2):
                yg = [yghost[i, c, r] for i in range(11)]
                here = side_of_face(cells[c], prims[c], 2)
                left = [jnp.where(first_y, yg[i], roll_to(here[i], 1)) for i in range(11)]
                lower_y = face_flux(left, here)
                last_flux = face_flux(here, yg)
                for f in range(NF):
                    upper_y = jnp.where(last_y, last_flux[f], roll_to(lower_y[f], -1))
                    change[c][f] = change[c][f] + (upper_y - lower_y[f])
                    edge = jnp.where(place_y < 8, lower_y[f], last_flux[f])
                    yb[c][f] = edge if half == 0 else yb[c][f] + edge
            for c in range(2):
                for f in range(NF):
                    carry[11 + f, c] = cells[c][f] - step * (change[c][f] - flux_x[c][f])
        for f in range(NF):
            zsum[f, r] = zsum[f, r] + zb[f]
            for c in range(2):
                ysum[f, r, c] = ysum[f, r, c] + yb[c][f]
        return unused

    lax.fori_loop(0, CW, pair, 0)
    flux_x = [face_flux([carry[i, c] for i in range(11)], [xghost[1, i, c] for i in range(11)]) for c in range(2)]
    finish(FW, [[carry[11 + f, c] for f in range(NF)] for c in range(2)], flux_x)
    for c in range(2):
        for f in range(NF):
            xsum[1, f, c] = xsum[1, f, c] + flux_x[c][f]

    odd = (lane & 1) == 1
    odd_z = (lane & 16) == 16
    outer = (place_y == 0) | (place_y == 15)

    def shifted(values, shift):
        return [roll_to(v, shift) for v in values]

    def added(left, right):
        return [a + b for a, b in zip(left, right)]

    def dense(values):
        values = added(values, shifted(values, -1))
        return [jnp.where(odd, b, a) for a, b in zip(values, shifted(values, -7))]

    ends = [xsum[side, f, c] for f in range(NF) for side in range(2) for c in range(2)]
    ends = dense(added(ends, shifted(ends, -16)))
    for i, v in enumerate(ends):
        xpool[i] = v
    for f in range(NF):
        sums = [[last_ref[f, 2 * r + 1, c] + last_ref[f, 2 * r + 2, c] for r in range(CW)] for c in range(2)]
        turned = [shifted(sums[0], -1), shifted(sums[1], 1)]
        average = [jnp.where(odd, sums[1][r] + turned[1][r], sums[0][r] + turned[0][r]) for r in range(CW)]
        average = added(average, shifted(average, -16))
        v = [[ysum[f, r, c] for r in range(CW)] for c in range(2)]
        turned = [shifted(v[1], 1), shifted(v[1], -1)]
        fluxes = [
            jnp.where(outer, v[0][r], jnp.where(place_y < 8, turned[0][r], turned[1][r])) for r in range(CW)
        ]
        fluxes = added(fluxes, shifted(fluxes, 16))
        ends = dense([zsum[f, r] for r in range(CW)])
        for low, part in (
            (18, shifted(ends, 18)),
            (114, shifted(ends, 2)),
            (50, [roll_to(xpool[f * 4 + r // 4], 50 - r % 4 * 32) for r in range(CW)]),
            (82, [roll_to(xpool[f * 4 + 2 + r // 4], 82 - r % 4 * 32) for r in range(CW)]),
        ):
            mask = (lane >= low) & (lane < low + 8)
            fluxes = [jnp.where(mask, part[r], fluxes[r]) for r in range(CW)]
        for r in range(CW):
            row = jnp.where(odd_z, fluxes[r] * 0.0625, average[r] * 0.125)
            packed[pl.ds(f * 8 + r, NP, stride=NF * 8), :] = row

    lower_x = (lane >= 50) & (lane < 58)
    upper_x = (lane >= 82) & (lane < 90)
    others = ~(lower_x | upper_x)
    for p in range(NP):
        own, before, after = slots(p)
        for f in range(NF):
            tile = packed[pl.ds(p * 40 + f * 8, 8), :]
            for slot, mask in ((own, others), (before, lower_x), (after, upper_x)):
                target = out_ref.at[pl.ds(pl.multiple_of(slot * 40 + f * 8, 8), 8), :]
                pltpu.store(target, tile, mask=mask)


def coarse_kernel(coarse_ref, low_ref, high_ref, next_ref, yedge_ref, zedge_ref, xedge_ref, carry):
    step = 0.5 * time_step
    upper_edge = (lax.broadcasted_iota(jnp.int32, (ZC, LN), 1) & (CW - 1)) == CW - 1
    values = [low_ref[pl.ds(f * ZC, ZC), :] for f in range(NF)]
    for i, v in enumerate(side_of_face(values, primitives(values), 1)):
        carry[i] = v

    def store(ref, f, x, value):
        ref[pl.ds(pl.multiple_of(f * 256 + x * ZC, ZC), ZC), :] = value

    def plane(x, unused):
        cells = [coarse_ref[pl.ds(pl.multiple_of(f * 256 + x * ZC, ZC), ZC), :] for f in range(NF)]
        prims = primitives(cells)
        here = side_of_face(cells, prims, 1)
        flux_x = face_flux([carry[i] for i in range(11)], here)

        @pl.when(x > 0)
        def _():
            for f in range(NF):
                store(next_ref, f, x - 1, carry[11 + f] - step * flux_x[f])

        @pl.when(x == 0)
        def _():
            for f in range(NF):
                xedge_ref[pl.ds(f * 64, ZC), :] = 0.5 * flux_x[f]

        for i in range(11):
            carry[i] = here[i]
        here = side_of_face(cells, prims, 3)
        left = [pltpu.roll(v, 1, 0) for v in here]
        lower_z = face_flux(left, here)
        here = side_of_face(cells, prims, 2)
        left = [pltpu.roll(v, 1, 1) for v in here]
        lower_y = face_flux(left, here)
        for f in range(NF):
            upper_y = pltpu.roll(lower_y[f], LN - 1, 1)
            change = (pltpu.roll(lower_z[f], ZC - 1, 0) - lower_z[f]) + (upper_y - lower_y[f])
            carry[11 + f] = cells[f] - step * (change - flux_x[f])
            store(yedge_ref, f, x, 0.5 * jnp.where(upper_edge, upper_y, lower_y[f]))
            for k in range(ZC // CW):
                zedge_ref[pl.ds((f * 4 + k) * 8 + x, 1), :] = 0.5 * lower_z[f][k * CW : k * CW + 1, :]
        return unused

    lax.fori_loop(0, CW, plane, 0)
    values = [high_ref[pl.ds(f * ZC, ZC), :] for f in range(NF)]
    flux_x = face_flux([carry[i] for i in range(11)], side_of_face(values, primitives(values), 1))
    for f in range(NF):
        store(next_ref, f, CW - 1, carry[11 + f] - step * flux_x[f])
        xedge_ref[pl.ds(f * 64 + ZC, ZC), :] = 0.5 * flux_x[f]


def apply_kernel(count, slot_ref, result_ref, base_ref, yedge_ref, zedge_ref, xedge_ref, out_ref, zsum):
    per_device = ZC // CW * YB
    lane = lanes()
    sub = lax.broadcasted_iota(jnp.int32, (8, LN), 0)
    out_ref[...] = base_ref[...]
    zsum[...] = jnp.zeros(zsum.shape, jnp.float32)

    def place_of(row):
        return split_box(slot_ref[4 * count + row], per_device)[1]

    def weight(row, face):
        return slot_ref[(4 + NP) * count + row * 6 + face].astype(jnp.float32) * (time_step if face % 2 else -time_step)

    def one(source, unused):
        before_row, own, after_row = (slot_ref[k * count + source] for k in range(3))
        row0 = pl.multiple_of(source * 40, 8)

        def tile(f):
            return result_ref[pl.ds(row0 + f * 8, 8), :]

        def unmix(y0, first):
            place = lane - y0
            return (first + (place & 3) * 2 + ((place >> 2) & 1)) & (LN - 1)

        for upper in range(2):
            row = before_row if upper else after_row

            @pl.when(row >= 0)
            def _():
                z0, y0 = anchors(place_of(row))
                scale = weight(row, upper)
                inside = (lane >= y0) & (lane < y0 + CW)
                index = unmix(y0, 82 if upper else 50)
                plane = 0 if upper else CW - 1
                new, places = [], []
                for f in range(NF):
                    place = pl.ds(pl.multiple_of(f * 256 + plane * ZC + z0, 8), 8)
                    edge = xedge_ref[pl.ds(pl.multiple_of(f * 64 + (1 - upper) * ZC + z0, 8), 8), :]
                    old = out_ref[place, :]
                    places.append(place)
                    new.append(jnp.where(inside, old + scale * (take_lanes(tile(f), index) - edge), old))
                for place, value in zip(places, new):
                    out_ref[place, :] = value

        @pl.when(own >= 0)
        def _():
            z0, y0 = anchors(place_of(own))
            inside = (lane >= y0) & (lane < y0 + CW)
            block = z0 >> 3
            for upper, target, face in ((0, (block - 1) & 3, block), (1, (block + 1) & 3, (block + 1) & 3)):
                scale = jnp.where(inside, weight(own, 2 + upper), 0.0)
                index = unmix(y0, 114 if upper else 18)
                for f in range(NF):
                    edge = zedge_ref[pl.ds(pl.multiple_of(f * 32 + face * 8, 8), 8), :]
                    part = jnp.where(inside, take_lanes(tile(f), index) - edge, 0.0)
                    zsum[f, upper, target] = zsum[f, upper, target] + scale * part
            before = lane == ((y0 - 1) & (LN - 1))
            after = lane == ((y0 + CW) & (LN - 1))
            part = (sub & 3) * 32 + (sub >> 2)
            faces = jnp.where(before, part + 16, (sub & 3) * 32 + 31 - (sub >> 2))
            index = jnp.where(inside, part + 2 * ((lane - y0) & 7), faces)
            scale = jnp.where(before, weight(own, 4), jnp.where(after, weight(own, 5), 0.0))
            for f in range(NF):
                new, places = [], []
                for x in range(CW):
                    place = pl.ds(pl.multiple_of(f * 256 + x * ZC + z0, 8), 8)
                    line = jnp.broadcast_to(result_ref[pl.ds(row0 + f * 8 + x, 1), :], (8, LN))
                    got = take_lanes(line, index)
                    places.append(place)
                    new.append(jnp.where(inside, got, out_ref[place, :] + scale * (got - yedge_ref[place, :])))
                for place, value in zip(places, new):
                    out_ref[place, :] = value

        return unused

    lax.fori_loop(0, count, one, 0)
    for f in range(NF):
        for x in range(CW):
            for block in range(ZC // CW):
                for upper in range(2):
                    row = pl.ds(f * 256 + x * ZC + block * 8 + (0 if upper else 7), 1)
                    out_ref[row, :] = out_ref[row, :] + zsum[f, upper, block, x : x + 1]


def local(coarse_state, fine_state, patch_box, face_flags):
    count = lax.axis_size("box")
    assert coarse_state.shape == (NF, CW, ZC, LN) and fine_state.shape == (NP, NF, FW, FW * FW)
    coarse = coarse_state.reshape(NF * CW * ZC, LN)
    f32 = jnp.float32
    vmem = pl.BlockSpec(memory_space=pltpu.VMEM)
    smem = pl.BlockSpec(memory_space=pltpu.SMEM)
    hbm = pl.BlockSpec(memory_space=pltpu.HBM)
    anywhere = pl.BlockSpec(memory_space=pl.ANY)

    def shaped(*shape):
        return jax.ShapeDtypeStruct(shape, f32)

    def call(kernel, out_shape, in_specs, out_specs, flops, size, scratch=(), limit=16):
        return pl.pallas_call(
            kernel,
            out_shape=out_shape,
            in_specs=in_specs,
            out_specs=out_specs,
            scratch_shapes=scratch,
            cost_estimate=pl.CostEstimate(flops=flops, bytes_accessed=size, transcendentals=0),
            compiler_params=pltpu.CompilerParams(vmem_limit_bytes=limit * 1024 * 1024),
        )

    packets, first, last, slots, _ = call(
        functools.partial(pack_kernel, count),
        (
            shaped(count * 16, LN),
            shaped(NF, ZC, LN),
            shaped(NF, ZC, LN),
            jax.ShapeDtypeStruct((4 * count,), jnp.int32),
            jax.ShapeDtypeStruct((count + 2,), jnp.int32),
        ),
        [hbm, hbm],
        (vmem, vmem, vmem, smem, smem),
        1000000,
        1000000,
        (
            pltpu.SMEM((count * NP,), jnp.int32),
            pltpu.VMEM((NF, ZC, CW, LN), f32),
            pltpu.SemaphoreType.DMA((3 + CW,)),
        ),
        limit=63,
    )(patch_box, coarse_state)
    arrived = lax.all_to_all(packets.reshape(count, 16, LN), "box", split_axis=0, concat_axis=0, tiled=True)
    ring = [(i, (i + 1) % count) for i in range(count)]
    low = lax.ppermute(last, "box", ring)
    high = lax.ppermute(first, "box", [(b, a) for a, b in ring])
    middle, cells = call(
        interior_kernel,
        (
            shaped(NF, FW + 1, 2, NP, LN),
            shaped(9, FW, 2, NP, LN),
        ),
        [hbm],
        (vmem, vmem),
        10000000,
        4000000,
        (
            pltpu.VMEM((NF, FW, 2, NP, LN), f32),
            pltpu.VMEM((16, 2, 8, LN), f32),
            pltpu.SemaphoreType.DMA((2 * NP,)),
        ),
    )(fine_state)
    outbox, state = call(
        functools.partial(fine_kernel, count),
        (shaped(count * 40, LN), shaped(NF, FW + 1, 2, NP, LN)),
        [smem] + [vmem] * 3,
        (vmem, vmem),
        20000000,
        4000000,
        (
            pltpu.VMEM((NP * 16, LN), f32),
            pltpu.VMEM((16, NP, LN), f32),
            pltpu.VMEM((11, CW, 8, LN), f32),
            pltpu.VMEM((11, 2, CW, 8, LN), f32),
            pltpu.VMEM((2, 11, 2, 8, LN), f32),
            pltpu.VMEM((NF, FW, 2, 8, LN), f32),
            pltpu.VMEM((16, 2, 8, LN), f32),
            pltpu.VMEM((NF, CW, 8, LN), f32),
            pltpu.VMEM((NF, CW, 2, 8, LN), f32),
            pltpu.VMEM((2, NF, 2, 8, LN), f32),
            pltpu.VMEM((4 * NF, NP, LN), f32),
            pltpu.VMEM((NP * 40, LN), f32),
        ),
    )(patch_box, arrived.reshape(count * 16, LN), middle, cells)
    returned = lax.all_to_all(outbox.reshape(count, 40, LN), "box", split_axis=0, concat_axis=0, tiled=True)
    fine_next = call(
        collect_kernel,
        shaped(*fine_state.shape),
        [vmem],
        anywhere,
        1000000,
        4000000,
        (pltpu.SemaphoreType.DMA((2 * NP,)),),
    )(state)
    tables = jnp.concatenate([slots, patch_box, face_flags.reshape(-1)])
    size = NF * CW * ZC
    base, yedge, zedge, xedge = call(
        coarse_kernel,
        (shaped(size, LN), shaped(size, LN), shaped(NF * 32, LN), shaped(NF * 2 * ZC, LN)),
        [vmem] * 3,
        (vmem,) * 4,
        10000000,
        4000000,
        (pltpu.VMEM((16, ZC, LN), f32),),
    )(coarse, low.reshape(NF * ZC, LN), high.reshape(NF * ZC, LN))
    coarse_next = call(
        functools.partial(apply_kernel, count),
        shaped(size, LN),
        [smem] + [vmem] * 5,
        vmem,
        2000000,
        4000000,
        (pltpu.VMEM((NF, 2, ZC // CW, CW, LN), f32),),
    )(tables, returned.reshape(count * 40, LN), base, yedge, zedge, xedge)
    return coarse_next.reshape(coarse_state.shape), fine_next


def solution(mesh):
    placed = (
        P(None, "box", "grp", None),
        P(("grp", "box"), None, None, None),
        P("grp"),
        P("grp", None),
    )
    return jax.shard_map(
        local,
        mesh=mesh,
        in_specs=placed,
        out_specs=(P(None, "box", "grp", None), P(("grp", "box"), None, None, None)),
        check_vma=False,
    )
```

```python
import functools

import jax
import jax.numpy as jnp
from jax import lax
from jax.experimental import pallas as pl
from jax.experimental.pallas import tpu as pltpu
from jax.sharding import PartitionSpec as P


gas_gamma = 1.4
time_step = 0.05

NF = 5
CW = 8
FW = 16
NP = 8
LN = 128
ZC = 32
YB = LN // CW
SIDE = ((0, 0), (0, 33), (0, 66), (1, 0), (1, 33))
XUNIT = tuple((0, 99 + 8 * u) if u < 3 else (1, 66 + 8 * (u - 3)) for u in range(10))


def take_lanes(values, index):
    return jnp.take_along_axis(values, index, axis=1, mode="promise_in_bounds")


def lanes():
    return lax.broadcasted_iota(jnp.int32, (8, LN), 1)


def roll_to(values, shift):
    if isinstance(shift, int):
        shift = shift % LN
        return values if shift == 0 else pltpu.roll(values, shift, 1)
    return pltpu.roll(values, shift & (LN - 1), 1)


def primitives(state):
    inverse = 1.0 / state[0]
    speeds = [None] + [state[m] * inverse for m in (1, 2, 3)]
    squares = state[1] * speeds[1] + state[2] * speeds[2] + state[3] * speeds[3]
    pressure = (gas_gamma - 1.0) * (state[4] - 0.5 * squares)
    sound = jnp.sqrt(gas_gamma * pressure * inverse)
    return speeds, pressure, sound, state[4] + pressure


def side_of_face(state, prims, m):
    speeds, pressure, sound, total = prims
    v = speeds[m]
    flux = [state[m], state[1] * v, state[2] * v, state[3] * v, total * v]
    flux[m] = flux[m] + pressure
    return list(state) + flux + [jnp.abs(v) + sound]


def face_flux(left, right):
    fastest = jnp.maximum(left[10], right[10])
    return [left[5 + f] + right[5 + f] - fastest * (right[f] - left[f]) for f in range(NF)]


def split_box(number, per_device):
    if per_device & (per_device - 1) == 0:
        return number >> (per_device.bit_length() - 1), number & (per_device - 1)
    owner = lax.div(number, jnp.int32(per_device))
    return owner, number - owner * per_device


def fill_slots(box_ref, slot_ref, own_ref, me, count, per_device):
    def clear(i, unused):
        for k in range(3):
            slot_ref[k * count + i] = jnp.int32(-1)
        return unused

    lax.fori_loop(0, count, clear, 0)
    power = count & (count - 1) == 0
    shifted = me - 1

    def one(source, unused):
        for j in range(NP):
            row = source * NP + j
            owner, _ = split_box(box_ref[row], per_device)
            k = owner - shifted
            if power:
                k = k & (count - 1)
            else:
                k = jnp.where(k < 0, k + count, k)
                k = jnp.where(k >= count, k - count, k)
            slot_ref[jnp.minimum(k, 3) * count + source] = row
        return unused

    lax.fori_loop(0, count, one, 0)

    def listed(source, used):
        row = slot_ref[count + source]
        own_ref[1 + used] = row
        return used + jnp.where(row >= 0, 1, 0)

    own_ref[0] = lax.fori_loop(0, count, listed, 0)


def place_of(box_ref, row, per_device):
    return split_box(box_ref[jnp.maximum(row, 0)], per_device)[1]


def anchors(place):
    return (place >> 4) * CW, (place & (YB - 1)) * CW


def pack_kernel(count, box_hbm, coarse_hbm, out_ref, first_ref, last_ref, slot_ref, own_ref, box_ref, turned, semaphores):
    me = lax.axis_index("box")
    per_device = ZC // CW * YB
    lane = lanes()
    numbers = pltpu.make_async_copy(box_hbm, box_ref, semaphores.at[0])
    numbers.start()
    copies = [
        pltpu.make_async_copy(coarse_hbm.at[:, 0], first_ref, semaphores.at[1]),
        pltpu.make_async_copy(coarse_hbm.at[:, CW - 1], last_ref, semaphores.at[2]),
    ]
    for x in range(CW):
        copies.append(pltpu.make_async_copy(coarse_hbm.at[:, x], turned.at[:, :, x, :], semaphores.at[3 + x]))
    for copy in copies:
        copy.start()
    numbers.wait()
    fill_slots(box_ref, slot_ref, own_ref, me, count, per_device)
    for copy in copies[:2]:
        copy.wait()
    spot = jnp.where((lane >= 16) & (lane < 24), lane - 16, jnp.where((lane >= 25) & (lane < 33), lane - 25, -1))

    def edges(block, unused):
        for i in range(4):
            source = block * 4 + i
            before, after = slot_ref[source], slot_ref[2 * count + source]
            ends = [anchors(place_of(box_ref, row, per_device)) for row in (after, before)]
            tiles = [jnp.zeros((8, LN), jnp.float32)] * 2
            for u in range(10):
                f, upper = u // 2, u % 2
                z0, y0 = ends[upper]
                values = (first_ref if upper else last_ref)[f, pl.ds(pl.multiple_of(z0, 8), 8), :]
                tile, base = XUNIT[u]
                moved = roll_to(values, base - y0)
                tiles[tile] = jnp.where(lane >= base, moved, tiles[tile])
            row0 = pl.multiple_of(source * 16, 16)
            out_ref[pl.ds(row0, 8), :] = tiles[0]
            out_ref[pl.ds(row0 + 8, 8), :] = tiles[1]
        return unused

    lax.fori_loop(0, count // 4, edges, 0)
    for copy in copies[2:]:
        copy.wait()

    def faces(pair, unused):
        for i in range(2):
            own = own_ref[1 + jnp.minimum(2 * pair + i, used - 1)]
            row0 = pl.multiple_of(own // NP * 16, 16)
            z0, y0 = anchors(place_of(box_ref, own, per_device))
            below = (z0 - 1) & (ZC - 1)
            above = (z0 + CW) & (ZC - 1)
            sides = [None, None]
            pieces = []
            for f in range(NF):
                piece = jnp.where(lane < 8, roll_to(turned[f, below], -y0), roll_to(turned[f, above], 8 - y0))
                for k in range(CW):
                    piece = jnp.where(spot == k, roll_to(turned[f, z0 + k], 17 + k - y0), piece)
                pieces.append(piece)
            for f in range(NF):
                tile, base = SIDE[f]
                piece = roll_to(pieces[f], base)
                sides[tile] = piece if base == 0 else jnp.where(lane >= base, piece, sides[tile])
            pltpu.store(out_ref.at[pl.ds(row0, 8), :], sides[0], mask=lane < 99)
            pltpu.store(out_ref.at[pl.ds(row0 + 8, 8), :], sides[1], mask=lane < 66)
        return unused

    used = own_ref[0]
    lax.fori_loop(0, (used + 1) // 2, faces, 0)


def interior_kernel(fine_ref, middle_ref, cells_ref, given, carry, semaphores):
    step = 0.5 * time_step
    lane = lanes()
    low16 = lane < 16
    high16 = lane < 112
    first_y = (lane & 15) == 0
    copies = [
        pltpu.make_async_copy(fine_ref.at[p, :, :, pl.ds(c * LN, LN)], given.at[:, :, c, p, :], semaphores.at[p * 2 + c])
        for p in range(NP)
        for c in range(2)
    ]
    for copy in copies:
        copy.start()
    for copy in copies:
        copy.wait()
    for c in range(2):
        cells = [given[f, 0, c] for f in range(NF)]
        for i, v in enumerate(side_of_face(cells, primitives(cells), 1)):
            carry[i, c] = v
        for f in range(NF):
            carry[11 + f, c] = jnp.zeros((8, LN), jnp.float32)

    def pair(r, unused):
        for half in range(2):
            x = 2 * r + half
            cells = [[given[f, x, c] for f in range(NF)] for c in range(2)]
            prims = [primitives(u) for u in cells]
            for c in range(2):
                speeds, pressure, sound, _ = prims[c]
                for i, v in enumerate(cells[c] + [speeds[2], speeds[3], pressure, sound]):
                    cells_ref[i, x, c] = v
            flux_x = []
            for c in range(2):
                here = side_of_face(cells[c], prims[c], 1)
                flux = face_flux([carry[i, c] for i in range(11)], here)
                if half == 0:
                    flux = [jnp.where(r == 0, 0.0, v) for v in flux]
                flux_x.append(flux)
                for i in range(11):
                    carry[i, c] = here[i]
                for f in range(NF):
                    middle_ref[f, x, c] = carry[11 + f, c] - step * flux[f]
            here = [side_of_face(cells[c], prims[c], 3) for c in range(2)]
            turned = [[roll_to(v, 16) for v in here[c]] for c in range(2)]
            left = [turned[0], [jnp.where(low16, turned[0][i], turned[1][i]) for i in range(11)]]
            lower = [face_flux(left[c], here[c]) for c in range(2)]
            lower[0] = [jnp.where(low16, 0.0, v) for v in lower[0]]
            change = [[], []]
            for f in range(NF):
                back = [roll_to(lower[c][f], -16) for c in range(2)]
                change[0].append(jnp.where(high16, back[0], back[1]) - lower[0][f])
                change[1].append(jnp.where(high16, back[1], back[0]) - lower[1][f])
            for c in range(2):
                here = side_of_face(cells[c], prims[c], 2)
                lower_y = face_flux([roll_to(v, 1) for v in here], here)
                lower_y = [jnp.where(first_y, 0.0, v) for v in lower_y]
                for f in range(NF):
                    total = change[c][f] + (roll_to(lower_y[f], -1) - lower_y[f]) - flux_x[c][f]
                    carry[11 + f, c] = cells[c][f] - step * total
        return unused

    lax.fori_loop(0, CW, pair, 0)
    for c in range(2):
        for f in range(NF):
            middle_ref[f, FW, c] = carry[11 + f, c]


def collect_kernel(state_ref, out_ref, semaphores):
    copies = [
        pltpu.make_async_copy(
            state_ref.at[:, pl.ds(1, FW), c, p, :], out_ref.at[p, :, :, pl.ds(c * LN, LN)], semaphores.at[p * 2 + c]
        )
        for p in range(NP)
        for c in range(2)
    ]
    for copy in copies:
        copy.start()
    for copy in copies:
        copy.wait()


def fine_kernel(
    count,
    box_ref,
    ghost_ref,
    middle_ref,
    cells_ref,
    out_ref,
    last_ref,
    message,
    rows,
    zghost,
    yghost,
    xghost,
    middle,
    carry,
    zsum,
    ysum,
    xsum,
    xpool,
    packed,
):
    per_device = ZC // CW * YB
    me = lax.axis_index("box")
    lane = lanes()
    place_y = lane & 15
    first_y = place_y == 0
    last_y = place_y == 15
    low16 = lane < 16
    high16 = lane < 112

    def slots(p):
        owner, _ = split_box(box_ref[me * NP + p], per_device)
        return owner, jnp.where(owner == 0, count - 1, owner - 1), jnp.where(owner == count - 1, 0, owner + 1)

    for p in range(NP):
        own, before, after = slots(p)
        for tile in range(2):
            start = 99 if tile == 0 else 66
            lower_parity = 0 if tile == 0 else 1
            is_x = lane >= start
            is_lower = (((lane - start) >> 3) & 1) == lower_parity
            pieces = [ghost_ref[pl.ds(pl.multiple_of(s * 16 + tile * 8, 8), 8), :] for s in (own, before, after)]
            message[pl.ds(p * 16 + tile * 8, 8), :] = jnp.where(
                is_x, jnp.where(is_lower, pieces[1], pieces[2]), pieces[0]
            )
    for i in range(16):
        rows[i] = message[pl.ds(i, NP, stride=16), :]
    pair_y = place_y >> 1
    for f in range(NF):
        tile, base = SIDE[f]
        index = jnp.where(lane < 64, base, base + 8) + pair_y
        for r in range(CW):
            zghost[f, r] = take_lanes(rows[tile * 8 + r], index)
        for c in range(2):
            index = jnp.where(place_y < 8, base + 16, base + 25) + (lane >> 5) + 4 * c
            for r in range(CW):
                yghost[f, c, r] = take_lanes(rows[tile * 8 + r], index)
    dense = {}
    for c in range(2):
        for f in range(NF):
            (tile_low, low), (tile_high, high) = XUNIT[2 * f], XUNIT[2 * f + 1]
            for k in range(4):
                moved = roll_to(rows[tile_low * 8 + 4 * c + k], 32 * k - low)
                if (tile_high, high) != (tile_low, low + 8):
                    other = roll_to(rows[tile_high * 8 + 4 * c + k], 32 * k + 8 - high)
                    moved = jnp.where((lane & 15) < 8, moved, other)
                dense[c, f] = moved if k == 0 else jnp.where(lane >= 32 * k, moved, dense[c, f])
    for upper in range(2):
        unfold = (lane & 96) + pair_y + 8 * upper
        for c in range(2):
            for f in range(NF):
                xghost[upper, f, c] = take_lanes(dense[c, f], unfold)
    for half in range(2):
        some = pl.ds(4 * half, 4)
        values = [zghost[f, some] for f in range(NF)]
        for i, v in enumerate(side_of_face(values, primitives(values), 3)[NF:]):
            zghost[NF + i, some] = v
        for c in range(2):
            values = [yghost[f, c, some] for f in range(NF)]
            for i, v in enumerate(side_of_face(values, primitives(values), 2)[NF:]):
                yghost[NF + i, c, some] = v
    for upper in range(2):
        values = [xghost[upper, f] for f in range(NF)]
        for i, v in enumerate(side_of_face(values, primitives(values), 1)[NF:]):
            xghost[upper, NF + i] = v

    step = 0.5 * time_step

    sign_z = jnp.where(lane < 64, -1.0, 1.0)
    sign_y = jnp.where(place_y < 8, -1.0, 1.0)
    scale_z = [jnp.where(low16, step, 0.0), jnp.where(high16, 0.0, -step)]
    scale_y = jnp.where(first_y, step, jnp.where(last_y, -step, 0.0))

    def outer_flux(inside, ghost, sign):
        fastest = jnp.maximum(inside[10], ghost[10]) * sign
        return [inside[5 + f] + ghost[5 + f] - fastest * (ghost[f] - inside[f]) for f in range(NF)]

    def outer_faces(r, unused):
        both = pl.ds(2 * r, 2)
        cells = [[cells_ref[i, both, c] for i in range(9)] for c in range(2)]

        def inside(values, m):
            speeds = [None, None, values[5], values[6]]
            return side_of_face(values[:NF], (speeds, values[7], values[8], values[4] + values[7]), m)

        edge = [jnp.where(lane < 64, cells[0][i], cells[1][i]) for i in range(9)]
        flux_z = outer_flux(inside(edge, 3), [zghost[i, r] for i in range(11)], sign_z)
        for f in range(NF):
            zsum[f, r] = flux_z[f][0] + flux_z[f][1]
        for c in range(2):
            flux_y = outer_flux(inside(cells[c], 2), [yghost[i, c, r] for i in range(11)], sign_y)
            for f in range(NF):
                ysum[f, r, c] = flux_y[f][0] + flux_y[f][1]
                old = middle_ref[f, pl.ds(2 * r + 1, 2), c]
                middle[f, both, c] = old + flux_y[f] * scale_y + flux_z[f] * scale_z[c]
        return unused

    lax.fori_loop(0, CW, outer_faces, 0)
    for side, plane in ((0, 0), (1, FW - 1)):
        values = [cells_ref[f, plane] for f in range(NF)]
        sides = [[xghost[side, i] for i in range(11)], side_of_face(values, primitives(values), 1)]
        flux_x = face_flux(*(sides[::-1] if side else sides))
        for f in range(NF):
            xsum[side, f] = flux_x[f]
            middle[f, plane] = middle[f, plane] + (-step if side else step) * flux_x[f]

    def raw_of(cells, prims, m):
        return cells + [prims[0][m], prims[1], prims[2]]

    def side_of_raw(raw, m):
        speeds = [None] * 4
        speeds[m] = raw[5]
        return side_of_face(raw[:NF], (speeds, raw[6], raw[7], raw[4] + raw[6]), m)

    def finish(plane, part, flux):
        for c in range(2):
            for f in range(NF):
                last_ref[f, plane, c] = part[c][f] - step * flux[c][f]

    for c in range(2):
        for i in range(11):
            carry[i, c] = xghost[0, i, c]
        for f in range(NF):
            carry[11 + f, c] = jnp.zeros((8, LN), jnp.float32)

    def pair(r, unused):
        zg = [zghost[i, r] for i in range(11)]
        zb = [None] * NF
        yb = [[None] * NF for _ in range(2)]
        for half in range(2):
            x = 2 * r + half
            cells = [[middle[f, x, c] for f in range(NF)] for c in range(2)]
            prims = [primitives(u) for u in cells]
            flux_x = []
            for c in range(2):
                here = side_of_face(cells[c], prims[c], 1)
                behind = [carry[i, c] for i in range(11)]
                flux_x.append(face_flux(behind, here))
                for i in range(11):
                    carry[i, c] = here[i]
            finish(x, [[carry[11 + f, c] for f in range(NF)] for c in range(2)], flux_x)

            if half == 0:

                @pl.when(r == 0)
                def _():
                    for c in range(2):
                        for f in range(NF):
                            xsum[0, f, c] = xsum[0, f, c] + flux_x[c][f]

            raw = [raw_of(cells[c], prims[c], 3) for c in range(2)]
            here = [side_of_raw(raw[c], 3) for c in range(2)]
            turned = [[roll_to(v, 16) for v in raw[c]] for c in range(2)]
            left = side_of_raw(turned[0], 3)
            left = [
                [jnp.where(low16, zg[i], left[i]) for i in range(11)],
                side_of_raw([jnp.where(low16, a, b) for a, b in zip(*turned)], 3),
            ]
            lower = [face_flux(left[c], here[c]) for c in range(2)]
            last = face_flux(here[1], zg)
            change = [[], []]
            for f in range(NF):
                back = [roll_to(lower[c][f], -16) for c in range(2)]
                change[0].append(jnp.where(high16, back[0], back[1]) - lower[0][f])
                change[1].append(jnp.where(high16, back[1], last[f]) - lower[1][f])
                edge = jnp.where(lane < 64, lower[0][f], last[f])
                zb[f] = edge if half == 0 else zb[f] + edge
            for c in range(2):
                yg = [yghost[i, c, r] for i in range(11)]
                raw = raw_of(cells[c], prims[c], 2)
                here = side_of_raw(raw, 2)
                left = side_of_raw([roll_to(v, 1) for v in raw], 2)
                left = [jnp.where(first_y, yg[i], left[i]) for i in range(11)]
                lower_y = face_flux(left, here)
                last_flux = face_flux(here, yg)
                for f in range(NF):
                    upper_y = jnp.where(last_y, last_flux[f], roll_to(lower_y[f], -1))
                    change[c][f] = change[c][f] + (upper_y - lower_y[f])
                    edge = jnp.where(place_y < 8, lower_y[f], last_flux[f])
                    yb[c][f] = edge if half == 0 else yb[c][f] + edge
            for c in range(2):
                for f in range(NF):
                    carry[11 + f, c] = cells[c][f] - step * (change[c][f] - flux_x[c][f])
        for f in range(NF):
            zsum[f, r] = zsum[f, r] + zb[f]
            for c in range(2):
                ysum[f, r, c] = ysum[f, r, c] + yb[c][f]
        return unused

    lax.fori_loop(0, CW, pair, 0)
    flux_x = [face_flux([carry[i, c] for i in range(11)], [xghost[1, i, c] for i in range(11)]) for c in range(2)]
    finish(FW, [[carry[11 + f, c] for f in range(NF)] for c in range(2)], flux_x)
    for c in range(2):
        for f in range(NF):
            xsum[1, f, c] = xsum[1, f, c] + flux_x[c][f]

    odd = (lane & 1) == 1
    odd_z = (lane & 16) == 16
    outer = (place_y == 0) | (place_y == 15)
    middle_y = (place_y >= 2) & (place_y < 10)
    z_ends = (lane < 16) | (lane >= 112)

    def shifted(values, shift):
        return [roll_to(v, shift) for v in values]

    def added(left, right):
        return [a + b for a, b in zip(left, right)]

    def dense(values):
        values = added(values, shifted(values, -1))
        return [jnp.where(odd, b, a) for a, b in zip(values, shifted(values, -7))]

    ends = [xsum[side, f, c] for f in range(NF) for side in range(2) for c in range(2)]
    ends = dense(added(ends, shifted(ends, -16)))
    for i, v in enumerate(ends):
        xpool[i] = v
    for f in range(NF):
        sums = [[last_ref[f, 2 * r + 1, c] + last_ref[f, 2 * r + 2, c] for r in range(CW)] for c in range(2)]
        turned = [shifted(sums[0], -1), shifted(sums[1], 1)]
        average = [jnp.where(odd, sums[1][r] + turned[1][r], sums[0][r] + turned[0][r]) for r in range(CW)]
        average = added(average, shifted(average, -16))
        v = [[ysum[f, r, c] for r in range(CW)] for c in range(2)]
        turned = [shifted(v[1], 1), shifted(v[1], -1)]
        fluxes = [
            jnp.where(outer, v[0][r], jnp.where(place_y < 8, turned[0][r], turned[1][r])) for r in range(CW)
        ]
        v = [zsum[f, r] for r in range(CW)]
        v = added(v, shifted(v, -1))
        v = [jnp.where(odd, b, a) for a, b in zip(shifted(v, 2), shifted(v, -5))]
        fluxes = [jnp.where(middle_y, jnp.where(z_ends, v[r], 0.0), fluxes[r]) for r in range(CW)]
        fluxes = added(fluxes, shifted(fluxes, 16))
        for low, part in (
            (50, [roll_to(xpool[f * 4 + r // 4], 50 - r % 4 * 32) for r in range(CW)]),
            (82, [roll_to(xpool[f * 4 + 2 + r // 4], 82 - r % 4 * 32) for r in range(CW)]),
        ):
            mask = (lane >= low) & (lane < low + 8)
            fluxes = [jnp.where(mask, part[r], fluxes[r]) for r in range(CW)]
        for r in range(CW):
            row = jnp.where(odd_z, fluxes[r] * 0.0625, average[r] * 0.125)
            packed[pl.ds(f * 8 + r, NP, stride=NF * 8), :] = row

    lower_x = (lane >= 50) & (lane < 58)
    upper_x = (lane >= 82) & (lane < 90)
    others = ~(lower_x | upper_x)
    for p in range(NP):
        own, before, after = slots(p)
        for f in range(NF):
            tile = packed[pl.ds(p * 40 + f * 8, 8), :]
            for slot, mask in ((own, others), (before, lower_x), (after, upper_x)):
                target = out_ref.at[pl.ds(pl.multiple_of(slot * 40 + f * 8, 8), 8), :]
                pltpu.store(target, tile, mask=mask)


def coarse_kernel(coarse_ref, low_ref, high_ref, next_ref, yedge_ref, zedge_ref, xedge_ref, carry):
    step = 0.5 * time_step
    upper_edge = (lax.broadcasted_iota(jnp.int32, (ZC, LN), 1) & (CW - 1)) == CW - 1
    values = [low_ref[pl.ds(f * ZC, ZC), :] for f in range(NF)]
    for i, v in enumerate(side_of_face(values, primitives(values), 1)):
        carry[i] = v

    def store(ref, f, x, value):
        ref[pl.ds(pl.multiple_of(f * 256 + x * ZC, ZC), ZC), :] = value

    def plane(x, unused):
        cells = [coarse_ref[pl.ds(pl.multiple_of(f * 256 + x * ZC, ZC), ZC), :] for f in range(NF)]
        prims = primitives(cells)
        here = side_of_face(cells, prims, 1)
        flux_x = face_flux([carry[i] for i in range(11)], here)

        @pl.when(x > 0)
        def _():
            for f in range(NF):
                store(next_ref, f, x - 1, carry[11 + f] - step * flux_x[f])

        @pl.when(x == 0)
        def _():
            for f in range(NF):
                xedge_ref[pl.ds(f * 64, ZC), :] = 0.5 * flux_x[f]

        for i in range(11):
            carry[i] = here[i]
        here = side_of_face(cells, prims, 3)
        left = [pltpu.roll(v, 1, 0) for v in here]
        lower_z = face_flux(left, here)
        here = side_of_face(cells, prims, 2)
        left = [pltpu.roll(v, 1, 1) for v in here]
        lower_y = face_flux(left, here)
        for f in range(NF):
            upper_y = pltpu.roll(lower_y[f], LN - 1, 1)
            change = (pltpu.roll(lower_z[f], ZC - 1, 0) - lower_z[f]) + (upper_y - lower_y[f])
            carry[11 + f] = cells[f] - step * (change - flux_x[f])
            store(yedge_ref, f, x, 0.5 * jnp.where(upper_edge, upper_y, lower_y[f]))
            for k in range(ZC // CW):
                zedge_ref[pl.ds((f * 4 + k) * 8 + x, 1), :] = 0.5 * lower_z[f][k * CW : k * CW + 1, :]
        return unused

    lax.fori_loop(0, CW, plane, 0)
    values = [high_ref[pl.ds(f * ZC, ZC), :] for f in range(NF)]
    flux_x = face_flux([carry[i] for i in range(11)], side_of_face(values, primitives(values), 1))
    for f in range(NF):
        store(next_ref, f, CW - 1, carry[11 + f] - step * flux_x[f])
        xedge_ref[pl.ds(f * 64 + ZC, ZC), :] = 0.5 * flux_x[f]


def apply_kernel(count, slot_ref, result_ref, base_ref, yedge_ref, zedge_ref, xedge_ref, out_hbm, zsum, out_ref, semaphores):
    per_device = ZC // CW * YB
    lane = lanes()
    sub = lax.broadcasted_iota(jnp.int32, (8, LN), 0)
    out_ref[...] = base_ref[...]
    zsum[...] = jnp.zeros(zsum.shape, jnp.float32)

    def place_of(row):
        return split_box(slot_ref[4 * count + row], per_device)[1]

    def weight(row, face):
        return slot_ref[(4 + NP) * count + row * 6 + face].astype(jnp.float32) * (time_step if face % 2 else -time_step)

    def one(source, unused):
        before_row, own, after_row = (slot_ref[k * count + source] for k in range(3))
        row0 = pl.multiple_of(source * 40, 8)

        def tile(f):
            return result_ref[pl.ds(row0 + f * 8, 8), :]

        def unmix(y0, first):
            place = lane - y0
            return (first + (place & 3) * 2 + ((place >> 2) & 1)) & (LN - 1)

        for upper in range(2):
            row = before_row if upper else after_row

            @pl.when(row >= 0)
            def _():
                z0, y0 = anchors(place_of(row))
                scale = weight(row, upper)
                inside = (lane >= y0) & (lane < y0 + CW)
                index = unmix(y0, 82 if upper else 50)
                plane = 0 if upper else CW - 1
                new, places = [], []
                for f in range(NF):
                    place = pl.ds(pl.multiple_of(f * 256 + plane * ZC + z0, 8), 8)
                    edge = xedge_ref[pl.ds(pl.multiple_of(f * 64 + (1 - upper) * ZC + z0, 8), 8), :]
                    old = out_ref[place, :]
                    places.append(place)
                    new.append(jnp.where(inside, old + scale * (take_lanes(tile(f), index) - edge), old))
                for place, value in zip(places, new):
                    out_ref[place, :] = value

        @pl.when(own >= 0)
        def _():
            z0, y0 = anchors(place_of(own))
            inside = (lane >= y0) & (lane < y0 + CW)
            block = z0 >> 3
            for upper, target, face in ((0, (block - 1) & 3, block), (1, (block + 1) & 3, (block + 1) & 3)):
                scale = jnp.where(inside, weight(own, 2 + upper), 0.0)
                index = unmix(y0, 114 if upper else 18)
                for f in range(NF):
                    edge = zedge_ref[pl.ds(pl.multiple_of(f * 32 + face * 8, 8), 8), :]
                    part = jnp.where(inside, take_lanes(tile(f), index) - edge, 0.0)
                    zsum[f, upper, target] = zsum[f, upper, target] + scale * part
            before = lane == ((y0 - 1) & (LN - 1))
            after = lane == ((y0 + CW) & (LN - 1))
            part = (sub & 3) * 32 + (sub >> 2)
            faces = jnp.where(before, part + 16, (sub & 3) * 32 + 31 - (sub >> 2))
            index = jnp.where(inside, part + 2 * ((lane - y0) & 7), faces)
            scale = jnp.where(before, weight(own, 4), jnp.where(after, weight(own, 5), 0.0))
            for f in range(NF):
                new, places = [], []
                for x in range(CW):
                    place = pl.ds(pl.multiple_of(f * 256 + x * ZC + z0, 8), 8)
                    line = jnp.broadcast_to(result_ref[pl.ds(row0 + f * 8 + x, 1), :], (8, LN))
                    got = take_lanes(line, index)
                    places.append(place)
                    new.append(jnp.where(inside, got, out_ref[place, :] + scale * (got - yedge_ref[place, :])))
                for place, value in zip(places, new):
                    out_ref[place, :] = value

        return unused

    lax.fori_loop(0, count, one, 0)
    copies = []
    for f in range(NF):
        for x in range(CW):
            for block in range(ZC // CW):
                for upper in range(2):
                    row = pl.ds(f * 256 + x * ZC + block * 8 + (0 if upper else 7), 1)
                    out_ref[row, :] = out_ref[row, :] + zsum[f, upper, block, x : x + 1]
        field = pl.ds(f * 256, 256)
        copies.append(pltpu.make_async_copy(out_ref.at[field, :], out_hbm.at[field, :], semaphores.at[f]))
        copies[f].start()
    for copy in copies:
        copy.wait()


def local(coarse_state, fine_state, patch_box, face_flags):
    count = lax.axis_size("box")
    assert coarse_state.shape == (NF, CW, ZC, LN) and fine_state.shape == (NP, NF, FW, FW * FW)
    coarse = coarse_state.reshape(NF * CW * ZC, LN)
    f32 = jnp.float32
    vmem = pl.BlockSpec(memory_space=pltpu.VMEM)
    smem = pl.BlockSpec(memory_space=pltpu.SMEM)
    hbm = pl.BlockSpec(memory_space=pltpu.HBM)
    anywhere = pl.BlockSpec(memory_space=pl.ANY)

    def shaped(*shape):
        return jax.ShapeDtypeStruct(shape, f32)

    def call(kernel, out_shape, in_specs, out_specs, flops, size, scratch=(), limit=16):
        return pl.pallas_call(
            kernel,
            out_shape=out_shape,
            in_specs=in_specs,
            out_specs=out_specs,
            scratch_shapes=scratch,
            cost_estimate=pl.CostEstimate(flops=flops, bytes_accessed=size, transcendentals=0),
            compiler_params=pltpu.CompilerParams(vmem_limit_bytes=limit * 1024 * 1024),
        )

    packets, first, last, slots, _ = call(
        functools.partial(pack_kernel, count),
        (
            shaped(count * 16, LN),
            shaped(NF, ZC, LN),
            shaped(NF, ZC, LN),
            jax.ShapeDtypeStruct((4 * count,), jnp.int32),
            jax.ShapeDtypeStruct((count + 2,), jnp.int32),
        ),
        [hbm, hbm],
        (vmem, vmem, vmem, smem, smem),
        1000000,
        1000000,
        (
            pltpu.SMEM((count * NP,), jnp.int32),
            pltpu.VMEM((NF, ZC, CW, LN), f32),
            pltpu.SemaphoreType.DMA((3 + CW,)),
        ),
        limit=63,
    )(patch_box, coarse_state)
    arrived = lax.all_to_all(packets.reshape(count, 16, LN), "box", split_axis=0, concat_axis=0, tiled=True)
    ring = [(i, (i + 1) % count) for i in range(count)]
    low = lax.ppermute(last, "box", ring)
    high = lax.ppermute(first, "box", [(b, a) for a, b in ring])
    middle, cells = call(
        interior_kernel,
        (
            shaped(NF, FW + 1, 2, NP, LN),
            shaped(9, FW, 2, NP, LN),
        ),
        [hbm],
        (vmem, vmem),
        10000000,
        4000000,
        (
            pltpu.VMEM((NF, FW, 2, NP, LN), f32),
            pltpu.VMEM((16, 2, 8, LN), f32),
            pltpu.SemaphoreType.DMA((2 * NP,)),
        ),
    )(fine_state)
    outbox, state = call(
        functools.partial(fine_kernel, count),
        (shaped(count * 40, LN), shaped(NF, FW + 1, 2, NP, LN)),
        [smem] + [vmem] * 3,
        (vmem, vmem),
        20000000,
        4000000,
        (
            pltpu.VMEM((NP * 16, LN), f32),
            pltpu.VMEM((16, NP, LN), f32),
            pltpu.VMEM((11, CW, 8, LN), f32),
            pltpu.VMEM((11, 2, CW, 8, LN), f32),
            pltpu.VMEM((2, 11, 2, 8, LN), f32),
            pltpu.VMEM((NF, FW, 2, 8, LN), f32),
            pltpu.VMEM((16, 2, 8, LN), f32),
            pltpu.VMEM((NF, CW, 8, LN), f32),
            pltpu.VMEM((NF, CW, 2, 8, LN), f32),
            pltpu.VMEM((2, NF, 2, 8, LN), f32),
            pltpu.VMEM((4 * NF, NP, LN), f32),
            pltpu.VMEM((NP * 40, LN), f32),
        ),
    )(patch_box, arrived.reshape(count * 16, LN), middle, cells)
    returned = lax.all_to_all(outbox.reshape(count, 40, LN), "box", split_axis=0, concat_axis=0, tiled=True)
    fine_next = call(
        collect_kernel,
        shaped(*fine_state.shape),
        [vmem],
        anywhere,
        1000000,
        4000000,
        (pltpu.SemaphoreType.DMA((2 * NP,)),),
    )(state)
    tables = jnp.concatenate([slots, patch_box, face_flags.reshape(-1)])
    size = NF * CW * ZC
    base, yedge, zedge, xedge = call(
        coarse_kernel,
        (shaped(size, LN), shaped(size, LN), shaped(NF * 32, LN), shaped(NF * 2 * ZC, LN)),
        [vmem] * 3,
        (vmem,) * 4,
        10000000,
        4000000,
        (pltpu.VMEM((16, ZC, LN), f32),),
    )(coarse, low.reshape(NF * ZC, LN), high.reshape(NF * ZC, LN))
    coarse_next = call(
        functools.partial(apply_kernel, count),
        shaped(size, LN),
        [smem] + [vmem] * 5,
        anywhere,
        2000000,
        4000000,
        (
            pltpu.VMEM((NF, 2, ZC // CW, CW, LN), f32),
            pltpu.VMEM((size, LN), f32),
            pltpu.SemaphoreType.DMA((NF,)),
        ),
    )(tables, returned.reshape(count * 40, LN), base, yedge, zedge, xedge)
    return coarse_next.reshape(coarse_state.shape), fine_next


def solution(mesh):
    placed = (
        P(None, "box", "grp", None),
        P(("grp", "box"), None, None, None),
        P("grp"),
        P("grp", None),
    )
    return jax.shard_map(
        local,
        mesh=mesh,
        in_specs=placed,
        out_specs=(P(None, "box", "grp", None), P(("grp", "box"), None, None, None)),
        check_vma=False,
    )
```

```python
import functools

import jax
import jax.numpy as jnp
from jax import lax
from jax.experimental import pallas as pl
from jax.experimental.pallas import tpu as pltpu
from jax.sharding import PartitionSpec as P


gas_gamma = 1.4
time_step = 0.05

NF = 5
CW = 8
FW = 16
NP = 8
LN = 128
ZC = 32
YB = LN // CW
SIDE = ((0, 0), (0, 33), (0, 66), (1, 0), (1, 33))
XUNIT = tuple((0, 99 + 8 * u) if u < 3 else (1, 66 + 8 * (u - 3)) for u in range(10))


def take_lanes(values, index):
    return jnp.take_along_axis(values, index, axis=1, mode="promise_in_bounds")


def lanes():
    return lax.broadcasted_iota(jnp.int32, (8, LN), 1)


def roll_to(values, shift):
    if isinstance(shift, int):
        shift = shift % LN
        return values if shift == 0 else pltpu.roll(values, shift, 1)
    return pltpu.roll(values, shift & (LN - 1), 1)


def primitives(state):
    inverse = 1.0 / state[0]
    speeds = [None] + [state[m] * inverse for m in (1, 2, 3)]
    squares = state[1] * speeds[1] + state[2] * speeds[2] + state[3] * speeds[3]
    pressure = (gas_gamma - 1.0) * (state[4] - 0.5 * squares)
    sound = jnp.sqrt(gas_gamma * pressure * inverse)
    return speeds, pressure, sound, state[4] + pressure


def side_of_face(state, prims, m):
    speeds, pressure, sound, total = prims
    v = speeds[m]
    flux = [state[m], state[1] * v, state[2] * v, state[3] * v, total * v]
    flux[m] = flux[m] + pressure
    return list(state) + flux + [jnp.abs(v) + sound]


def face_flux(left, right):
    fastest = jnp.maximum(left[10], right[10])
    return [left[5 + f] + right[5 + f] - fastest * (right[f] - left[f]) for f in range(NF)]


def split_box(number, per_device):
    if per_device & (per_device - 1) == 0:
        return number >> (per_device.bit_length() - 1), number & (per_device - 1)
    owner = lax.div(number, jnp.int32(per_device))
    return owner, number - owner * per_device


def fill_slots(box_ref, slot_ref, own_ref, me, count, per_device):
    def clear(i, unused):
        for k in range(3):
            slot_ref[k * count + i] = jnp.int32(-1)
        return unused

    lax.fori_loop(0, count, clear, 0)
    power = count & (count - 1) == 0
    shifted = me - 1

    def one(source, unused):
        for j in range(NP):
            row = source * NP + j
            owner, _ = split_box(box_ref[row], per_device)
            k = owner - shifted
            if power:
                k = k & (count - 1)
            else:
                k = jnp.where(k < 0, k + count, k)
                k = jnp.where(k >= count, k - count, k)
            slot_ref[jnp.minimum(k, 3) * count + source] = row
        return unused

    lax.fori_loop(0, count, one, 0)

    def listed(source, used):
        row = slot_ref[count + source]
        own_ref[1 + used] = row
        return used + jnp.where(row >= 0, 1, 0)

    own_ref[0] = lax.fori_loop(0, count, listed, 0)


def place_of(box_ref, row, per_device):
    return split_box(box_ref[jnp.maximum(row, 0)], per_device)[1]


def anchors(place):
    return (place >> 4) * CW, (place & (YB - 1)) * CW


def pack_kernel(count, box_hbm, coarse_hbm, out_ref, first_ref, last_ref, slot_ref, own_ref, box_ref, turned, beside, semaphores):
    me = lax.axis_index("box")
    per_device = ZC // CW * YB
    lane = lanes()
    numbers = pltpu.make_async_copy(box_hbm, box_ref, semaphores.at[0])
    numbers.start()
    copies = [
        pltpu.make_async_copy(coarse_hbm.at[:, 0], first_ref, semaphores.at[1]),
        pltpu.make_async_copy(coarse_hbm.at[:, CW - 1], last_ref, semaphores.at[2]),
    ]
    for x in range(CW):
        copies.append(pltpu.make_async_copy(coarse_hbm.at[:, x], turned.at[:, :, x, :], semaphores.at[3 + x]))
    for copy in copies:
        copy.start()
    numbers.wait()
    fill_slots(box_ref, slot_ref, own_ref, me, count, per_device)
    for copy in copies[:2]:
        copy.wait()

    def edges(block, unused):
        for i in range(4):
            source = block * 4 + i
            before, after = slot_ref[source], slot_ref[2 * count + source]
            ends = [anchors(place_of(box_ref, row, per_device)) for row in (after, before)]
            tiles = [jnp.zeros((8, LN), jnp.float32)] * 2
            for u in range(10):
                f, upper = u // 2, u % 2
                z0, y0 = ends[upper]
                values = (first_ref if upper else last_ref)[f, pl.ds(pl.multiple_of(z0, 8), 8), :]
                tile, base = XUNIT[u]
                moved = roll_to(values, base - y0)
                tiles[tile] = jnp.where(lane >= base, moved, tiles[tile])
            row0 = pl.multiple_of(source * 16, 16)
            out_ref[pl.ds(row0, 8), :] = tiles[0]
            out_ref[pl.ds(row0 + 8, 8), :] = tiles[1]
        return unused

    lax.fori_loop(0, count // 4, edges, 0)
    for copy in copies[2:]:
        copy.wait()

    residue = lane & (CW - 1)

    def columns(block, unused):
        for f in range(NF):
            moved = [roll_to(turned[f, block * CW + k], k + 1) for k in range(CW)]
            low = high = moved[0]
            for k in range(1, CW):
                low = jnp.where(residue == k, moved[k], low)
                high = jnp.where(residue == (k + 1) % CW, moved[k], high)
            beside[0, f, block] = low
            beside[1, f, block] = high
        return unused

    lax.fori_loop(0, ZC // CW, columns, 0)

    def faces(pair, unused):
        for i in range(2):
            own = own_ref[1 + jnp.minimum(2 * pair + i, used - 1)]
            row0 = pl.multiple_of(own // NP * 16, 16)
            z0, y0 = anchors(place_of(box_ref, own, per_device))
            block = z0 >> 3
            below = (z0 - 1) & (ZC - 1)
            above = (z0 + CW) & (ZC - 1)
            inside = (lane >= y0) & (lane < y0 + CW)
            sides = [None, None]
            for f in range(NF):
                tile, base = SIDE[f]
                low = roll_to(turned[f, below], base - y0)
                high = roll_to(turned[f, above], base + 8 - y0)
                both = roll_to(jnp.where(inside, beside[0, f, block], beside[1, f, block]), base + 16 - y0)
                piece = jnp.where(lane < base + 8, low, jnp.where(lane < base + 16, high, both))
                sides[tile] = piece if base == 0 else jnp.where(lane >= base, piece, sides[tile])
            pltpu.store(out_ref.at[pl.ds(row0, 8), :], sides[0], mask=lane < 99)
            pltpu.store(out_ref.at[pl.ds(row0 + 8, 8), :], sides[1], mask=lane < 66)
        return unused

    used = own_ref[0]
    lax.fori_loop(0, (used + 1) // 2, faces, 0)


def interior_kernel(fine_ref, middle_ref, cells_ref, given, carry, semaphores):
    step = 0.5 * time_step
    lane = lanes()
    low16 = lane < 16
    high16 = lane < 112
    first_y = (lane & 15) == 0
    copies = [
        pltpu.make_async_copy(fine_ref.at[p, :, :, pl.ds(c * LN, LN)], given.at[:, :, c, p, :], semaphores.at[p * 2 + c])
        for p in range(NP)
        for c in range(2)
    ]
    for copy in copies:
        copy.start()
    for copy in copies:
        copy.wait()
    for c in range(2):
        cells = [given[f, 0, c] for f in range(NF)]
        for i, v in enumerate(side_of_face(cells, primitives(cells), 1)):
            carry[i, c] = v
        for f in range(NF):
            carry[11 + f, c] = jnp.zeros((8, LN), jnp.float32)

    def pair(r, unused):
        for half in range(2):
            x = 2 * r + half
            cells = [[given[f, x, c] for f in range(NF)] for c in range(2)]
            prims = [primitives(u) for u in cells]
            for c in range(2):
                speeds, pressure, sound, _ = prims[c]
                for i, v in enumerate(cells[c] + [speeds[2], speeds[3], pressure, sound]):
                    cells_ref[i, x, c] = v
            flux_x = []
            for c in range(2):
                here = side_of_face(cells[c], prims[c], 1)
                flux = face_flux([carry[i, c] for i in range(11)], here)
                if half == 0:
                    flux = [jnp.where(r == 0, 0.0, v) for v in flux]
                flux_x.append(flux)
                for i in range(11):
                    carry[i, c] = here[i]
                for f in range(NF):
                    middle_ref[f, x, c] = carry[11 + f, c] - step * flux[f]
            here = [side_of_face(cells[c], prims[c], 3) for c in range(2)]
            turned = [[roll_to(v, 16) for v in here[c]] for c in range(2)]
            left = [turned[0], [jnp.where(low16, turned[0][i], turned[1][i]) for i in range(11)]]
            lower = [face_flux(left[c], here[c]) for c in range(2)]
            lower[0] = [jnp.where(low16, 0.0, v) for v in lower[0]]
            change = [[], []]
            for f in range(NF):
                back = [roll_to(lower[c][f], -16) for c in range(2)]
                change[0].append(jnp.where(high16, back[0], back[1]) - lower[0][f])
                change[1].append(jnp.where(high16, back[1], back[0]) - lower[1][f])
            for c in range(2):
                here = side_of_face(cells[c], prims[c], 2)
                lower_y = face_flux([roll_to(v, 1) for v in here], here)
                lower_y = [jnp.where(first_y, 0.0, v) for v in lower_y]
                for f in range(NF):
                    total = change[c][f] + (roll_to(lower_y[f], -1) - lower_y[f]) - flux_x[c][f]
                    carry[11 + f, c] = cells[c][f] - step * total
        return unused

    lax.fori_loop(0, CW, pair, 0)
    for c in range(2):
        for f in range(NF):
            middle_ref[f, FW, c] = carry[11 + f, c]


def collect_kernel(state_ref, out_ref, semaphores):
    copies = [
        pltpu.make_async_copy(
            state_ref.at[:, pl.ds(1, FW), c, p, :], out_ref.at[p, :, :, pl.ds(c * LN, LN)], semaphores.at[p * 2 + c]
        )
        for p in range(NP)
        for c in range(2)
    ]
    for copy in copies:
        copy.start()
    for copy in copies:
        copy.wait()


def fine_kernel(
    count,
    box_ref,
    ghost_ref,
    middle_ref,
    cells_ref,
    out_ref,
    last_ref,
    message,
    rows,
    zghost,
    yghost,
    xghost,
    middle,
    carry,
    zsum,
    ysum,
    xsum,
    xpool,
    packed,
):
    per_device = ZC // CW * YB
    me = lax.axis_index("box")
    lane = lanes()
    place_y = lane & 15
    first_y = place_y == 0
    last_y = place_y == 15
    low16 = lane < 16
    high16 = lane < 112

    def slots(p):
        owner, _ = split_box(box_ref[me * NP + p], per_device)
        return owner, jnp.where(owner == 0, count - 1, owner - 1), jnp.where(owner == count - 1, 0, owner + 1)

    for p in range(NP):
        own, before, after = slots(p)
        for tile in range(2):
            start = 99 if tile == 0 else 66
            lower_parity = 0 if tile == 0 else 1
            is_x = lane >= start
            is_lower = (((lane - start) >> 3) & 1) == lower_parity
            pieces = [ghost_ref[pl.ds(pl.multiple_of(s * 16 + tile * 8, 8), 8), :] for s in (own, before, after)]
            message[pl.ds(p * 16 + tile * 8, 8), :] = jnp.where(
                is_x, jnp.where(is_lower, pieces[1], pieces[2]), pieces[0]
            )
    for i in range(16):
        rows[i] = message[pl.ds(i, NP, stride=16), :]
    pair_y = place_y >> 1
    for f in range(NF):
        tile, base = SIDE[f]
        index = jnp.where(lane < 64, base, base + 8) + pair_y
        for r in range(CW):
            zghost[f, r] = take_lanes(rows[tile * 8 + r], index)
        for c in range(2):
            index = jnp.where(place_y < 8, base + 16, base + 25) + (lane >> 5) + 4 * c
            for r in range(CW):
                yghost[f, c, r] = take_lanes(rows[tile * 8 + r], index)
    dense = {}
    for c in range(2):
        for f in range(NF):
            (tile_low, low), (tile_high, high) = XUNIT[2 * f], XUNIT[2 * f + 1]
            for k in range(4):
                moved = roll_to(rows[tile_low * 8 + 4 * c + k], 32 * k - low)
                if (tile_high, high) != (tile_low, low + 8):
                    other = roll_to(rows[tile_high * 8 + 4 * c + k], 32 * k + 8 - high)
                    moved = jnp.where((lane & 15) < 8, moved, other)
                dense[c, f] = moved if k == 0 else jnp.where(lane >= 32 * k, moved, dense[c, f])
    for upper in range(2):
        unfold = (lane & 96) + pair_y + 8 * upper
        for c in range(2):
            for f in range(NF):
                xghost[upper, f, c] = take_lanes(dense[c, f], unfold)
    for half in range(2):
        some = pl.ds(4 * half, 4)
        values = [zghost[f, some] for f in range(NF)]
        for i, v in enumerate(side_of_face(values, primitives(values), 3)[NF:]):
            zghost[NF + i, some] = v
        for c in range(2):
            values = [yghost[f, c, some] for f in range(NF)]
            for i, v in enumerate(side_of_face(values, primitives(values), 2)[NF:]):
                yghost[NF + i, c, some] = v
    for upper in range(2):
        values = [xghost[upper, f] for f in range(NF)]
        for i, v in enumerate(side_of_face(values, primitives(values), 1)[NF:]):
            xghost[upper, NF + i] = v

    step = 0.5 * time_step

    sign_z = jnp.where(lane < 64, -1.0, 1.0)
    sign_y = jnp.where(place_y < 8, -1.0, 1.0)
    scale_z = [jnp.where(low16, step, 0.0), jnp.where(high16, 0.0, -step)]
    scale_y = jnp.where(first_y, step, jnp.where(last_y, -step, 0.0))

    def outer_flux(inside, ghost, sign):
        fastest = jnp.maximum(inside[10], ghost[10]) * sign
        return [inside[5 + f] + ghost[5 + f] - fastest * (ghost[f] - inside[f]) for f in range(NF)]

    def outer_faces(r, unused):
        both = pl.ds(2 * r, 2)
        cells = [[cells_ref[i, both, c] for i in range(9)] for c in range(2)]

        def inside(values, m):
            speeds = [None, None, values[5], values[6]]
            return side_of_face(values[:NF], (speeds, values[7], values[8], values[4] + values[7]), m)

        edge = [jnp.where(lane < 64, cells[0][i], cells[1][i]) for i in range(9)]
        flux_z = outer_flux(inside(edge, 3), [zghost[i, r] for i in range(11)], sign_z)
        for f in range(NF):
            zsum[f, r] = flux_z[f][0] + flux_z[f][1]
        for c in range(2):
            flux_y = outer_flux(inside(cells[c], 2), [yghost[i, c, r] for i in range(11)], sign_y)
            for f in range(NF):
                ysum[f, r, c] = flux_y[f][0] + flux_y[f][1]
                old = middle_ref[f, pl.ds(2 * r + 1, 2), c]
                middle[f, both, c] = old + flux_y[f] * scale_y + flux_z[f] * scale_z[c]
        return unused

    lax.fori_loop(0, CW, outer_faces, 0)
    for side, plane in ((0, 0), (1, FW - 1)):
        values = [cells_ref[f, plane] for f in range(NF)]
        sides = [[xghost[side, i] for i in range(11)], side_of_face(values, primitives(values), 1)]
        flux_x = face_flux(*(sides[::-1] if side else sides))
        for f in range(NF):
            xsum[side, f] = flux_x[f]
            middle[f, plane] = middle[f, plane] + (-step if side else step) * flux_x[f]

    def raw_of(cells, prims, m):
        return cells + [prims[0][m], prims[1], prims[2]]

    def side_of_raw(raw, m):
        speeds = [None] * 4
        speeds[m] = raw[5]
        return side_of_face(raw[:NF], (speeds, raw[6], raw[7], raw[4] + raw[6]), m)

    def finish(plane, part, flux):
        for c in range(2):
            for f in range(NF):
                last_ref[f, plane, c] = part[c][f] - step * flux[c][f]

    for c in range(2):
        for i in range(11):
            carry[i, c] = xghost[0, i, c]
        for f in range(NF):
            carry[11 + f, c] = jnp.zeros((8, LN), jnp.float32)

    def pair(r, unused):
        zg = [zghost[i, r] for i in range(11)]
        zb = [None] * NF
        yb = [[None] * NF for _ in range(2)]
        for half in range(2):
            x = 2 * r + half
            cells = [[middle[f, x, c] for f in range(NF)] for c in range(2)]
            prims = [primitives(u) for u in cells]
            flux_x = []
            for c in range(2):
                here = side_of_face(cells[c], prims[c], 1)
                behind = [carry[i, c] for i in range(11)]
                flux_x.append(face_flux(behind, here))
                for i in range(11):
                    carry[i, c] = here[i]
            finish(x, [[carry[11 + f, c] for f in range(NF)] for c in range(2)], flux_x)

            if half == 0:

                @pl.when(r == 0)
                def _():
                    for c in range(2):
                        for f in range(NF):
                            xsum[0, f, c] = xsum[0, f, c] + flux_x[c][f]

            raw = [raw_of(cells[c], prims[c], 3) for c in range(2)]
            here = [side_of_raw(raw[c], 3) for c in range(2)]
            turned = [[roll_to(v, 16) for v in raw[c]] for c in range(2)]
            left = side_of_raw(turned[0], 3)
            left = [
                [jnp.where(low16, zg[i], left[i]) for i in range(11)],
                side_of_raw([jnp.where(low16, a, b) for a, b in zip(*turned)], 3),
            ]
            lower = [face_flux(left[c], here[c]) for c in range(2)]
            last = face_flux(here[1], zg)
            change = [[], []]
            for f in range(NF):
                back = [roll_to(lower[c][f], -16) for c in range(2)]
                change[0].append(jnp.where(high16, back[0], back[1]) - lower[0][f])
                change[1].append(jnp.where(high16, back[1], last[f]) - lower[1][f])
                edge = jnp.where(lane < 64, lower[0][f], last[f])
                zb[f] = edge if half == 0 else zb[f] + edge
            for c in range(2):
                yg = [yghost[i, c, r] for i in range(11)]
                raw = raw_of(cells[c], prims[c], 2)
                here = side_of_raw(raw, 2)
                left = side_of_raw([roll_to(v, 1) for v in raw], 2)
                left = [jnp.where(first_y, yg[i], left[i]) for i in range(11)]
                lower_y = face_flux(left, here)
                last_flux = face_flux(here, yg)
                for f in range(NF):
                    upper_y = jnp.where(last_y, last_flux[f], roll_to(lower_y[f], -1))
                    change[c][f] = change[c][f] + (upper_y - lower_y[f])
                    edge = jnp.where(place_y < 8, lower_y[f], last_flux[f])
                    yb[c][f] = edge if half == 0 else yb[c][f] + edge
            for c in range(2):
                for f in range(NF):
                    carry[11 + f, c] = cells[c][f] - step * (change[c][f] - flux_x[c][f])
        for f in range(NF):
            zsum[f, r] = zsum[f, r] + zb[f]
            for c in range(2):
                ysum[f, r, c] = ysum[f, r, c] + yb[c][f]
        return unused

    lax.fori_loop(0, CW, pair, 0)
    flux_x = [face_flux([carry[i, c] for i in range(11)], [xghost[1, i, c] for i in range(11)]) for c in range(2)]
    finish(FW, [[carry[11 + f, c] for f in range(NF)] for c in range(2)], flux_x)
    for c in range(2):
        for f in range(NF):
            xsum[1, f, c] = xsum[1, f, c] + flux_x[c][f]

    odd = (lane & 1) == 1
    odd_z = (lane & 16) == 16
    outer = (place_y == 0) | (place_y == 15)
    middle_y = (place_y >= 2) & (place_y < 10)
    z_ends = (lane < 16) | (lane >= 112)

    def shifted(values, shift):
        return [roll_to(v, shift) for v in values]

    def added(left, right):
        return [a + b for a, b in zip(left, right)]

    def dense(values):
        values = added(values, shifted(values, -1))
        return [jnp.where(odd, b, a) for a, b in zip(values, shifted(values, -7))]

    ends = [xsum[side, f, c] for f in range(NF) for side in range(2) for c in range(2)]
    ends = dense(added(ends, shifted(ends, -16)))
    for i, v in enumerate(ends):
        xpool[i] = v
    for f in range(NF):
        sums = [[last_ref[f, 2 * r + 1, c] + last_ref[f, 2 * r + 2, c] for r in range(CW)] for c in range(2)]
        turned = [shifted(sums[0], -1), shifted(sums[1], 1)]
        average = [jnp.where(odd, sums[1][r] + turned[1][r], sums[0][r] + turned[0][r]) for r in range(CW)]
        average = added(average, shifted(average, -16))
        v = [[ysum[f, r, c] for r in range(CW)] for c in range(2)]
        turned = [shifted(v[1], 1), shifted(v[1], -1)]
        fluxes = [
            jnp.where(outer, v[0][r], jnp.where(place_y < 8, turned[0][r], turned[1][r])) for r in range(CW)
        ]
        v = [zsum[f, r] for r in range(CW)]
        v = added(v, shifted(v, -1))
        v = [jnp.where(odd, b, a) for a, b in zip(shifted(v, 2), shifted(v, -5))]
        fluxes = [jnp.where(middle_y, jnp.where(z_ends, v[r], 0.0), fluxes[r]) for r in range(CW)]
        fluxes = added(fluxes, shifted(fluxes, 16))
        for low, part in (
            (50, [roll_to(xpool[f * 4 + r // 4], 50 - r % 4 * 32) for r in range(CW)]),
            (82, [roll_to(xpool[f * 4 + 2 + r // 4], 82 - r % 4 * 32) for r in range(CW)]),
        ):
            mask = (lane >= low) & (lane < low + 8)
            fluxes = [jnp.where(mask, part[r], fluxes[r]) for r in range(CW)]
        for r in range(CW):
            row = jnp.where(odd_z, fluxes[r] * 0.0625, average[r] * 0.125)
            packed[pl.ds(f * 8 + r, NP, stride=NF * 8), :] = row

    lower_x = (lane >= 50) & (lane < 58)
    upper_x = (lane >= 82) & (lane < 90)
    others = ~(lower_x | upper_x)
    for p in range(NP):
        own, before, after = slots(p)
        for f in range(NF):
            tile = packed[pl.ds(p * 40 + f * 8, 8), :]
            for slot, mask in ((own, others), (before, lower_x), (after, upper_x)):
                target = out_ref.at[pl.ds(pl.multiple_of(slot * 40 + f * 8, 8), 8), :]
                pltpu.store(target, tile, mask=mask)


def coarse_kernel(coarse_ref, low_ref, high_ref, next_ref, yedge_ref, zedge_ref, xedge_ref, carry):
    step = 0.5 * time_step
    upper_edge = (lax.broadcasted_iota(jnp.int32, (ZC, LN), 1) & (CW - 1)) == CW - 1
    values = [low_ref[pl.ds(f * ZC, ZC), :] for f in range(NF)]
    for i, v in enumerate(side_of_face(values, primitives(values), 1)):
        carry[i] = v

    def store(ref, f, x, value):
        ref[pl.ds(pl.multiple_of(f * 256 + x * ZC, ZC), ZC), :] = value

    def plane(x, unused):
        cells = [coarse_ref[pl.ds(pl.multiple_of(f * 256 + x * ZC, ZC), ZC), :] for f in range(NF)]
        prims = primitives(cells)
        here = side_of_face(cells, prims, 1)
        flux_x = face_flux([carry[i] for i in range(11)], here)

        @pl.when(x > 0)
        def _():
            for f in range(NF):
                store(next_ref, f, x - 1, carry[11 + f] - step * flux_x[f])

        @pl.when(x == 0)
        def _():
            for f in range(NF):
                xedge_ref[pl.ds(f * 64, ZC), :] = 0.5 * flux_x[f]

        for i in range(11):
            carry[i] = here[i]
        here = side_of_face(cells, prims, 3)
        left = [pltpu.roll(v, 1, 0) for v in here]
        lower_z = face_flux(left, here)
        here = side_of_face(cells, prims, 2)
        left = [pltpu.roll(v, 1, 1) for v in here]
        lower_y = face_flux(left, here)
        for f in range(NF):
            upper_y = pltpu.roll(lower_y[f], LN - 1, 1)
            change = (pltpu.roll(lower_z[f], ZC - 1, 0) - lower_z[f]) + (upper_y - lower_y[f])
            carry[11 + f] = cells[f] - step * (change - flux_x[f])
            store(yedge_ref, f, x, 0.5 * jnp.where(upper_edge, upper_y, lower_y[f]))
            for k in range(ZC // CW):
                zedge_ref[pl.ds((f * 4 + k) * 8 + x, 1), :] = 0.5 * lower_z[f][k * CW : k * CW + 1, :]
        return unused

    lax.fori_loop(0, CW, plane, 0)
    values = [high_ref[pl.ds(f * ZC, ZC), :] for f in range(NF)]
    flux_x = face_flux([carry[i] for i in range(11)], side_of_face(values, primitives(values), 1))
    for f in range(NF):
        store(next_ref, f, CW - 1, carry[11 + f] - step * flux_x[f])
        xedge_ref[pl.ds(f * 64 + ZC, ZC), :] = 0.5 * flux_x[f]


def apply_kernel(count, slot_ref, result_ref, base_ref, yedge_ref, zedge_ref, xedge_ref, out_hbm, zsum, out_ref, semaphores):
    per_device = ZC // CW * YB
    lane = lanes()
    sub = lax.broadcasted_iota(jnp.int32, (8, LN), 0)
    out_ref[...] = base_ref[...]
    zsum[...] = jnp.zeros(zsum.shape, jnp.float32)

    def place_of(row):
        return split_box(slot_ref[4 * count + row], per_device)[1]

    def weight(row, face):
        return slot_ref[(4 + NP) * count + row * 6 + face].astype(jnp.float32) * (time_step if face % 2 else -time_step)

    def one(source, unused):
        before_row, own, after_row = (slot_ref[k * count + source] for k in range(3))
        row0 = pl.multiple_of(source * 40, 8)

        def tile(f):
            return result_ref[pl.ds(row0 + f * 8, 8), :]

        def unmix(y0, first):
            place = lane - y0
            return (first + (place & 3) * 2 + ((place >> 2) & 1)) & (LN - 1)

        for upper in range(2):
            row = before_row if upper else after_row

            @pl.when(row >= 0)
            def _():
                z0, y0 = anchors(place_of(row))
                scale = weight(row, upper)
                inside = (lane >= y0) & (lane < y0 + CW)
                index = unmix(y0, 82 if upper else 50)
                plane = 0 if upper else CW - 1
                new, places = [], []
                for f in range(NF):
                    place = pl.ds(pl.multiple_of(f * 256 + plane * ZC + z0, 8), 8)
                    edge = xedge_ref[pl.ds(pl.multiple_of(f * 64 + (1 - upper) * ZC + z0, 8), 8), :]
                    old = out_ref[place, :]
                    places.append(place)
                    new.append(jnp.where(inside, old + scale * (take_lanes(tile(f), index) - edge), old))
                for place, value in zip(places, new):
                    out_ref[place, :] = value

        @pl.when(own >= 0)
        def _():
            z0, y0 = anchors(place_of(own))
            inside = (lane >= y0) & (lane < y0 + CW)
            block = z0 >> 3
            for upper, target, face in ((0, (block - 1) & 3, block), (1, (block + 1) & 3, (block + 1) & 3)):
                scale = jnp.where(inside, weight(own, 2 + upper), 0.0)
                index = unmix(y0, 114 if upper else 18)
                for f in range(NF):
                    edge = zedge_ref[pl.ds(pl.multiple_of(f * 32 + face * 8, 8), 8), :]
                    part = jnp.where(inside, take_lanes(tile(f), index) - edge, 0.0)
                    zsum[f, upper, target] = zsum[f, upper, target] + scale * part
            before = lane == ((y0 - 1) & (LN - 1))
            after = lane == ((y0 + CW) & (LN - 1))
            part = (sub & 3) * 32 + (sub >> 2)
            faces = jnp.where(before, part + 16, (sub & 3) * 32 + 31 - (sub >> 2))
            index = jnp.where(inside, part + 2 * ((lane - y0) & 7), faces)
            scale = jnp.where(before, weight(own, 4), jnp.where(after, weight(own, 5), 0.0))
            for f in range(NF):
                new, places = [], []
                for x in range(CW):
                    place = pl.ds(pl.multiple_of(f * 256 + x * ZC + z0, 8), 8)
                    line = jnp.broadcast_to(result_ref[pl.ds(row0 + f * 8 + x, 1), :], (8, LN))
                    got = take_lanes(line, index)
                    places.append(place)
                    new.append(jnp.where(inside, got, out_ref[place, :] + scale * (got - yedge_ref[place, :])))
                for place, value in zip(places, new):
                    out_ref[place, :] = value

        return unused

    lax.fori_loop(0, count, one, 0)
    copies = []
    for f in range(NF):
        for x in range(CW):
            for block in range(ZC // CW):
                for upper in range(2):
                    row = pl.ds(f * 256 + x * ZC + block * 8 + (0 if upper else 7), 1)
                    out_ref[row, :] = out_ref[row, :] + zsum[f, upper, block, x : x + 1]
        field = pl.ds(f * 256, 256)
        copies.append(pltpu.make_async_copy(out_ref.at[field, :], out_hbm.at[field, :], semaphores.at[f]))
        copies[f].start()
    for copy in copies:
        copy.wait()


def local(coarse_state, fine_state, patch_box, face_flags):
    count = lax.axis_size("box")
    assert coarse_state.shape == (NF, CW, ZC, LN) and fine_state.shape == (NP, NF, FW, FW * FW)
    coarse = coarse_state.reshape(NF * CW * ZC, LN)
    f32 = jnp.float32
    vmem = pl.BlockSpec(memory_space=pltpu.VMEM)
    smem = pl.BlockSpec(memory_space=pltpu.SMEM)
    hbm = pl.BlockSpec(memory_space=pltpu.HBM)
    anywhere = pl.BlockSpec(memory_space=pl.ANY)

    def shaped(*shape):
        return jax.ShapeDtypeStruct(shape, f32)

    def call(kernel, out_shape, in_specs, out_specs, flops, size, scratch=(), limit=16):
        return pl.pallas_call(
            kernel,
            out_shape=out_shape,
            in_specs=in_specs,
            out_specs=out_specs,
            scratch_shapes=scratch,
            cost_estimate=pl.CostEstimate(flops=flops, bytes_accessed=size, transcendentals=0),
            compiler_params=pltpu.CompilerParams(vmem_limit_bytes=limit * 1024 * 1024),
        )

    packets, first, last, slots, _ = call(
        functools.partial(pack_kernel, count),
        (
            shaped(count * 16, LN),
            shaped(NF, ZC, LN),
            shaped(NF, ZC, LN),
            jax.ShapeDtypeStruct((4 * count,), jnp.int32),
            jax.ShapeDtypeStruct((count + 2,), jnp.int32),
        ),
        [hbm, hbm],
        (vmem, vmem, vmem, smem, smem),
        1000000,
        1000000,
        (
            pltpu.SMEM((count * NP,), jnp.int32),
            pltpu.VMEM((NF, ZC, CW, LN), f32),
            pltpu.VMEM((2, NF, ZC // CW, CW, LN), f32),
            pltpu.SemaphoreType.DMA((3 + CW,)),
        ),
        limit=63,
    )(patch_box, coarse_state)
    arrived = lax.all_to_all(packets.reshape(count, 16, LN), "box", split_axis=0, concat_axis=0, tiled=True)
    ring = [(i, (i + 1) % count) for i in range(count)]
    low = lax.ppermute(last, "box", ring)
    high = lax.ppermute(first, "box", [(b, a) for a, b in ring])
    middle, cells = call(
        interior_kernel,
        (
            shaped(NF, FW + 1, 2, NP, LN),
            shaped(9, FW, 2, NP, LN),
        ),
        [hbm],
        (vmem, vmem),
        10000000,
        4000000,
        (
            pltpu.VMEM((NF, FW, 2, NP, LN), f32),
            pltpu.VMEM((16, 2, 8, LN), f32),
            pltpu.SemaphoreType.DMA((2 * NP,)),
        ),
    )(fine_state)
    outbox, state = call(
        functools.partial(fine_kernel, count),
        (shaped(count * 40, LN), shaped(NF, FW + 1, 2, NP, LN)),
        [smem] + [vmem] * 3,
        (vmem, vmem),
        20000000,
        4000000,
        (
            pltpu.VMEM((NP * 16, LN), f32),
            pltpu.VMEM((16, NP, LN), f32),
            pltpu.VMEM((11, CW, 8, LN), f32),
            pltpu.VMEM((11, 2, CW, 8, LN), f32),
            pltpu.VMEM((2, 11, 2, 8, LN), f32),
            pltpu.VMEM((NF, FW, 2, 8, LN), f32),
            pltpu.VMEM((16, 2, 8, LN), f32),
            pltpu.VMEM((NF, CW, 8, LN), f32),
            pltpu.VMEM((NF, CW, 2, 8, LN), f32),
            pltpu.VMEM((2, NF, 2, 8, LN), f32),
            pltpu.VMEM((4 * NF, NP, LN), f32),
            pltpu.VMEM((NP * 40, LN), f32),
        ),
    )(patch_box, arrived.reshape(count * 16, LN), middle, cells)
    returned = lax.all_to_all(outbox.reshape(count, 40, LN), "box", split_axis=0, concat_axis=0, tiled=True)
    fine_next = call(
        collect_kernel,
        shaped(*fine_state.shape),
        [vmem],
        anywhere,
        1000000,
        4000000,
        (pltpu.SemaphoreType.DMA((2 * NP,)),),
    )(state)
    tables = jnp.concatenate([slots, patch_box, face_flags.reshape(-1)])
    size = NF * CW * ZC
    base, yedge, zedge, xedge = call(
        coarse_kernel,
        (shaped(size, LN), shaped(size, LN), shaped(NF * 32, LN), shaped(NF * 2 * ZC, LN)),
        [vmem] * 3,
        (vmem,) * 4,
        10000000,
        4000000,
        (pltpu.VMEM((16, ZC, LN), f32),),
    )(coarse, low.reshape(NF * ZC, LN), high.reshape(NF * ZC, LN))
    coarse_next = call(
        functools.partial(apply_kernel, count),
        shaped(size, LN),
        [smem] + [vmem] * 5,
        anywhere,
        2000000,
        4000000,
        (
            pltpu.VMEM((NF, 2, ZC // CW, CW, LN), f32),
            pltpu.VMEM((size, LN), f32),
            pltpu.SemaphoreType.DMA((NF,)),
        ),
    )(tables, returned.reshape(count * 40, LN), base, yedge, zedge, xedge)
    return coarse_next.reshape(coarse_state.shape), fine_next


def solution(mesh):
    placed = (
        P(None, "box", "grp", None),
        P(("grp", "box"), None, None, None),
        P("grp"),
        P("grp", None),
    )
    return jax.shard_map(
        local,
        mesh=mesh,
        in_specs=placed,
        out_specs=(P(None, "box", "grp", None), P(("grp", "box"), None, None, None)),
        check_vma=False,
    )
```

```python
import functools

import jax
import jax.numpy as jnp
from jax import lax
from jax.experimental import pallas as pl
from jax.experimental.pallas import tpu as pltpu
from jax.sharding import PartitionSpec as P


gas_gamma = 1.4
time_step = 0.05

NF = 5
CW = 8
FW = 16
NP = 8
LN = 128
ZC = 32
YB = LN // CW
SIDE = ((0, 0), (0, 33), (0, 66), (1, 0), (1, 33))
XUNIT = tuple((0, 99 + 8 * u) if u < 3 else (1, 66 + 8 * (u - 3)) for u in range(10))


def take_lanes(values, index):
    return jnp.take_along_axis(values, index, axis=1, mode="promise_in_bounds")


def lanes():
    return lax.broadcasted_iota(jnp.int32, (8, LN), 1)


def roll_to(values, shift):
    if isinstance(shift, int):
        shift = shift % LN
        return values if shift == 0 else pltpu.roll(values, shift, 1)
    return pltpu.roll(values, shift & (LN - 1), 1)


def primitives(state):
    inverse = 1.0 / state[0]
    speeds = [None] + [state[m] * inverse for m in (1, 2, 3)]
    squares = state[1] * speeds[1] + state[2] * speeds[2] + state[3] * speeds[3]
    pressure = (gas_gamma - 1.0) * (state[4] - 0.5 * squares)
    sound = jnp.sqrt(gas_gamma * pressure * inverse)
    return speeds, pressure, sound, state[4] + pressure


def side_of_face(state, prims, m):
    speeds, pressure, sound, total = prims
    v = speeds[m]
    flux = [state[m], state[1] * v, state[2] * v, state[3] * v, total * v]
    flux[m] = flux[m] + pressure
    return list(state) + flux + [jnp.abs(v) + sound]


def face_flux(left, right):
    fastest = jnp.maximum(left[10], right[10])
    return [left[5 + f] + right[5 + f] - fastest * (right[f] - left[f]) for f in range(NF)]


def raw_of(cells, prims, m):
    return cells + [prims[0][m], prims[1], prims[2]]


def side_of_raw(raw, m):
    speeds = [None] * 4
    speeds[m] = raw[5]
    return side_of_face(raw[:NF], (speeds, raw[6], raw[7], raw[4] + raw[6]), m)


def split_box(number, per_device):
    if per_device & (per_device - 1) == 0:
        return number >> (per_device.bit_length() - 1), number & (per_device - 1)
    owner = lax.div(number, jnp.int32(per_device))
    return owner, number - owner * per_device


def fill_slots(box_ref, slot_ref, own_ref, me, count, per_device):
    def clear(i, unused):
        for k in range(3):
            slot_ref[k * count + i] = jnp.int32(-1)
        return unused

    lax.fori_loop(0, count, clear, 0)
    power = count & (count - 1) == 0
    shifted = me - 1

    def one(source, unused):
        for j in range(NP):
            row = source * NP + j
            owner, _ = split_box(box_ref[row], per_device)
            k = owner - shifted
            if power:
                k = k & (count - 1)
            else:
                k = jnp.where(k < 0, k + count, k)
                k = jnp.where(k >= count, k - count, k)
            slot_ref[jnp.minimum(k, 3) * count + source] = row
        return unused

    lax.fori_loop(0, count, one, 0)

    def listed(source, used):
        row = slot_ref[count + source]
        own_ref[1 + used] = row
        return used + jnp.where(row >= 0, 1, 0)

    own_ref[0] = lax.fori_loop(0, count, listed, 0)


def place_of(box_ref, row, per_device):
    return split_box(box_ref[jnp.maximum(row, 0)], per_device)[1]


def anchors(place):
    return (place >> 4) * CW, (place & (YB - 1)) * CW


def pack_kernel(count, box_hbm, coarse_hbm, out_ref, first_ref, last_ref, slot_ref, own_ref, box_ref, turned, beside, semaphores):
    me = lax.axis_index("box")
    per_device = ZC // CW * YB
    lane = lanes()
    numbers = pltpu.make_async_copy(box_hbm, box_ref, semaphores.at[0])
    numbers.start()
    copies = [
        pltpu.make_async_copy(coarse_hbm.at[:, 0], first_ref, semaphores.at[1]),
        pltpu.make_async_copy(coarse_hbm.at[:, CW - 1], last_ref, semaphores.at[2]),
    ]
    for x in range(CW):
        copies.append(pltpu.make_async_copy(coarse_hbm.at[:, x], turned.at[:, :, x, :], semaphores.at[3 + x]))
    for copy in copies:
        copy.start()
    numbers.wait()
    fill_slots(box_ref, slot_ref, own_ref, me, count, per_device)
    for copy in copies[:2]:
        copy.wait()

    def edges(block, unused):
        for i in range(4):
            source = block * 4 + i
            before, after = slot_ref[source], slot_ref[2 * count + source]
            ends = [anchors(place_of(box_ref, row, per_device)) for row in (after, before)]
            tiles = [jnp.zeros((8, LN), jnp.float32)] * 2
            for u in range(10):
                f, upper = u // 2, u % 2
                z0, y0 = ends[upper]
                values = (first_ref if upper else last_ref)[f, pl.ds(pl.multiple_of(z0, 8), 8), :]
                tile, base = XUNIT[u]
                moved = roll_to(values, base - y0)
                tiles[tile] = jnp.where(lane >= base, moved, tiles[tile])
            row0 = pl.multiple_of(source * 16, 16)
            out_ref[pl.ds(row0, 8), :] = tiles[0]
            out_ref[pl.ds(row0 + 8, 8), :] = tiles[1]
        return unused

    lax.fori_loop(0, count // 4, edges, 0)
    for copy in copies[2:]:
        copy.wait()

    residue = lane & (CW - 1)

    def columns(block, unused):
        for f in range(NF):
            moved = [roll_to(turned[f, block * CW + k], k + 1) for k in range(CW)]
            low = high = moved[0]
            for k in range(1, CW):
                low = jnp.where(residue == k, moved[k], low)
                high = jnp.where(residue == (k + 1) % CW, moved[k], high)
            beside[0, f, block] = low
            beside[1, f, block] = high
        return unused

    lax.fori_loop(0, ZC // CW, columns, 0)

    def faces(pair, unused):
        for i in range(2):
            own = own_ref[1 + jnp.minimum(2 * pair + i, used - 1)]
            row0 = pl.multiple_of(own // NP * 16, 16)
            z0, y0 = anchors(place_of(box_ref, own, per_device))
            block = z0 >> 3
            below = (z0 - 1) & (ZC - 1)
            above = (z0 + CW) & (ZC - 1)
            inside = (lane >= y0) & (lane < y0 + CW)
            sides = [None, None]
            for f in range(NF):
                tile, base = SIDE[f]
                low = roll_to(turned[f, below], base - y0)
                high = roll_to(turned[f, above], base + 8 - y0)
                both = roll_to(jnp.where(inside, beside[0, f, block], beside[1, f, block]), base + 16 - y0)
                piece = jnp.where(lane < base + 8, low, jnp.where(lane < base + 16, high, both))
                sides[tile] = piece if base == 0 else jnp.where(lane >= base, piece, sides[tile])
            pltpu.store(out_ref.at[pl.ds(row0, 8), :], sides[0], mask=lane < 99)
            pltpu.store(out_ref.at[pl.ds(row0 + 8, 8), :], sides[1], mask=lane < 66)
        return unused

    used = own_ref[0]
    lax.fori_loop(0, (used + 1) // 2, faces, 0)


def interior_kernel(fine_ref, middle_ref, cells_ref, given, carry, semaphores):
    step = 0.5 * time_step
    lane = lanes()
    low16 = lane < 16
    high16 = lane < 112
    first_y = (lane & 15) == 0
    copies = [
        pltpu.make_async_copy(fine_ref.at[p, :, :, pl.ds(c * LN, LN)], given.at[:, :, c, p, :], semaphores.at[p * 2 + c])
        for p in range(NP)
        for c in range(2)
    ]
    for copy in copies:
        copy.start()
    for copy in copies:
        copy.wait()
    for c in range(2):
        cells = [given[f, 0, c] for f in range(NF)]
        for i, v in enumerate(side_of_face(cells, primitives(cells), 1)):
            carry[i, c] = v
        for f in range(NF):
            carry[11 + f, c] = jnp.zeros((8, LN), jnp.float32)

    def pair(r, unused):
        for half in range(2):
            x = 2 * r + half
            cells = [[given[f, x, c] for f in range(NF)] for c in range(2)]
            prims = [primitives(u) for u in cells]
            for c in range(2):
                speeds, pressure, sound, _ = prims[c]
                for i, v in enumerate(cells[c] + [speeds[2], speeds[3], pressure, sound]):
                    cells_ref[i, x, c] = v
            flux_x = []
            for c in range(2):
                here = side_of_face(cells[c], prims[c], 1)
                flux = face_flux([carry[i, c] for i in range(11)], here)
                if half == 0:
                    flux = [jnp.where(r == 0, 0.0, v) for v in flux]
                flux_x.append(flux)
                for i in range(11):
                    carry[i, c] = here[i]
                for f in range(NF):
                    middle_ref[f, x, c] = carry[11 + f, c] - step * flux[f]
            raw = [raw_of(cells[c], prims[c], 3) for c in range(2)]
            here = [side_of_raw(raw[c], 3) for c in range(2)]
            turned = [[roll_to(v, 16) for v in raw[c]] for c in range(2)]
            left = [turned[0], [jnp.where(low16, a, b) for a, b in zip(*turned)]]
            left = [side_of_raw(v, 3) for v in left]
            lower = [face_flux(left[c], here[c]) for c in range(2)]
            lower[0] = [jnp.where(low16, 0.0, v) for v in lower[0]]
            change = [[], []]
            for f in range(NF):
                back = [roll_to(lower[c][f], -16) for c in range(2)]
                change[0].append(jnp.where(high16, back[0], back[1]) - lower[0][f])
                change[1].append(jnp.where(high16, back[1], back[0]) - lower[1][f])
            for c in range(2):
                raw = raw_of(cells[c], prims[c], 2)
                here = side_of_raw(raw, 2)
                lower_y = face_flux(side_of_raw([roll_to(v, 1) for v in raw], 2), here)
                lower_y = [jnp.where(first_y, 0.0, v) for v in lower_y]
                for f in range(NF):
                    total = change[c][f] + (roll_to(lower_y[f], -1) - lower_y[f]) - flux_x[c][f]
                    carry[11 + f, c] = cells[c][f] - step * total
        return unused

    lax.fori_loop(0, CW, pair, 0)
    for c in range(2):
        for f in range(NF):
            middle_ref[f, FW, c] = carry[11 + f, c]


def collect_kernel(state_ref, out_ref, semaphores):
    copies = [
        pltpu.make_async_copy(
            state_ref.at[:, pl.ds(1, FW), c, p, :], out_ref.at[p, :, :, pl.ds(c * LN, LN)], semaphores.at[p * 2 + c]
        )
        for p in range(NP)
        for c in range(2)
    ]
    for copy in copies:
        copy.start()
    for copy in copies:
        copy.wait()


def fine_kernel(
    count,
    box_ref,
    ghost_ref,
    middle_ref,
    cells_ref,
    out_ref,
    last_ref,
    message,
    rows,
    zghost,
    yghost,
    xghost,
    middle,
    carry,
    zsum,
    ysum,
    xsum,
    xpool,
    packed,
):
    per_device = ZC // CW * YB
    me = lax.axis_index("box")
    lane = lanes()
    place_y = lane & 15
    first_y = place_y == 0
    last_y = place_y == 15
    low16 = lane < 16
    high16 = lane < 112

    def slots(p):
        owner, _ = split_box(box_ref[me * NP + p], per_device)
        return owner, jnp.where(owner == 0, count - 1, owner - 1), jnp.where(owner == count - 1, 0, owner + 1)

    for p in range(NP):
        own, before, after = slots(p)
        for tile in range(2):
            start = 99 if tile == 0 else 66
            lower_parity = 0 if tile == 0 else 1
            is_x = lane >= start
            is_lower = (((lane - start) >> 3) & 1) == lower_parity
            pieces = [ghost_ref[pl.ds(pl.multiple_of(s * 16 + tile * 8, 8), 8), :] for s in (own, before, after)]
            message[pl.ds(p * 16 + tile * 8, 8), :] = jnp.where(
                is_x, jnp.where(is_lower, pieces[1], pieces[2]), pieces[0]
            )
    for i in range(16):
        rows[i] = message[pl.ds(i, NP, stride=16), :]
    pair_y = place_y >> 1
    for f in range(NF):
        tile, base = SIDE[f]
        index = jnp.where(lane < 64, base, base + 8) + pair_y
        for r in range(CW):
            zghost[f, r] = take_lanes(rows[tile * 8 + r], index)
        for c in range(2):
            index = jnp.where(place_y < 8, base + 16, base + 25) + (lane >> 5) + 4 * c
            for r in range(CW):
                yghost[f, c, r] = take_lanes(rows[tile * 8 + r], index)
    dense = {}
    for c in range(2):
        for f in range(NF):
            (tile_low, low), (tile_high, high) = XUNIT[2 * f], XUNIT[2 * f + 1]
            for k in range(4):
                moved = roll_to(rows[tile_low * 8 + 4 * c + k], 32 * k - low)
                if (tile_high, high) != (tile_low, low + 8):
                    other = roll_to(rows[tile_high * 8 + 4 * c + k], 32 * k + 8 - high)
                    moved = jnp.where((lane & 15) < 8, moved, other)
                dense[c, f] = moved if k == 0 else jnp.where(lane >= 32 * k, moved, dense[c, f])
    for upper in range(2):
        unfold = (lane & 96) + pair_y + 8 * upper
        for c in range(2):
            for f in range(NF):
                xghost[upper, f, c] = take_lanes(dense[c, f], unfold)
    for half in range(2):
        some = pl.ds(4 * half, 4)
        values = [zghost[f, some] for f in range(NF)]
        for i, v in enumerate(side_of_face(values, primitives(values), 3)[NF:]):
            zghost[NF + i, some] = v
        for c in range(2):
            values = [yghost[f, c, some] for f in range(NF)]
            for i, v in enumerate(side_of_face(values, primitives(values), 2)[NF:]):
                yghost[NF + i, c, some] = v
    for upper in range(2):
        values = [xghost[upper, f] for f in range(NF)]
        for i, v in enumerate(side_of_face(values, primitives(values), 1)[NF:]):
            xghost[upper, NF + i] = v

    step = 0.5 * time_step

    sign_z = jnp.where(lane < 64, -1.0, 1.0)
    sign_y = jnp.where(place_y < 8, -1.0, 1.0)
    scale_z = [jnp.where(low16, step, 0.0), jnp.where(high16, 0.0, -step)]
    scale_y = jnp.where(first_y, step, jnp.where(last_y, -step, 0.0))

    def outer_flux(inside, ghost, sign):
        fastest = jnp.maximum(inside[10], ghost[10]) * sign
        return [inside[5 + f] + ghost[5 + f] - fastest * (ghost[f] - inside[f]) for f in range(NF)]

    def outer_faces(r, unused):
        both = pl.ds(2 * r, 2)
        cells = [[cells_ref[i, both, c] for i in range(9)] for c in range(2)]

        def inside(values, m):
            speeds = [None, None, values[5], values[6]]
            return side_of_face(values[:NF], (speeds, values[7], values[8], values[4] + values[7]), m)

        edge = [jnp.where(lane < 64, cells[0][i], cells[1][i]) for i in range(9)]
        flux_z = outer_flux(inside(edge, 3), [zghost[i, r] for i in range(11)], sign_z)
        for f in range(NF):
            zsum[f, r] = flux_z[f][0] + flux_z[f][1]
        for c in range(2):
            flux_y = outer_flux(inside(cells[c], 2), [yghost[i, c, r] for i in range(11)], sign_y)
            for f in range(NF):
                ysum[f, r, c] = flux_y[f][0] + flux_y[f][1]
                old = middle_ref[f, pl.ds(2 * r + 1, 2), c]
                middle[f, both, c] = old + flux_y[f] * scale_y + flux_z[f] * scale_z[c]
        return unused

    lax.fori_loop(0, CW, outer_faces, 0)
    for side, plane in ((0, 0), (1, FW - 1)):
        values = [cells_ref[f, plane] for f in range(NF)]
        sides = [[xghost[side, i] for i in range(11)], side_of_face(values, primitives(values), 1)]
        flux_x = face_flux(*(sides[::-1] if side else sides))
        for f in range(NF):
            xsum[side, f] = flux_x[f]
            middle[f, plane] = middle[f, plane] + (-step if side else step) * flux_x[f]

    def finish(plane, part, flux):
        for c in range(2):
            for f in range(NF):
                last_ref[f, plane, c] = part[c][f] - step * flux[c][f]

    for c in range(2):
        for i in range(11):
            carry[i, c] = xghost[0, i, c]
        for f in range(NF):
            carry[11 + f, c] = jnp.zeros((8, LN), jnp.float32)

    def pair(r, unused):
        zg = [zghost[i, r] for i in range(11)]
        zb = [None] * NF
        yb = [[None] * NF for _ in range(2)]
        for half in range(2):
            x = 2 * r + half
            cells = [[middle[f, x, c] for f in range(NF)] for c in range(2)]
            prims = [primitives(u) for u in cells]
            flux_x = []
            for c in range(2):
                here = side_of_face(cells[c], prims[c], 1)
                behind = [carry[i, c] for i in range(11)]
                flux_x.append(face_flux(behind, here))
                for i in range(11):
                    carry[i, c] = here[i]
            finish(x, [[carry[11 + f, c] for f in range(NF)] for c in range(2)], flux_x)

            if half == 0:

                @pl.when(r == 0)
                def _():
                    for c in range(2):
                        for f in range(NF):
                            xsum[0, f, c] = xsum[0, f, c] + flux_x[c][f]

            raw = [raw_of(cells[c], prims[c], 3) for c in range(2)]
            here = [side_of_raw(raw[c], 3) for c in range(2)]
            turned = [[roll_to(v, 16) for v in raw[c]] for c in range(2)]
            left = side_of_raw(turned[0], 3)
            left = [
                [jnp.where(low16, zg[i], left[i]) for i in range(11)],
                side_of_raw([jnp.where(low16, a, b) for a, b in zip(*turned)], 3),
            ]
            lower = [face_flux(left[c], here[c]) for c in range(2)]
            last = face_flux(here[1], zg)
            change = [[], []]
            for f in range(NF):
                back = [roll_to(lower[c][f], -16) for c in range(2)]
                change[0].append(jnp.where(high16, back[0], back[1]) - lower[0][f])
                change[1].append(jnp.where(high16, back[1], last[f]) - lower[1][f])
                edge = jnp.where(lane < 64, lower[0][f], last[f])
                zb[f] = edge if half == 0 else zb[f] + edge
            for c in range(2):
                yg = [yghost[i, c, r] for i in range(11)]
                raw = raw_of(cells[c], prims[c], 2)
                here = side_of_raw(raw, 2)
                left = side_of_raw([roll_to(v, 1) for v in raw], 2)
                left = [jnp.where(first_y, yg[i], left[i]) for i in range(11)]
                lower_y = face_flux(left, here)
                last_flux = face_flux(here, yg)
                for f in range(NF):
                    upper_y = jnp.where(last_y, last_flux[f], roll_to(lower_y[f], -1))
                    change[c][f] = change[c][f] + (upper_y - lower_y[f])
                    edge = jnp.where(place_y < 8, lower_y[f], last_flux[f])
                    yb[c][f] = edge if half == 0 else yb[c][f] + edge
            for c in range(2):
                for f in range(NF):
                    carry[11 + f, c] = cells[c][f] - step * (change[c][f] - flux_x[c][f])
        for f in range(NF):
            zsum[f, r] = zsum[f, r] + zb[f]
            for c in range(2):
                ysum[f, r, c] = ysum[f, r, c] + yb[c][f]
        return unused

    lax.fori_loop(0, CW, pair, 0)
    flux_x = [face_flux([carry[i, c] for i in range(11)], [xghost[1, i, c] for i in range(11)]) for c in range(2)]
    finish(FW, [[carry[11 + f, c] for f in range(NF)] for c in range(2)], flux_x)
    for c in range(2):
        for f in range(NF):
            xsum[1, f, c] = xsum[1, f, c] + flux_x[c][f]

    odd = (lane & 1) == 1
    odd_z = (lane & 16) == 16
    outer = (place_y == 0) | (place_y == 15)
    middle_y = (place_y >= 2) & (place_y < 10)
    z_ends = (lane < 16) | (lane >= 112)

    def shifted(values, shift):
        return [roll_to(v, shift) for v in values]

    def added(left, right):
        return [a + b for a, b in zip(left, right)]

    def dense(values):
        values = added(values, shifted(values, -1))
        return [jnp.where(odd, b, a) for a, b in zip(values, shifted(values, -7))]

    ends = [xsum[side, f, c] for f in range(NF) for side in range(2) for c in range(2)]
    ends = dense(added(ends, shifted(ends, -16)))
    for i, v in enumerate(ends):
        xpool[i] = v
    for f in range(NF):
        sums = [[last_ref[f, 2 * r + 1, c] + last_ref[f, 2 * r + 2, c] for r in range(CW)] for c in range(2)]
        turned = [shifted(sums[0], -1), shifted(sums[1], 1)]
        average = [jnp.where(odd, sums[1][r] + turned[1][r], sums[0][r] + turned[0][r]) for r in range(CW)]
        average = added(average, shifted(average, -16))
        v = [[ysum[f, r, c] for r in range(CW)] for c in range(2)]
        turned = [shifted(v[1], 1), shifted(v[1], -1)]
        fluxes = [
            jnp.where(outer, v[0][r], jnp.where(place_y < 8, turned[0][r], turned[1][r])) for r in range(CW)
        ]
        v = [zsum[f, r] for r in range(CW)]
        v = added(v, shifted(v, -1))
        v = [jnp.where(odd, b, a) for a, b in zip(shifted(v, 2), shifted(v, -5))]
        fluxes = [jnp.where(middle_y, jnp.where(z_ends, v[r], 0.0), fluxes[r]) for r in range(CW)]
        fluxes = added(fluxes, shifted(fluxes, 16))
        for low, part in (
            (50, [roll_to(xpool[f * 4 + r // 4], 50 - r % 4 * 32) for r in range(CW)]),
            (82, [roll_to(xpool[f * 4 + 2 + r // 4], 82 - r % 4 * 32) for r in range(CW)]),
        ):
            mask = (lane >= low) & (lane < low + 8)
            fluxes = [jnp.where(mask, part[r], fluxes[r]) for r in range(CW)]
        for r in range(CW):
            row = jnp.where(odd_z, fluxes[r] * 0.0625, average[r] * 0.125)
            packed[pl.ds(f * 8 + r, NP, stride=NF * 8), :] = row

    lower_x = (lane >= 50) & (lane < 58)
    upper_x = (lane >= 82) & (lane < 90)
    others = ~(lower_x | upper_x)
    for p in range(NP):
        own, before, after = slots(p)
        for f in range(NF):
            tile = packed[pl.ds(p * 40 + f * 8, 8), :]
            for slot, mask in ((own, others), (before, lower_x), (after, upper_x)):
                target = out_ref.at[pl.ds(pl.multiple_of(slot * 40 + f * 8, 8), 8), :]
                pltpu.store(target, tile, mask=mask)


def coarse_kernel(coarse_ref, low_ref, high_ref, next_ref, yedge_ref, zedge_ref, xedge_ref, carry):
    step = 0.5 * time_step
    upper_edge = (lax.broadcasted_iota(jnp.int32, (ZC, LN), 1) & (CW - 1)) == CW - 1
    values = [low_ref[pl.ds(f * ZC, ZC), :] for f in range(NF)]
    for i, v in enumerate(side_of_face(values, primitives(values), 1)):
        carry[i] = v

    def store(ref, f, x, value):
        ref[pl.ds(pl.multiple_of(f * 256 + x * ZC, ZC), ZC), :] = value

    def plane(x, unused):
        cells = [coarse_ref[pl.ds(pl.multiple_of(f * 256 + x * ZC, ZC), ZC), :] for f in range(NF)]
        prims = primitives(cells)
        here = side_of_face(cells, prims, 1)
        flux_x = face_flux([carry[i] for i in range(11)], here)

        @pl.when(x > 0)
        def _():
            for f in range(NF):
                store(next_ref, f, x - 1, carry[11 + f] - step * flux_x[f])

        @pl.when(x == 0)
        def _():
            for f in range(NF):
                xedge_ref[pl.ds(f * 64, ZC), :] = 0.5 * flux_x[f]

        for i in range(11):
            carry[i] = here[i]
        here = side_of_face(cells, prims, 3)
        left = [pltpu.roll(v, 1, 0) for v in here]
        lower_z = face_flux(left, here)
        here = side_of_face(cells, prims, 2)
        left = [pltpu.roll(v, 1, 1) for v in here]
        lower_y = face_flux(left, here)
        for f in range(NF):
            upper_y = pltpu.roll(lower_y[f], LN - 1, 1)
            change = (pltpu.roll(lower_z[f], ZC - 1, 0) - lower_z[f]) + (upper_y - lower_y[f])
            carry[11 + f] = cells[f] - step * (change - flux_x[f])
            store(yedge_ref, f, x, 0.5 * jnp.where(upper_edge, upper_y, lower_y[f]))
            for k in range(ZC // CW):
                zedge_ref[pl.ds((f * 4 + k) * 8 + x, 1), :] = 0.5 * lower_z[f][k * CW : k * CW + 1, :]
        return unused

    lax.fori_loop(0, CW, plane, 0)
    values = [high_ref[pl.ds(f * ZC, ZC), :] for f in range(NF)]
    flux_x = face_flux([carry[i] for i in range(11)], side_of_face(values, primitives(values), 1))
    for f in range(NF):
        store(next_ref, f, CW - 1, carry[11 + f] - step * flux_x[f])
        xedge_ref[pl.ds(f * 64 + ZC, ZC), :] = 0.5 * flux_x[f]


def apply_kernel(count, slot_ref, result_ref, base_ref, yedge_ref, zedge_ref, xedge_ref, out_hbm, zsum, out_ref, semaphores):
    per_device = ZC // CW * YB
    lane = lanes()
    sub = lax.broadcasted_iota(jnp.int32, (8, LN), 0)
    out_ref[...] = base_ref[...]
    zsum[...] = jnp.zeros(zsum.shape, jnp.float32)

    def place_of(row):
        return split_box(slot_ref[4 * count + row], per_device)[1]

    def weight(row, face):
        return slot_ref[(4 + NP) * count + row * 6 + face].astype(jnp.float32) * (time_step if face % 2 else -time_step)

    def one(source, unused):
        before_row, own, after_row = (slot_ref[k * count + source] for k in range(3))
        row0 = pl.multiple_of(source * 40, 8)

        def tile(f):
            return result_ref[pl.ds(row0 + f * 8, 8), :]

        def unmix(y0, first):
            place = lane - y0
            return (first + (place & 3) * 2 + ((place >> 2) & 1)) & (LN - 1)

        for upper in range(2):
            row = before_row if upper else after_row

            @pl.when(row >= 0)
            def _():
                z0, y0 = anchors(place_of(row))
                scale = weight(row, upper)
                inside = (lane >= y0) & (lane < y0 + CW)
                index = unmix(y0, 82 if upper else 50)
                plane = 0 if upper else CW - 1
                new, places = [], []
                for f in range(NF):
                    place = pl.ds(pl.multiple_of(f * 256 + plane * ZC + z0, 8), 8)
                    edge = xedge_ref[pl.ds(pl.multiple_of(f * 64 + (1 - upper) * ZC + z0, 8), 8), :]
                    old = out_ref[place, :]
                    places.append(place)
                    new.append(jnp.where(inside, old + scale * (take_lanes(tile(f), index) - edge), old))
                for place, value in zip(places, new):
                    out_ref[place, :] = value

        @pl.when(own >= 0)
        def _():
            z0, y0 = anchors(place_of(own))
            inside = (lane >= y0) & (lane < y0 + CW)
            block = z0 >> 3
            for upper, target, face in ((0, (block - 1) & 3, block), (1, (block + 1) & 3, (block + 1) & 3)):
                scale = jnp.where(inside, weight(own, 2 + upper), 0.0)
                index = unmix(y0, 114 if upper else 18)
                for f in range(NF):
                    edge = zedge_ref[pl.ds(pl.multiple_of(f * 32 + face * 8, 8), 8), :]
                    part = jnp.where(inside, take_lanes(tile(f), index) - edge, 0.0)
                    zsum[f, upper, target] = zsum[f, upper, target] + scale * part
            before = lane == ((y0 - 1) & (LN - 1))
            after = lane == ((y0 + CW) & (LN - 1))
            part = (sub & 3) * 32 + (sub >> 2)
            faces = jnp.where(before, part + 16, (sub & 3) * 32 + 31 - (sub >> 2))
            index = jnp.where(inside, part + 2 * ((lane - y0) & 7), faces)
            scale = jnp.where(before, weight(own, 4), jnp.where(after, weight(own, 5), 0.0))
            for f in range(NF):
                new, places = [], []
                for x in range(CW):
                    place = pl.ds(pl.multiple_of(f * 256 + x * ZC + z0, 8), 8)
                    line = jnp.broadcast_to(result_ref[pl.ds(row0 + f * 8 + x, 1), :], (8, LN))
                    got = take_lanes(line, index)
                    places.append(place)
                    new.append(jnp.where(inside, got, out_ref[place, :] + scale * (got - yedge_ref[place, :])))
                for place, value in zip(places, new):
                    out_ref[place, :] = value

        return unused

    lax.fori_loop(0, count, one, 0)
    copies = []
    for f in range(NF):
        for x in range(CW):
            for block in range(ZC // CW):
                for upper in range(2):
                    row = pl.ds(f * 256 + x * ZC + block * 8 + (0 if upper else 7), 1)
                    out_ref[row, :] = out_ref[row, :] + zsum[f, upper, block, x : x + 1]
        field = pl.ds(f * 256, 256)
        copies.append(pltpu.make_async_copy(out_ref.at[field, :], out_hbm.at[field, :], semaphores.at[f]))
        copies[f].start()
    for copy in copies:
        copy.wait()


def local(coarse_state, fine_state, patch_box, face_flags):
    count = lax.axis_size("box")
    assert coarse_state.shape == (NF, CW, ZC, LN) and fine_state.shape == (NP, NF, FW, FW * FW)
    coarse = coarse_state.reshape(NF * CW * ZC, LN)
    f32 = jnp.float32
    vmem = pl.BlockSpec(memory_space=pltpu.VMEM)
    smem = pl.BlockSpec(memory_space=pltpu.SMEM)
    hbm = pl.BlockSpec(memory_space=pltpu.HBM)
    anywhere = pl.BlockSpec(memory_space=pl.ANY)

    def shaped(*shape):
        return jax.ShapeDtypeStruct(shape, f32)

    def call(kernel, out_shape, in_specs, out_specs, flops, size, scratch=(), limit=16):
        return pl.pallas_call(
            kernel,
            out_shape=out_shape,
            in_specs=in_specs,
            out_specs=out_specs,
            scratch_shapes=scratch,
            cost_estimate=pl.CostEstimate(flops=flops, bytes_accessed=size, transcendentals=0),
            compiler_params=pltpu.CompilerParams(vmem_limit_bytes=limit * 1024 * 1024),
        )

    packets, first, last, slots, _ = call(
        functools.partial(pack_kernel, count),
        (
            shaped(count * 16, LN),
            shaped(NF, ZC, LN),
            shaped(NF, ZC, LN),
            jax.ShapeDtypeStruct((4 * count,), jnp.int32),
            jax.ShapeDtypeStruct((count + 2,), jnp.int32),
        ),
        [hbm, hbm],
        (vmem, vmem, vmem, smem, smem),
        1000000,
        1000000,
        (
            pltpu.SMEM((count * NP,), jnp.int32),
            pltpu.VMEM((NF, ZC, CW, LN), f32),
            pltpu.VMEM((2, NF, ZC // CW, CW, LN), f32),
            pltpu.SemaphoreType.DMA((3 + CW,)),
        ),
        limit=63,
    )(patch_box, coarse_state)
    arrived = lax.all_to_all(packets.reshape(count, 16, LN), "box", split_axis=0, concat_axis=0, tiled=True)
    ring = [(i, (i + 1) % count) for i in range(count)]
    low = lax.ppermute(last, "box", ring)
    high = lax.ppermute(first, "box", [(b, a) for a, b in ring])
    middle, cells = call(
        interior_kernel,
        (
            shaped(NF, FW + 1, 2, NP, LN),
            shaped(9, FW, 2, NP, LN),
        ),
        [hbm],
        (vmem, vmem),
        10000000,
        4000000,
        (
            pltpu.VMEM((NF, FW, 2, NP, LN), f32),
            pltpu.VMEM((16, 2, 8, LN), f32),
            pltpu.SemaphoreType.DMA((2 * NP,)),
        ),
    )(fine_state)
    outbox, state = call(
        functools.partial(fine_kernel, count),
        (shaped(count * 40, LN), shaped(NF, FW + 1, 2, NP, LN)),
        [smem] + [vmem] * 3,
        (vmem, vmem),
        20000000,
        4000000,
        (
            pltpu.VMEM((NP * 16, LN), f32),
            pltpu.VMEM((16, NP, LN), f32),
            pltpu.VMEM((11, CW, 8, LN), f32),
            pltpu.VMEM((11, 2, CW, 8, LN), f32),
            pltpu.VMEM((2, 11, 2, 8, LN), f32),
            pltpu.VMEM((NF, FW, 2, 8, LN), f32),
            pltpu.VMEM((16, 2, 8, LN), f32),
            pltpu.VMEM((NF, CW, 8, LN), f32),
            pltpu.VMEM((NF, CW, 2, 8, LN), f32),
            pltpu.VMEM((2, NF, 2, 8, LN), f32),
            pltpu.VMEM((4 * NF, NP, LN), f32),
            pltpu.VMEM((NP * 40, LN), f32),
        ),
    )(patch_box, arrived.reshape(count * 16, LN), middle, cells)
    returned = lax.all_to_all(outbox.reshape(count, 40, LN), "box", split_axis=0, concat_axis=0, tiled=True)
    fine_next = call(
        collect_kernel,
        shaped(*fine_state.shape),
        [vmem],
        anywhere,
        1000000,
        4000000,
        (pltpu.SemaphoreType.DMA((2 * NP,)),),
    )(state)
    tables = jnp.concatenate([slots, patch_box, face_flags.reshape(-1)])
    size = NF * CW * ZC
    base, yedge, zedge, xedge = call(
        coarse_kernel,
        (shaped(size, LN), shaped(size, LN), shaped(NF * 32, LN), shaped(NF * 2 * ZC, LN)),
        [vmem] * 3,
        (vmem,) * 4,
        10000000,
        4000000,
        (pltpu.VMEM((16, ZC, LN), f32),),
    )(coarse, low.reshape(NF * ZC, LN), high.reshape(NF * ZC, LN))
    coarse_next = call(
        functools.partial(apply_kernel, count),
        shaped(size, LN),
        [smem] + [vmem] * 5,
        anywhere,
        2000000,
        4000000,
        (
            pltpu.VMEM((NF, 2, ZC // CW, CW, LN), f32),
            pltpu.VMEM((size, LN), f32),
            pltpu.SemaphoreType.DMA((NF,)),
        ),
    )(tables, returned.reshape(count * 40, LN), base, yedge, zedge, xedge)
    return coarse_next.reshape(coarse_state.shape), fine_next


def solution(mesh):
    placed = (
        P(None, "box", "grp", None),
        P(("grp", "box"), None, None, None),
        P("grp"),
        P("grp", None),
    )
    return jax.shard_map(
        local,
        mesh=mesh,
        in_specs=placed,
        out_specs=(P(None, "box", "grp", None), P(("grp", "box"), None, None, None)),
        check_vma=False,
    )
```
